32 devices in a mesh: dp: 4 (over x, core), row: 2 (over y), col: 4 (over z).
Axes of the slice: x: 2, y: 2, z: 4, core: 2. Of those that a mesh axis runs over, the one named last changes fastest.
Arguments:
- hidden_in: bfloat16 [4096, 2048], P(('dp', 'col'), 'row'), may hold values from -6 to 6
- segment: int32 [4, 1024], P('dp'), may hold values from 0 to 3, never falling along the last dimension, each value on 1 to 512 neighbouring positions
- norm1_gain: float32 [2048], P('row'), may hold values from 0.5 to 1.5
- norm1_bias: float32 [2048], P('row'), may hold values from -2 to 2
- norm2_gain: float32 [2048], P('row'), may hold values from 0.5 to 1.5
- norm2_bias: float32 [2048], P('row'), may hold values from -2 to 2
- qkv_weight: bfloat16 [2048, 6144], P('row', 'col'), may hold values from -1 to 1
- qkv_bias: float32 [6144], P('col'), may hold values from -2 to 2
- dense_weight: bfloat16 [2048, 2048], P('col', 'row'), may hold values from -1 to 1
- dense_bias: float32 [2048], P('row'), may hold values from -2 to 2
- up_weight: bfloat16 [2048, 8192], P('row', 'col'), may hold values from -0.125 to 0.125
- up_bias: float32 [8192], P('col'), may hold values from -3 to 3
- down_weight: bfloat16 [8192, 2048], P('col', 'row'), may hold values from -0.0625 to 0.0625
- down_bias: float32 [2048], P('row'), may hold values from -2 to 2
- cotangent: bfloat16 [4096, 2048], P(('dp', 'col'), 'row'), may hold values from -6 to 6
Outputs:
- block_out: bfloat16 [4096, 2048], P(('dp', 'col'), 'row')
- input_grad: float32 [4096, 2048], P(('dp', 'col'), 'row')
- norm1_gain_grad: float32 [2048], P('row')
- norm1_bias_grad: float32 [2048], P('row')
- norm2_gain_grad: float32 [2048], P('row')
- norm2_bias_grad: float32 [2048], P('row')
- qkv_weight_grad: float32 [2048, 6144], P('row', 'col')
- qkv_bias_grad: float32 [6144], P('col')
- dense_weight_grad: float32 [2048, 2048], P('col', 'row')
- dense_bias_grad: float32 [2048], P('row')
- up_weight_grad: float32 [2048, 8192], P('row', 'col')
- up_bias_grad: float32 [8192], P('col')
- down_weight_grad: float32 [8192, 2048], P('col', 'row')
- down_bias_grad: float32 [2048], P('row')
The draws below stay inside these ranges and needn't reach their ends.
Inputs may be any that keep to these rules, and one draw needn't show every extreme that they name: Each row holds one data group's 1024 token slots; segment numbers never fall along a row, a run of equal numbers is one sequence of at most 512 tokens, and some sequence is exactly 512 long.
All inputs are finite; a program needn't handle non-finite values.
Results may differ from the reference program's by a relative error of at most 0.0093.
Values may be sent and summed in bfloat16 or wider, within the bound.
A program may use at most 192 MiB of HBM per device.

```python
import math
import jax
import jax.numpy as jnp
import numpy as np
from jax import lax

D = 2048
FF = 8192
HEADS = 8
HD = 256
ROT = 64
TOK_GRP = 1024
SEGS = 4
SEQ_MAX = 512
BLOCK_ROWS = 512
TOKENS = 4096
N_DP = 4


def draw_qkv_weight(key, part):
    bound_value = 6.0 / math.sqrt(D)
    base = jax.random.normal(key, (D, 3 * D), jnp.float32) * (1.0 / math.sqrt(D))
    base = jnp.clip(base, -bound_value, bound_value)
    return base.astype(jnp.bfloat16)


def block_scale(stream_key, shape, shards, smallest, largest):
    def one(position, blocks):
        heights = jax.random.uniform(jax.random.fold_in(jax.random.fold_in(stream_key, 6), position), (blocks,), jnp.float32, smallest / len(shards), largest / len(shards))
        return jnp.repeat(jnp.exp(heights), shape[position] // blocks).reshape((-1,) + (1,) * (len(shape) - position - 1))

    gain = one(*shards[0])
    for cut in shards[1:]:
        gain = gain * one(*cut)
    return gain


def split_up(count, total, limit, slope):
    loads = [(1 << 20) // math.isqrt(standing ** slope) + 1 for standing in range(2, count + 1)]
    spare, given = total - limit - (count - 1), [1] * (count - 1)
    while spare > 0:
        free = [i for i in range(count - 1) if given[i] < limit]
        whole, budget = sum([loads[i] for i in free]), spare
        for i in free:
            addition = min(limit - given[i], max(1, budget * loads[i] // whole), spare)
            given[i] = given[i] + addition
            spare = spare - addition
    return np.array([limit] + given)


def uneven(stream_key, count, total, limit, skew):
    if count == 2:
        one = jax.random.randint(stream_key, (), max(1, total - limit), min(limit, total - 1) + 1)
        return jnp.stack([one, total - one])
    lengths = jnp.asarray(split_up(count, total, limit, skew), jnp.int32)
    twos = (count - 1) // 2
    source_of, sink = lengths[1:1 + 2 * twos:2], lengths[2:2 + 2 * twos:2]
    margin = jnp.minimum(source_of - 1, limit - sink)
    shifted = jax.random.randint(jax.random.fold_in(stream_key, 1), (twos,), 0, 1 << 20) % (margin + 1)
    lengths = lengths.at[1:1 + 2 * twos:2].set(source_of - shifted).at[2:2 + 2 * twos:2].set(sink + shifted)
    return lengths[jax.random.permutation(jax.random.fold_in(stream_key, 2), count)]


def gaussian(rng, shape, spread, most, shards=(), kind=jnp.bfloat16):
    entries = jax.random.normal(rng, shape, jnp.float32) * spread
    if len(shards) > 0:
        entries = block_scale(rng, shape, shards, -0.22, 0.18) * entries
    return jnp.clip(entries, min=-most, max=most).astype(kind)


def setup_inputs(seed: int = 0) -> dict:
    arg_keys = jax.random.split(jax.random.key(seed), 16)
    return {
        "hidden_in": gaussian(arg_keys[0], (TOKENS, D), 1.0, 6.0, ((0, 16), (1, 2))),
        "segment": jax.vmap(lambda own: jnp.searchsorted(jnp.cumsum(uneven(own, SEGS, TOK_GRP, SEQ_MAX, 2)), jnp.arange(TOK_GRP), side="right"))(jax.random.split(arg_keys[1], N_DP)).reshape((N_DP, TOK_GRP)).astype(jnp.int32),
        "norm1_gain": jnp.clip(1.0 + 0.1 * jax.random.normal(arg_keys[2], (D,), jnp.float32), 0.5, 1.5),
        "norm1_bias": gaussian(arg_keys[3], (D,), 0.3, 2.0, ((0, 2),), jnp.float32),
        "norm2_gain": jnp.clip(1.0 + 0.1 * jax.random.normal(arg_keys[4], (D,), jnp.float32), 0.5, 1.5),
        "norm2_bias": gaussian(arg_keys[5], (D,), 0.3, 2.0, ((0, 2),), jnp.float32),
        "qkv_weight": draw_qkv_weight(jax.random.fold_in(arg_keys[15], 71), 0),
        "qkv_bias": gaussian(arg_keys[7], (3 * D,), 0.3, 2.0, ((0, 4),), jnp.float32),
        "dense_weight": gaussian(arg_keys[8], (D, D), (D // 64) ** -0.5, 1.0, ((0, 4), (1, 2))),
        "dense_bias": gaussian(arg_keys[9], (D,), 0.3, 2.0, ((0, 2),), jnp.float32),
        "up_weight": gaussian(arg_keys[10], (D, FF), D ** -0.5, 0.125, ((0, 2), (1, 4))),
        "up_bias": gaussian(arg_keys[11], (FF,), 0.5, 3.0, ((0, 4),), jnp.float32),
        "down_weight": gaussian(arg_keys[12], (FF, D), FF ** -0.5, 0.0625, ((0, 4), (1, 2))),
        "down_bias": gaussian(arg_keys[13], (D,), 0.3, 2.0, ((0, 2),), jnp.float32),
        "cotangent": gaussian(arg_keys[14], (TOKENS, D), 1.0, 6.0, ((0, 16), (1, 2))),
    }


@jax.custom_vjp
def low(v):
    return lax.optimization_barrier(v.astype(jnp.bfloat16)).astype(jnp.float32)

@jax.custom_vjp
def low_back(v):
    return v

def low_keep(v):
    return (low(v), None)

def low_pass(kept, grad):
    return (grad,)

def back_keep(v):
    return (v, None)

def back_low(kept, grad):
    return (low(grad),)
low.defvjp(low_keep, low_pass)
low_back.defvjp(back_keep, back_low)
eps_norm = 1e-05
rope_base = 10000.0
precise = lax.Precision.HIGHEST

def positions_of(segment_row):
    length = segment_row.shape[0]
    starts = lax.optimization_barrier(jnp.sum((segment_row[None, :] < segment_row[:, None]).astype(jnp.int32), axis=1))
    return jnp.arange(length, dtype=jnp.int32) - starts

def rope_tables(segment_row):
    where_at = positions_of(segment_row).astype(jnp.float32)
    inverse = jnp.power(rope_base, -2.0 * jnp.arange(ROT // 2, dtype=jnp.float32) / ROT)
    angles = where_at[:, None] * inverse[None, :]
    return (jnp.cos(angles)[:, None, :], jnp.sin(angles)[:, None, :])

def rotate(vector, cosine, sine_part):
    split_at = ROT // 2
    first_half = vector[..., :split_at]
    second_half = vector[..., split_at:ROT]
    passed = vector[..., ROT:]
    return jnp.concatenate([first_half * cosine - second_half * sine_part, second_half * cosine + first_half * sine_part, passed], axis=-1)

def attend(query, keys, values, segment_row):
    total_rows = query.shape[0]
    blocks = total_rows // BLOCK_ROWS
    row_ids = jnp.arange(total_rows, dtype=jnp.int32)
    scale_value = 1.0 / math.sqrt(HD)

    def one_block(inputs):
        query_block, segment_block, rows_block = inputs
        scores = jnp.einsum('qhd,khd->hqk', query_block, keys, precision=precise) * scale_value
        scores = low_back(scores)
        allowed = (segment_block[:, None] == segment_row[None, :]) & (rows_block[:, None] >= row_ids[None, :])
        scores = jnp.where(allowed[None], scores, -jnp.inf)
        weights = low(jax.nn.softmax(scores, axis=-1))
        return jnp.einsum('hqk,khd->qhd', weights, values, precision=precise)
    outputs = lax.map(jax.checkpoint(one_block), (query.reshape(blocks, BLOCK_ROWS, HEADS, HD), segment_row.reshape(blocks, BLOCK_ROWS), row_ids.reshape(blocks, BLOCK_ROWS)))
    return outputs.reshape(total_rows, HEADS, HD)

def forward(x_value, weights, segment_row):
    gain_one, bias_one, gain_two, bias_two, mixed_weight, mixed_bias, dense_w, dense_b, up_w, up_b, down_w, down_b = weights
    mean_value = lax.optimization_barrier(jnp.mean(x_value, axis=-1, keepdims=True))
    variance = lax.optimization_barrier(jnp.mean(x_value * x_value, axis=-1, keepdims=True)) - mean_value * mean_value
    normal = (x_value - mean_value) * lax.rsqrt(variance + eps_norm)
    normed_one = low(normal * gain_one + bias_one)
    normed_two = low(normal * gain_two + bias_two)
    mixed = low_back(jnp.dot(normed_one, mixed_weight, precision=precise, preferred_element_type=jnp.float32) + mixed_bias)
    mixed = mixed.reshape(-1, HEADS, 3, HD)
    cosine, sine_part = rope_tables(segment_row)
    query = low(rotate(mixed[:, :, 0], cosine, sine_part))
    keys = low(rotate(mixed[:, :, 1], cosine, sine_part))
    values = low(mixed[:, :, 2])
    attended = attend(query, keys, values, segment_row).reshape(-1, D)
    attended = low(low_back(attended))
    attn_branch = jnp.dot(attended, dense_w, precision=precise, preferred_element_type=jnp.float32) + dense_b
    up_value = low_back(jnp.dot(normed_two, up_w, precision=precise, preferred_element_type=jnp.float32) + up_b)
    hidden = low(jax.nn.gelu(up_value, approximate=False))
    mlp_branch = jnp.dot(hidden, down_w, precision=precise, preferred_element_type=jnp.float32) + down_b
    return x_value + attn_branch + mlp_branch

def reference(hidden_in, segment, norm1_gain, norm1_bias, norm2_gain, norm2_bias, qkv_weight, qkv_bias, dense_weight, dense_bias, up_weight, up_bias, down_weight, down_bias, cotangent):
    params = tuple((param.astype(jnp.float32) for param in (norm1_gain, norm1_bias, norm2_gain, norm2_bias, qkv_weight, qkv_bias, dense_weight, dense_bias, up_weight, up_bias, down_weight, down_bias)))
    grouped_in = hidden_in.reshape(N_DP, TOK_GRP, D)
    grouped_cot = cotangent.reshape(N_DP, TOK_GRP, D)

    def per_group(running, group_item):
        x_group, cot_group, segment_row = group_item

        def forward_fn(x_value, *weights):
            return forward(x_value, weights, segment_row)
        result, pullback = jax.vjp(forward_fn, x_group.astype(jnp.float32), *params)
        grads = pullback(cot_group.astype(jnp.float32))
        running = tuple((total_value + new_value for total_value, new_value in zip(running, grads[1:])))
        return (running, (result.astype(jnp.bfloat16), grads[0]))
    zeros_init = tuple((jnp.zeros_like(param) for param in params))
    totals, (outputs, input_grads) = lax.scan(per_group, zeros_init, (grouped_in, grouped_cot, segment))
    return (outputs.reshape(TOKENS, D), input_grads.reshape(TOKENS, D), totals[0], totals[1], totals[2], totals[3], totals[4], totals[5], totals[6], totals[7], totals[8], totals[9], totals[10], totals[11])
```

```python
import math

import jax
import jax.numpy as jnp
from jax import lax
from jax.sharding import PartitionSpec as P

HD = 256
ROT = 64
F32 = jnp.float32
BF16 = jnp.bfloat16

eps_norm = 1e-05
rope_base = 10000.0


def swap(value, axis, mask):
    size = lax.axis_size(axis)
    return lax.ppermute(value, axis, [(i, i ^ mask) for i in range(size)])


def shift(value, axis, step):
    size = lax.axis_size(axis)
    return lax.ppermute(
        value, axis, [(i, i + step) for i in range(size) if 0 <= i + step < size]
    )


def pick(index, *choices):
    return lax.select_n(index, *choices)


def gather_col(block):
    where = lax.axis_index("col")
    up_one, down_one = shift(block, "col", 1), shift(block, "col", -1)
    up_two, down_two = shift(up_one, "col", 1), shift(down_one, "col", -1)
    up_three, down_three = shift(up_two, "col", 1), shift(down_two, "col", -1)
    return [
        block,
        jnp.where(where % 2 == 0, down_one, up_one),
        jnp.where(where < 2, down_two, up_two),
        pick(where, down_three, down_one, up_one, up_three),
    ]


def half(array, index, axis):
    size = array.shape[axis] // 2
    return lax.dynamic_slice_in_dim(array, index * size, size, axis)


def fetch_block(send, quarter):
    rows = send.shape[0] // 4
    part = swap(lax.dynamic_slice_in_dim(send, quarter * rows, rows, 0), "row", 1)
    across = swap(part, "dp", 2)
    part_core, across_core = swap(part, "dp", 1), swap(across, "dp", 1)
    return [(0, part), (1, part_core), (2, across), (3, across_core)]


def join_rows(own, parts, quarter):
    rows = own.shape[0]
    full = jnp.concatenate([own, jnp.zeros_like(own)], axis=0)
    for mask, part in parts:
        start = rows + (quarter ^ mask) * part.shape[0]
        full = lax.dynamic_update_slice_in_dim(full, part, start, 0)
    return full


def join_columns(own, parts, quarter):
    columns = own.shape[1]
    full = jnp.concatenate([own, jnp.zeros_like(own)], axis=1)
    for mask, part in parts:
        start = (quarter ^ mask) * part.shape[0]
        full = lax.dynamic_update_slice(full, part, (start, columns))
    return full


def dp_sum(low):
    size = lax.axis_size("dp")
    mask = 2
    total = low.astype(F32)
    while mask < size:
        if mask > 2:
            low = total.astype(BF16)
        total = low.astype(F32) + swap(low, "dp", mask).astype(F32)
        mask *= 2
    return total


def small_sum(value, axes):
    return lax.psum(value, axes)


def two(index, first, second, axis):
    return jnp.concatenate(
        [jnp.where(index == 0, first, second), jnp.where(index == 0, second, first)], axis=axis
    )


def shards(
    hidden_in,
    segment,
    norm1_gain,
    norm1_bias,
    norm2_gain,
    norm2_bias,
    qkv_weight,
    qkv_bias,
    dense_weight,
    dense_bias,
    up_weight,
    up_bias,
    down_weight,
    down_bias,
    cotangent,
):
    row = lax.axis_index("row")
    col = lax.axis_index("col")
    dp = lax.axis_index("dp")
    core = dp % 2
    quarter = dp % 4
    block_rows, width_dev = hidden_in.shape
    width = 2 * width_dev
    segment_row = segment[0]
    group_rows = segment_row.shape[0]
    scale_value = 1.0 / math.sqrt(HD)

    x_own = gather_col(hidden_in)
    x_other = [swap(block, "row", 1) for block in x_own]
    cot_block = jnp.concatenate([cotangent, swap(cotangent, "row", 1)], axis=1)
    cot_full = jnp.concatenate(gather_col(cot_block), axis=0)
    norms_own = jnp.stack([norm1_gain, norm1_bias, norm2_gain, norm2_bias])
    norms = jnp.concatenate([norms_own, swap(norms_own, "row", 1)], axis=1)

    qkv_full = join_rows(
        half(qkv_weight, row, 1), fetch_block(half(qkv_weight, 1 - row, 1), quarter), quarter
    )
    up_full = join_rows(
        half(up_weight, row, 1), fetch_block(half(up_weight, 1 - row, 1), quarter), quarter
    )
    dense_full = join_columns(
        half(dense_weight, row, 0), fetch_block(half(dense_weight, 1 - row, 0), quarter), quarter
    )
    down_full = join_columns(
        half(down_weight, row, 0), fetch_block(half(down_weight, 1 - row, 0), quarter), quarter
    )

    x_full = jnp.concatenate(
        [jnp.concatenate([a, b], axis=1) for a, b in zip(x_own, x_other)], axis=0
    ).astype(F32)
    mean_value = jnp.sum(x_full, axis=1, keepdims=True) / width
    square = jnp.sum(x_full * x_full, axis=1, keepdims=True) / width
    inverse_std = lax.rsqrt(square - mean_value * mean_value + eps_norm)
    normal = (x_full - mean_value) * inverse_std
    normed_one = (normal * norms[0] + norms[1]).astype(BF16)
    normed_two = (normal * norms[2] + norms[3]).astype(BF16)

    segment_blocks = segment_row.reshape(-1, block_rows)
    block_ids = col ^ jnp.arange(segment_blocks.shape[0], dtype=jnp.int32)
    slot_ids = (
        block_ids[:, None] * block_rows + jnp.arange(block_rows, dtype=jnp.int32)[None, :]
    ).reshape(-1)
    segment_own = segment_row[slot_ids]
    starts = jnp.sum((segment_row[None, :] < segment_own[:, None]).astype(jnp.int32), axis=1)
    where_at = (slot_ids - starts).astype(F32)
    inverse = jnp.power(rope_base, -2.0 * jnp.arange(ROT // 2, dtype=F32) / ROT)
    angles = where_at[:, None] * inverse[None, :]
    cosine, sine = jnp.cos(angles), jnp.sin(angles)

    def rotate(vector, sine_part):
        first, second = vector[:, : ROT // 2], vector[:, ROT // 2 : ROT]
        return jnp.concatenate(
            [
                first * cosine - second * sine_part,
                second * cosine + first * sine_part,
                vector[:, ROT:],
            ],
            axis=1,
        )

    mixed = jnp.dot(normed_one, qkv_full, preferred_element_type=F32) + half(qkv_bias, row, 0)
    query = rotate(mixed[:, :HD], sine).astype(BF16)
    keys = rotate(mixed[:, HD : 2 * HD], sine).astype(BF16)
    values = mixed[:, 2 * HD :].astype(BF16)
    allowed = (segment_own[:, None] == segment_own[None, :]) & (
        slot_ids[:, None] >= slot_ids[None, :]
    )
    scores = jnp.einsum("qd,kd->qk", query, keys, preferred_element_type=F32) * scale_value
    scores = jnp.where(allowed, scores, -jnp.inf)
    largest = jnp.max(scores, axis=-1, keepdims=True)
    shifted = jnp.exp(scores - largest)
    totals = jnp.sum(shifted, axis=-1, keepdims=True)
    probs = shifted / totals
    probs_low = probs.astype(BF16)
    attended = jnp.dot(probs_low, values, preferred_element_type=F32).astype(BF16)

    up_value = jnp.dot(normed_two, up_full, preferred_element_type=F32) + half(up_bias, row, 0)
    normal_cdf = 0.5 * (1.0 + lax.erf(up_value * (1.0 / math.sqrt(2.0))))
    hidden = (up_value * normal_cdf).astype(BF16)
    slope = normal_cdf + up_value * jnp.exp(-0.5 * up_value * up_value) * (
        1.0 / math.sqrt(2.0 * math.pi)
    )

    branch = (
        jnp.dot(attended, dense_full, preferred_element_type=F32)
        + jnp.dot(hidden, down_full, preferred_element_type=F32)
    ).astype(BF16)
    branch = branch.reshape(-1, block_rows, width)
    branch_sum = branch[0].astype(F32)
    for mask in range(1, branch.shape[0]):
        branch_sum = branch_sum + swap(branch[mask], "col", mask).astype(F32)
    branch_sum = branch_sum[:, :width_dev] + swap(
        branch_sum[:, width_dev:].astype(BF16), "row", 1
    ).astype(F32)
    block_out = (
        hidden_in.astype(F32) + branch_sum + (dense_bias + down_bias)
    ).astype(BF16)

    def chip_sum(left, right, split):
        if split == "left":
            send_left, keep_left = half(left, 1 - core, 1), half(left, core, 1)
            send_right = keep_right = right
        else:
            send_left = keep_left = left
            send_right, keep_right = half(right, 1 - core, 1), half(right, core, 1)
        dims = (((0,), (0,)), ((), ()))
        sent = lax.dot_general(send_left, send_right, dims, preferred_element_type=F32)
        came = swap(sent.astype(BF16), "dp", 1)
        kept = lax.dot_general(keep_left, keep_right, dims, preferred_element_type=F32)
        return (kept + came.astype(F32)).astype(BF16)

    def finish(own, other):
        done_own = dp_sum(own).astype(BF16)
        done_other = dp_sum(swap(other, "row", 1)).astype(BF16)
        return done_own, swap(done_own, "dp", 1), done_other, swap(done_other, "dp", 1)

    def assemble(parts, axis):
        own, own_core, other, other_core = (part.astype(F32) for part in parts)
        return two(row, two(core, own, own_core, axis), two(core, other, other_core, axis), axis)

    down_part = chip_sum(hidden, cot_full, "left")
    down_grad = assemble(finish(down_part[:, :width_dev], down_part[:, width_dev:]), 0)
    dense_part = chip_sum(attended, cot_full, "left")
    dense_grad = assemble(finish(dense_part[:, :width_dev], dense_part[:, width_dev:]), 0)
    out_bias_grad = jnp.sum(cot_full[:, :width_dev], axis=0, dtype=F32)

    hidden_grad = jnp.einsum("td,cd->tc", cot_full, down_full, preferred_element_type=F32)
    up_grad = (hidden_grad * slope).astype(BF16)
    up_part = chip_sum(normed_two, up_grad, "right")
    up_weight_grad = assemble(finish(up_part[:width_dev], up_part[width_dev:]), 1)
    attended_grad = jnp.einsum(
        "td,cd->tc", cot_full, dense_full, preferred_element_type=F32
    ).astype(BF16)

    probs_grad = jnp.einsum("qd,kd->qk", attended_grad, values, preferred_element_type=F32)
    delta = jnp.sum(probs_grad * probs, axis=-1, keepdims=True)
    scores_grad = (probs * (probs_grad - delta)).astype(BF16)
    query_grad = jnp.dot(scores_grad, keys, preferred_element_type=F32) * scale_value
    key_grad = (
        jnp.einsum("qk,qd->kd", scores_grad, query, preferred_element_type=F32) * scale_value
    )
    value_grad = jnp.einsum("qk,qd->kd", probs_low, attended_grad, preferred_element_type=F32)
    mixed_grad = jnp.concatenate(
        [rotate(query_grad, -sine), rotate(key_grad, -sine), value_grad], axis=1
    ).astype(BF16)
    mixed_part = chip_sum(normed_one, mixed_grad, "right")
    qkv_weight_grad = assemble(finish(mixed_part[:width_dev], mixed_part[width_dev:]), 1)

    grad_one = jnp.einsum("tc,dc->td", mixed_grad, qkv_full, preferred_element_type=F32)
    grad_two = jnp.einsum("tc,dc->td", up_grad, up_full, preferred_element_type=F32)
    norm_sums = jnp.stack(
        [
            jnp.sum(grad_one * normal, axis=0),
            jnp.sum(grad_one, axis=0),
            jnp.sum(grad_two * normal, axis=0),
            jnp.sum(grad_two, axis=0),
        ]
    )
    normal_grad = grad_one * norms[0] + grad_two * norms[2]
    mean_grad = jnp.sum(normal_grad, axis=1, keepdims=True) / width
    mean_along = jnp.sum(normal_grad * normal, axis=1, keepdims=True) / width
    x_grad = inverse_std * (normal_grad - mean_grad - normal * mean_along)
    x_grad_own = x_grad[:, :width_dev]
    x_grad_other = swap(x_grad[:, width_dev:].astype(BF16), "row", 1)
    x_grad_low = (x_grad_own + x_grad_other.astype(F32)).astype(BF16)
    x_grad_low = x_grad_low.reshape(-1, block_rows, width_dev)
    input_grad = cotangent.astype(F32) + x_grad_low[0].astype(F32)
    for mask in range(1, x_grad_low.shape[0]):
        input_grad = input_grad + swap(x_grad_low[mask], "col", mask).astype(F32)

    norm_sums = norm_sums[:, :width_dev] + swap(norm_sums[:, width_dev:], "row", 1)
    norm_sums = small_sum(norm_sums, ("dp", "col"))
    bias_sums = jnp.concatenate(
        [
            jnp.sum(mixed_grad, axis=0, dtype=F32),
            jnp.sum(up_grad, axis=0, dtype=F32),
            out_bias_grad,
        ]
    )
    bias_sums = small_sum(bias_sums, ("dp",))
    heads = mixed_grad.shape[1]
    units = heads + up_grad.shape[1]
    out_bias_grad = bias_sums[units:]
    own_sums = bias_sums[:units]
    other_sums = swap(own_sums, "row", 1)
    qkv_bias_grad = two(row, own_sums[:heads], other_sums[:heads], 0)
    up_bias_grad = two(row, own_sums[heads:], other_sums[heads:], 0)

    return (
        block_out,
        input_grad,
        norm_sums[0],
        norm_sums[1],
        norm_sums[2],
        norm_sums[3],
        qkv_weight_grad,
        qkv_bias_grad,
        dense_grad,
        out_bias_grad,
        up_weight_grad,
        up_bias_grad,
        down_grad,
        out_bias_grad,
    )


def solution(mesh):
    return jax.shard_map(
        shards,
        mesh=mesh,
        in_specs=(
            P(("dp", "col"), "row"),
            P("dp", None),
            P("row"),
            P("row"),
            P("row"),
            P("row"),
            P("row", "col"),
            P("col"),
            P("col", "row"),
            P("row"),
            P("row", "col"),
            P("col"),
            P("col", "row"),
            P("row"),
            P(("dp", "col"), "row"),
        ),
        out_specs=(
            P(("dp", "col"), "row"),
            P(("dp", "col"), "row"),
            P("row"),
            P("row"),
            P("row"),
            P("row"),
            P("row", "col"),
            P("col"),
            P("col", "row"),
            P("row"),
            P("row", "col"),
            P("col"),
            P("col", "row"),
            P("row"),
        ),
        check_vma=False,
    )
```

```python
import functools
import math

import jax
import jax.numpy as jnp
from jax import lax
from jax.experimental import pallas as pl
from jax.experimental.pallas import tpu as pltpu
from jax.sharding import PartitionSpec as P

HD = 256
ROT = 64
F32 = jnp.float32
BF16 = jnp.bfloat16
MESH = pl.DeviceIdType.MESH

eps_norm = 1e-05
rope_base = 10000.0
TILE = 512
NN = (((1,), (0,)), ((), ()))
NT = (((1,), (1,)), ((), ()))
TN = (((0,), (0,)), ((), ()))


def dot(left, right, dims):
    return lax.dot_general(left, right, dims, preferred_element_type=F32)


class Copies:
    def __init__(self, send_sem, recv_sem):
        self.send_sem, self.recv_sem = send_sem, recv_sem
        self.made, self.open = {}, {}

    def start(self, name, source, target, device, when=None):
        index = len(self.made)
        copy = pltpu.make_async_remote_copy(
            src_ref=source,
            dst_ref=target,
            send_sem=self.send_sem.at[index],
            recv_sem=self.recv_sem.at[index],
            device_id=device,
            device_id_type=MESH,
        )
        self.made[name] = copy
        self.open[name] = when
        guarded(when, copy.start)

    def came(self, name, when=None):
        guarded(when, self.made[name].wait_recv)

    def sent(self, *names):
        for name in names:
            guarded(self.open.pop(name), self.made[name].wait_send)

    def sent_all(self):
        self.sent(*list(self.open))


def guarded(when, action):
    if when is None:
        action()
    else:
        pl.when(when)(action)


def at(start, size):
    return pl.ds(pl.multiple_of(start, size), size)


def tiles(count, body):
    lax.fori_loop(0, count, lambda i, carry: (body(i), carry)[1], 0)


def step_kernel(
    sizes,
    hid, cot, wq, wu, wd, wn, seg, gain1, bias1, gain2, bias2, qkv_b, up_b, dense_b, down_b,
    out, in_grad, small, g_qkv, g_dense, g_up, g_down,
    X, G, WQ, WU, WD, WN, N, STAT, QKV, ATT, HID, SLOPE, DUP, DAT, OUTP, ORECV, OY, DZ,
    S_dn, S_de, S_up, S_qk, R_dn, R_de, X_dn, X_de, A_de, TMP, NV, COS, SIN, NSUM, SM, SMO, SMR,
    send_sem, recv_sem, local_sem, credit,
):
    blk, wid, cols = sizes
    rows_all = blk * cols
    width = 2 * wid
    heads, units = WQ.shape[1], WU.shape[1]
    hh, uh, dh = heads // 2, units // 2, HD // 2
    r = lax.axis_index("row")
    c = lax.axis_index("col")
    dp = lax.axis_index("dp")
    k = lax.rem(dp, 2)
    hi = lax.rem(lax.div(dp, 2), 2)
    q = k + 2 * hi
    core_dev = {"dp": dp + 1 - 2 * k}
    x_dev = {"dp": dp + 2 - 4 * hi}
    y_dev = {"row": 1 - r}
    c_low, c_high = lax.rem(c, 2), lax.div(c, 2)
    col_of = [c, c + 1 - 2 * c_low, c + 2 - 4 * c_high, 3 - c]
    own, other = pl.ds(0, wid), pl.ds(wid, wid)
    scale = 1.0 / math.sqrt(HD)
    copies = Copies(send_sem, recv_sem)

    barrier = pltpu.get_barrier_semaphore()
    friends = [core_dev, x_dev, y_dev] + [{"col": col_of[s]} for s in (1, 2, 3)]
    for device in friends:
        pl.semaphore_signal(barrier, inc=1, device_id=device, device_id_type=MESH)

    local = []

    def fetch(source, target):
        copy = pltpu.make_async_copy(source, target, local_sem.at[len(local)])
        copy.start()
        local.append(copy)
        return copy

    fetch_x = fetch(hid, X.at[at(c * blk, blk), own])
    fetch_g = fetch(cot, G.at[at(c * blk, blk), own])
    fetch_u = fetch(wu.at[:, at(r * units, units)], WU.at[own, :])
    fetch_q = fetch(wq.at[:, at(r * heads, heads)], WQ.at[own, :])
    fetch_n = fetch(wn.at[at(r * units, units), :], WN.at[:, own])
    fetch_d = fetch(wd.at[at(r * HD, HD), :], WD.at[:, own])
    pl.semaphore_wait(barrier, len(friends))

    def rows(b):
        return at(b * blk, blk)

    def chain_send(tag, step, buf, columns, first=None):
        for word, move, edge in (("u", 1, c < cols - 1), ("d", -1, c >= 1)):
            block = c - move * (step - 1)
            valid = edge & (block >= 0) & (block <= cols - 1)
            source = first if first is not None else buf.at[rows(block), columns]
            copies.start(
                f"{tag}{word}{step}", source, buf.at[rows(block), columns], {"col": c + move}, valid
            )

    def chain_wait(tag, step):
        copies.came(f"{tag}u{step}", c >= step)
        copies.came(f"{tag}d{step}", c + step <= cols - 1)

    def row_send(name, s):
        b = col_of[s]
        copies.start(name, X.at[rows(b), own], X.at[rows(b), other], y_dev)

    q2 = q + 2 - 4 * hi

    def weight(name, source, full, row0, size, columns):
        def place(quarter):
            return full.at[at(row0 + quarter * size, size), columns]

        copies.start(f"{name}y", source, place(q), y_dev)

        def pass_on():
            copies.came(f"{name}y")
            copies.start(f"{name}x", place(q), place(q), x_dev)
            copies.start(f"{name}c", place(q), place(q), core_dev)

        def pass_far():
            copies.came(f"{name}x")
            copies.start(f"{name}f", place(q2), place(q2), core_dev)

        def done():
            copies.came(f"{name}c")
            copies.came(f"{name}f")

        return pass_on, pass_far, done

    everything = slice(None)
    chain_send("x", 1, X, own, hid)
    copies.start("xy0", hid, X.at[rows(c), other], y_dev)
    for j, vector in enumerate((gain1, bias1, gain2, bias2)):
        copies.start(f"nv{j}", vector, NV.at[pl.ds(j, 1), other], y_dev)
    wq4, wn4, wd4 = wid // 4, units // 4, HD // 4
    wu_on, wu_far, wu_done = weight(
        "wu", wu.at[at(q * wq4, wq4), at((1 - r) * units, units)], WU, wid, wq4, everything
    )

    seg_row = seg[...].astype(F32)
    seg_col = jnp.transpose(jnp.broadcast_to(seg_row, (128, rows_all)))
    STAT[:, 3:4] = seg_col[:, 0:1]
    for j, vector in enumerate((gain1, bias1, gain2, bias2)):
        NV[j : j + 1, own] = vector[...]

    def table(i):
        block = at(i * blk, blk)
        starts = jnp.sum(
            (seg_row < STAT[block, 3:4]).astype(F32), axis=1, keepdims=True
        )
        index = lax.broadcasted_iota(jnp.int32, (blk, 1), 0) + i * blk
        lane = lax.broadcasted_iota(jnp.int32, (1, 128), 1)
        turn = jnp.exp(
            lax.rem(lane, ROT // 2).astype(F32) * (-2.0 * math.log(rope_base) / ROT)
        )
        angles = (index.astype(F32) - starts) * turn
        COS[block, :] = jnp.where(lane < ROT, jnp.cos(angles), 1.0)
        SIN[block, :] = jnp.where(
            lane < ROT // 2, -jnp.sin(angles), jnp.where(lane < ROT, jnp.sin(angles), 0.0)
        )

    tiles(cols, table)

    def rotate(head, block, sign):
        first = head[:, :128]
        lane = lax.broadcasted_iota(jnp.int32, first.shape, 1)
        swapped = jnp.where(
            lane < ROT // 2, pltpu.roll(first, 128 - ROT // 2, 1), pltpu.roll(first, ROT // 2, 1)
        )
        turned = first * COS[block, :] + sign * (swapped * SIN[block, :])
        return jnp.concatenate([turned, head[:, 128:]], axis=1)

    sub = 64

    def norm_block(b):
        def part(i):
            rs = at(b * blk + i * sub, sub)
            x = X[rs, :].astype(F32)
            mean = jnp.sum(x, axis=1, keepdims=True) * (1.0 / width)
            square = jnp.sum(x * x, axis=1, keepdims=True) * (1.0 / width)
            inv = lax.rsqrt(square - mean * mean + eps_norm)
            STAT[rs, 0:1] = mean
            STAT[rs, 1:2] = inv
            normal = (x - mean) * inv
            OUTP[rs, :] = (normal * NV[0:1, :] + NV[1:2, :]).astype(BF16)
            N[rs, :] = (normal * NV[2:3, :] + NV[3:4, :]).astype(BF16)

        tiles(blk // sub, part)

    def up_block(b):
        def part(j):
            cs = at(j * TILE, TILE)
            bias = up_b[:, at(r * units + j * TILE, TILE)]
            up = dot(N[rows(b), :], WU[:, cs], NN) + bias
            cdf = 0.5 * (1.0 + lax.erf(up * (1.0 / math.sqrt(2.0))))
            HID[rows(b), cs] = (up * cdf).astype(BF16)
            SLOPE[rows(b), cs] = (
                cdf + up * jnp.exp(-0.5 * up * up) * (1.0 / math.sqrt(2.0 * math.pi))
            ).astype(BF16)

        tiles(units // TILE, part)

    fetch_x.wait()
    fetch_g.wait()
    chain_wait("x", 1)
    chain_send("x", 2, X, own)
    row_send("xy1", 1)
    copies.start("gy", cot, G.at[rows(c), other], y_dev)
    wu_on()
    chain_wait("x", 2)
    chain_send("x", 3, X, own)
    row_send("xy2", 2)
    chain_send("g", 1, G, own, cot)
    wu_far()
    fetch_u.wait()
    for j in range(4):
        copies.came(f"nv{j}")
    copies.came("xy0")
    norm_block(col_of[0])
    chain_wait("x", 3)
    row_send("xy3", 3)
    wq_on, wq_far, wq_done = weight(
        "wq", wq.at[at(q * wq4, wq4), at((1 - r) * heads, heads)], WQ, wid, wq4, everything
    )
    wn_on, wn_far, wn_done = weight(
        "wn", wn.at[at((1 - r) * units + q * wn4, wn4), :], WN, 0, wn4, other
    )
    wd_on, wd_far, wd_done = weight(
        "wd", wd.at[at((1 - r) * HD + q * wd4, wd4), :], WD, 0, wd4, other
    )
    wu_done()
    up_block(col_of[0])
    copies.came("xy1")
    norm_block(col_of[1])
    up_block(col_of[1])
    chain_wait("g", 1)
    chain_send("g", 2, G, own)
    copies.came("xy2")
    norm_block(col_of[2])
    up_block(col_of[2])
    copies.came("xy3")
    norm_block(col_of[3])
    chain_wait("g", 2)
    chain_send("g", 3, G, own)
    copies.came("gy")
    chain_send("h", 1, G, other)
    up_block(col_of[3])

    def grad_send(name, staged, left, right, n_rows, n_cols, target):
        def part(i):
            cs = at(i * TILE, TILE)
            staged[:, cs] = dot(left(None), right(cs), TN).astype(BF16)

        tiles(n_cols // TILE, part)
        copies.start(name, staged, target, core_dev)

    hid_keep, hid_send = at(k * uh, uh), at((1 - k) * uh, uh)
    att_keep, att_send = at(k * dh, dh), at((1 - k) * dh, dh)

    def out_grad(name, side, left_ref, keep, give, staged, landing):
        base = side * wid

        def give_part(i):
            cs = at(i * TILE, TILE)
            staged[:, cs] = dot(
                left_ref[:, give], G[:, at(base + i * TILE, TILE)], TN
            ).astype(BF16)

        tiles(wid // TILE, give_part)
        copies.start(f"{name}a", staged, landing, core_dev)

    def out_keep(name, side, left_ref, keep, landing):
        base = side * wid
        copies.came(f"{name}a")

        def keep_part(i):
            cs = at(i * TILE, TILE)
            mine = dot(left_ref[:, keep], G[:, at(base + i * TILE, TILE)], TN)
            landing[:, cs] = (mine + landing[:, cs].astype(F32)).astype(BF16)

        tiles(wid // TILE, keep_part)

    chain_wait("g", 3)
    out_grad("dn0", 0, HID, hid_keep, hid_send, DUP.at[pl.ds(0, uh), :], S_dn.at[0])
    out_keep("dn0", 0, HID, hid_keep, S_dn.at[0])
    copies.start("dn0x", S_dn.at[0], X_dn.at[0], x_dev)

    wq_on()
    fetch_q.wait()
    chain_wait("h", 1)
    chain_send("h", 2, G, other)
    wn_on()
    wd_on()
    wq_far()
    wq_done()

    def qkv_block(i):
        block = at(i * blk, blk)
        for j in range(3):
            bias = qkv_b[:, at(r * heads + j * HD, HD)]
            value = dot(OUTP[block, :], WQ[:, j * HD : (j + 1) * HD], NN) + bias
            if j < 2:
                value = rotate(value, block, 1.0)
            QKV[block, j * HD : (j + 1) * HD] = value.astype(BF16)

    tiles(cols, qkv_block)
    wn_far()
    wd_far()

    def key_range(i):
        low = max(0, i - 2) * blk
        return slice(i * blk, (i + 1) * blk), slice(low, (i + 1) * blk), low

    def block_scores(i):
        mine, span, low = key_range(i)
        n = span.stop - low
        s = dot(QKV[mine, 0:HD], QKV[span, HD : 2 * HD], NT) * scale
        row_id = lax.broadcasted_iota(jnp.int32, (blk, n), 0) + i * blk
        col_id = lax.broadcasted_iota(jnp.int32, (blk, n), 1) + low
        same = STAT[mine, 3:4] == seg_row[:, span]
        return jnp.where(same & (col_id <= row_id), s, -1e30)

    for i in range(cols):
        mine, span, low = key_range(i)
        s = block_scores(i)
        largest = jnp.max(s, axis=1, keepdims=True)
        p = jnp.exp(s - largest)
        total = jnp.sum(p, axis=1, keepdims=True)
        STAT[mine, 2:3] = largest + jnp.log(total)
        p_low = (p / total).astype(BF16)
        ATT[mine, :] = dot(p_low, QKV[span, 2 * HD :], NN).astype(BF16)
    chain_wait("h", 2)
    chain_send("h", 3, G, other)
    fetch_n.wait()
    fetch_d.wait()
    wn_done()
    wd_done()

    def branch_block(b):
        def part(j):
            cs = at(j * TILE, TILE)
            both = dot(ATT[rows(b), :], WD[:, cs], NN) + dot(HID[rows(b), :], WN[:, cs], NN)
            OUTP[rows(b), cs] = both.astype(BF16)

        tiles(width // TILE, part)

    chain_wait("h", 3)
    for s in (1, 2, 3):
        branch_block(col_of[s])
        copies.start(
            f"oz{s}", OUTP.at[rows(col_of[s]), :], ORECV.at[s - 1], {"col": col_of[s]}
        )
    out_grad("dn1", 1, HID, hid_keep, hid_send, DUP.at[pl.ds(uh, uh), :], S_dn.at[1])
    out_grad("de0", 0, ATT, att_keep, att_send, A_de.at[0], S_de.at[0])
    out_grad("de1", 1, ATT, att_keep, att_send, A_de.at[1], S_de.at[1])
    out_keep("dn1", 1, HID, hid_keep, S_dn.at[1])
    copies.start("dn1y", S_dn.at[1], R_dn, y_dev)
    branch_block(col_of[0])

    copies.sent("dn0a", "dn1a")

    def up_grad_part(i):
        block = at(i * blk, blk)
        for j in range(units // TILE):
            cs = slice(j * TILE, (j + 1) * TILE)
            back = dot(G[block, :], WN[cs, :], NT)
            DUP[block, cs] = (back * SLOPE[block, cs].astype(F32)).astype(BF16)

    tiles(cols, up_grad_part)
    keep_u, give_u = at(k * uh, uh), at((1 - k) * uh, uh)
    keep_h, give_h = at(k * hh, hh), at((1 - k) * hh, hh)

    def in_give(name, right_ref, give, n, staged, landing):
        for side in (0, 1):

            def part(i):
                rs = at(i * TILE, TILE)
                lefts = N[:, at(side * wid + i * TILE, TILE)]
                staged[side][rs, :] = dot(lefts, right_ref[:, give], TN).astype(BF16)

            tiles(wid // TILE, part)
            copies.start(f"{name}{side}a", staged[side], landing.at[side], core_dev)

    def in_keep(name, side, right_ref, keep, landing):
        copies.came(f"{name}{side}a")

        def part(i):
            rs = at(i * TILE, TILE)
            mine = dot(N[:, at(side * wid + i * TILE, TILE)], right_ref[:, keep], TN)
            landing[side, rs, :] = (mine + landing[side, rs, :].astype(F32)).astype(BF16)

        tiles(wid // TILE, part)

    in_give(
        "up", DUP, give_u, uh, [HID.at[:, pl.ds(0, uh)], HID.at[:, pl.ds(uh, uh)]], S_up
    )
    for i in range(cols):
        mine = slice(i * blk, (i + 1) * blk)
        DAT[mine, :] = dot(G[mine, :], WD[...], NT).astype(BF16)
    SM[6:7, :] = jnp.sum(G[:, own].astype(F32), axis=0, keepdims=True)
    out_keep("de0", 0, ATT, att_keep, S_de.at[0])
    out_keep("de1", 1, ATT, att_keep, S_de.at[1])

    copies.sent(*[f"{t}{w}{s}" for t in "gh" for w in "ud" for s in (1, 2, 3)])
    copies.sent("wnx", "wnc", "wnf")
    pl.semaphore_signal(credit.at[0], inc=1, device_id=x_dev, device_id_type=MESH)
    pl.semaphore_signal(credit.at[1], inc=1, device_id=y_dev, device_id_type=MESH)
    R_up, X_up = G.at[:, pl.ds(2 * uh, uh)], [G.at[:, pl.ds(j * uh, uh)] for j in (0, 1)]
    R_qk, X_qk = WN.at[:, pl.ds(2 * hh, hh)], [WN.at[:, pl.ds(j * hh, hh)] for j in (0, 1)]

    in_keep("up", 0, DUP, keep_u, S_up)
    pl.semaphore_wait(credit.at[0], 1)
    copies.start("up0x", S_up.at[0], X_up[0], x_dev)
    in_keep("up", 1, DUP, keep_u, S_up)
    pl.semaphore_wait(credit.at[1], 1)
    copies.start("up1y", S_up.at[1], R_up, y_dev)
    copies.start("de0x", S_de.at[0], X_de.at[0], x_dev)
    copies.start("de1y", S_de.at[1], R_de, y_dev)
    copies.sent("up0a", "up1a")
    pl.semaphore_signal(credit.at[2], inc=1, device_id=y_dev, device_id_type=MESH)

    def again(i):
        rs = at(i * sub, sub)
        normal = (X[rs, :].astype(F32) - STAT[rs, 0:1]) * STAT[rs, 1:2]
        N[rs, :] = (normal * NV[0:1, :] + NV[1:2, :]).astype(BF16)

    tiles(rows_all // sub, again)
    TMP[...] = jnp.zeros_like(TMP)
    for i in range(cols):
        mine, span, low = key_range(i)
        query = QKV[mine, 0:HD]
        p = jnp.exp(block_scores(i) - STAT[mine, 2:3])
        d_p = dot(DAT[mine, :], QKV[span, 2 * HD :], NT)
        delta = jnp.sum(d_p * p, axis=1, keepdims=True)
        d_s = (p * (d_p - delta)).astype(BF16)
        p_low = p.astype(BF16)
        d_query = dot(d_s, QKV[span, HD : 2 * HD], NN) * scale
        QKV[mine, 0:HD] = rotate(d_query, mine, -1.0).astype(BF16)
        for j in range(low // blk, i + 1):
            js = slice(j * blk - low, (j + 1) * blk - low)
            ks, vs = slice(j * HD, (j + 1) * HD), slice((cols + j) * HD, (cols + j + 1) * HD)
            TMP[:, ks] += dot(d_s[:, js], query, TN)
            TMP[:, vs] += dot(p_low[:, js], DAT[mine, :], TN)
    for j in range(cols):
        mine = slice(j * blk, (j + 1) * blk)
        ks, vs = slice(j * HD, (j + 1) * HD), slice((cols + j) * HD, (cols + j + 1) * HD)
        QKV[mine, HD : 2 * HD] = rotate(TMP[:, ks] * scale, mine, -1.0).astype(BF16)
        QKV[mine, 2 * HD :] = TMP[:, vs].astype(BF16)

    in_give(
        "qk", QKV, give_h, hh, [SLOPE.at[:, pl.ds(0, hh)], SLOPE.at[:, pl.ds(hh, hh)]], S_qk
    )
    copies.came("dn1y")
    copies.start("dn1x", R_dn, X_dn.at[1], x_dev)
    in_keep("qk", 0, QKV, keep_h, S_qk)
    copies.start("qk0x", S_qk.at[0], X_qk[0], x_dev)
    in_keep("qk", 1, QKV, keep_h, S_qk)
    copies.start("qk1y", S_qk.at[1], R_qk, y_dev)

    def finish(name, total, came, result, here):
        copies.came(f"{name}x")
        n = total.shape[0]
        step = min(n, 128)

        def part(i):
            rs = at(i * step, step)
            came[rs, :] = (total[rs, :].astype(F32) + came[rs, :].astype(F32)).astype(BF16)

        tiles(n // step, part)
        fetch(came, result.at[here])
        copies.start(f"{name}t", came, result.at[here], core_dev)

    wide = slice(None)

    def down_at(side):
        return (at(side * units + k * uh, uh), wide)

    def dense_at(side):
        return (at(side * HD + k * dh, dh), wide)

    def up_at(side):
        return (wide, at(side * units + k * uh, uh))

    def qkv_at(side):
        return (wide, at(side * heads + k * hh, hh))

    finish("dn0", S_dn.at[0], X_dn.at[0], g_down, down_at(r))

    NSUM[...] = jnp.zeros_like(NSUM)
    pl.semaphore_wait(credit.at[2], 1)

    def norm_back(b):
        rb = rows(b)
        mean, inv = STAT[rb, 0:1], STAT[rb, 1:2]

        def first(j, carry):
            along, plain = carry
            cs = at(j * TILE, TILE)
            one = dot(QKV[rb, :], WQ[cs, :], NT)
            two = dot(DUP[rb, :], WU[cs, :], NT)
            normal = (X[rb, cs].astype(F32) - mean) * inv
            NSUM[0:1, cs] += jnp.sum(one * normal, axis=0, keepdims=True)
            NSUM[1:2, cs] += jnp.sum(one, axis=0, keepdims=True)
            NSUM[2:3, cs] += jnp.sum(two * normal, axis=0, keepdims=True)
            NSUM[3:4, cs] += jnp.sum(two, axis=0, keepdims=True)
            grad = one * NV[0:1, cs] + two * NV[2:3, cs]
            TMP[:, cs] = grad
            along = along + jnp.sum(grad * normal, axis=1, keepdims=True)
            plain = plain + jnp.sum(grad, axis=1, keepdims=True)
            return along, plain

        zero = jnp.zeros((blk, 1), F32)
        along, plain = lax.fori_loop(0, width // TILE, first, (zero, zero))
        along, plain = along * (1.0 / width), plain * (1.0 / width)

        def second(j):
            cs = at(j * TILE, TILE)
            normal = (X[rb, cs].astype(F32) - mean) * inv
            N[rb, cs] = (inv * (TMP[:, cs] - plain - normal * along)).astype(BF16)

        tiles(width // TILE, second)

    for s in (1, 2, 3, 0):
        norm_back(col_of[s])
        copies.start(
            f"ey{s}", N.at[rows(col_of[s]), other], HID.at[rows(col_of[s]), :], y_dev
        )
        if s == 1:
            copies.came("up1y")
            copies.start("up1x", R_up, X_up[1], x_dev)
        if s == 2:
            copies.came("de1y")
            copies.start("de1x", R_de, X_de.at[1], x_dev)

    SM[0:4, :] = NSUM[0:4, own]
    SM[4:5, :] = jnp.sum(DUP[...].astype(F32), axis=0, keepdims=True)
    SM[5:6, 0:heads] = jnp.sum(QKV[...].astype(F32), axis=0, keepdims=True)
    SM[5:6, heads:] = jnp.zeros((1, wid - heads), F32)
    SM[7:8, :] = jnp.zeros((1, wid), F32)
    SMO[0:4, :] = NSUM[0:4, other]
    SMO[4:8, :] = jnp.zeros((4, wid), F32)
    copies.start("s0", SMO, SMR.at[0], y_dev)

    def small_next(j, device, top):
        def action():
            copies.came(f"s{j - 1}")
            copies.sent(f"s{j - 1}")
            SM[0:top, :] = SM[0:top, :] + SMR[j - 1, 0:top, :]
            if device is not None:
                copies.start(f"s{j}", SM, SMR.at[j], device)

        return action

    mine = rows(c)
    for s in (1, 2, 3):
        copies.came(f"oz{s}")

    def branch_sum(part, columns):
        rs = at(part * sub, sub)
        total = OUTP[at(c * blk + part * sub, sub), columns].astype(F32)
        for s in (1, 2, 3):
            total = total + ORECV[s - 1, rs, columns].astype(F32)
        return total

    def out_other(i):
        OUTP[at(c * blk + i * sub, sub), other] = branch_sum(i, other).astype(BF16)

    tiles(blk // sub, out_other)
    copies.start("oy", OUTP.at[mine, other], OY, y_dev)

    def x_block(s):
        def action():
            b = col_of[s]
            copies.came(f"ey{s}")

            def part(i):
                rs = at(b * blk + i * sub, sub)
                N[rs, own] = (N[rs, own].astype(F32) + HID[rs, :].astype(F32)).astype(BF16)

            tiles(blk // sub, part)
            if s > 0:
                copies.start(f"ez{s}", N.at[rows(b), own], DZ.at[s - 1], {"col": b})

        return action

    def out_last():
        copies.came("oy")

        def part(i):
            rs = at(i * sub, sub)
            total = branch_sum(i, own) + OY[rs, :].astype(F32)
            total = total + X[at(c * blk + i * sub, sub), own].astype(F32)
            out[rs, :] = (total + (dense_b[...] + down_b[...])).astype(BF16)

        tiles(blk // sub, part)

    def x_last():
        for s in (1, 2, 3):
            copies.came(f"ez{s}")

        def part(i):
            rs = at(i * sub, sub)
            total = N[at(c * blk + i * sub, sub), own].astype(F32)
            for s in (1, 2, 3):
                total = total + DZ[s - 1, rs, :].astype(F32)
            in_grad[rs, :] = cot[rs, :].astype(F32) + total

        tiles(blk // sub, part)

    def send_qk():
        copies.came("qk1y")
        copies.start("qk1x", R_qk, X_qk[1], x_dev)

    finish("up0", S_up.at[0], X_up[0], g_up, up_at(r))
    small_next(1, {"col": col_of[1]}, 4)()
    finish("de0", S_de.at[0], X_de.at[0], g_dense, dense_at(r))
    send_qk()
    small_next(2, {"col": col_of[2]}, 4)()
    finish("dn1", R_dn, X_dn.at[1], g_down, down_at(1 - r))
    x_block(1)()
    small_next(3, core_dev, 4)()
    finish("qk0", S_qk.at[0], X_qk[0], g_qkv, qkv_at(r))
    x_block(2)()
    small_next(4, x_dev, 8)()
    x_block(3)()
    finish("up1", R_up, X_up[1], g_up, up_at(1 - r))
    small_next(5, None, 8)()
    copies.start("s5", SM, SMR.at[5], y_dev)
    x_block(0)()
    finish("de1", R_de, X_de.at[1], g_dense, dense_at(1 - r))
    out_last()
    copies.came("s5")
    small[0:8, :] = SM[...]
    small[8:16, :] = SMR[5]
    x_last()
    finish("qk1", R_qk, X_qk[1], g_qkv, qkv_at(1 - r))
    for name in ("dn0", "up0", "de0", "dn1", "qk0", "up1", "de1", "qk1"):
        copies.came(f"{name}t")
    for copy in local[6:]:
        copy.wait()
    copies.sent_all()


def scratch(blk, wid, cols, units, heads):
    tokens, width = blk * cols, 2 * wid
    low = [
        (tokens, width), (tokens, width), (width, heads), (width, units), (HD, width),
        (units, width), (tokens, width),
    ]
    V = pltpu.VMEM
    return (
        [V(shape, BF16) for shape in low]
        + [V((tokens, 128), F32)]
        + [
            V(shape, BF16)
            for shape in (
                (tokens, heads), (tokens, HD), (tokens, units), (tokens, units), (tokens, units),
                (tokens, HD), (tokens, width), (3, blk, width), (blk, wid), (3, blk, wid),
                (2, units // 2, wid), (2, HD // 2, wid), (2, wid, units // 2), (2, wid, heads // 2),
                (units // 2, wid), (HD // 2, wid), (2, units // 2, wid), (2, HD // 2, wid),
                (2, HD // 2, wid),
            )
        ]
        + [
            V((blk, width), F32),
            V((8, width), F32),
            V((tokens, 128), F32),
            V((tokens, 128), F32),
            V((8, width), F32),
            V((8, wid), F32),
            V((8, wid), F32),
            V((6, 8, wid), F32),
            pltpu.SemaphoreType.DMA((100,)),
            pltpu.SemaphoreType.DMA((100,)),
            pltpu.SemaphoreType.DMA((16,)),
            pltpu.SemaphoreType.REGULAR((3,)),
        ]
    )


def swap(value, axis, mask):
    size = lax.axis_size(axis)
    return lax.ppermute(value, axis, [(i, i ^ mask) for i in range(size)])


def shards(
    hidden_in,
    segment,
    norm1_gain,
    norm1_bias,
    norm2_gain,
    norm2_bias,
    qkv_weight,
    qkv_bias,
    dense_weight,
    dense_bias,
    up_weight,
    up_bias,
    down_weight,
    down_bias,
    cotangent,
):
    blk, wid = hidden_in.shape
    cols = lax.axis_size("col")
    heads, units = qkv_weight.shape[1] // 2, up_weight.shape[1] // 2
    vectors = [
        v.reshape(1, -1)
        for v in (
            norm1_gain, norm1_bias, norm2_gain, norm2_bias, qkv_bias, up_bias, dense_bias, down_bias,
        )
    ]
    vmem = pl.BlockSpec(memory_space=pltpu.VMEM)
    far = pl.BlockSpec(memory_space=pl.ANY)
    shape = jax.ShapeDtypeStruct
    out, in_grad, small, g_qkv, g_dense, g_up, g_down = pl.pallas_call(
        functools.partial(step_kernel, (blk, wid, cols)),
        out_shape=(
            shape((blk, wid), BF16),
            shape((blk, wid), F32),
            shape((16, wid), F32),
            shape(qkv_weight.shape, BF16),
            shape(dense_weight.shape, BF16),
            shape(up_weight.shape, BF16),
            shape(down_weight.shape, BF16),
        ),
        in_specs=[vmem, vmem] + [far] * 4 + [vmem] * 9,
        out_specs=(vmem,) * 3 + (far,) * 4,
        scratch_shapes=scratch(blk, wid, cols, units, heads),
        compiler_params=pltpu.CompilerParams(
            collective_id=0, has_side_effects=True, vmem_limit_bytes=67043328
        ),
        name="step",
    )(
        hidden_in, cotangent, qkv_weight, up_weight, dense_weight, down_weight, segment, *vectors
    )

    grads = [g.astype(F32) for g in (g_qkv, g_dense, g_up, g_down)]
    mask = 4
    while mask < lax.axis_size("dp"):
        grads = [g + swap(g.astype(BF16), "dp", mask).astype(F32) for g in grads]
        small = small + swap(small, "dp", mask)
        mask *= 2
    row = lax.axis_index("row")

    def both(index):
        first, second = small[index], small[8 + index]
        return jnp.where(row == 0, first, second), jnp.where(row == 0, second, first)

    qkv_bias_grad = jnp.concatenate([part[:heads] for part in both(5)])
    up_bias_grad = jnp.concatenate(both(4))
    return (
        out,
        in_grad,
        small[0],
        small[1],
        small[2],
        small[3],
        grads[0],
        qkv_bias_grad,
        grads[1],
        small[6],
        grads[2],
        up_bias_grad,
        grads[3],
        small[6],
    )


def solution(mesh):
    return jax.shard_map(
        shards,
        mesh=mesh,
        in_specs=(
            P(("dp", "col"), "row"),
            P("dp", None),
            P("row"),
            P("row"),
            P("row"),
            P("row"),
            P("row", "col"),
            P("col"),
            P("col", "row"),
            P("row"),
            P("row", "col"),
            P("col"),
            P("col", "row"),
            P("row"),
            P(("dp", "col"), "row"),
        ),
        out_specs=(
            P(("dp", "col"), "row"),
            P(("dp", "col"), "row"),
            P("row"),
            P("row"),
            P("row"),
            P("row"),
            P("row", "col"),
            P("col"),
            P("col", "row"),
            P("row"),
            P("row", "col"),
            P("col"),
            P("col", "row"),
            P("row"),
        ),
        check_vma=False,
    )
```

```python
import functools
import math

import jax
import jax.numpy as jnp
from jax import lax
from jax.experimental import pallas as pl
from jax.experimental.pallas import tpu as pltpu
from jax.sharding import PartitionSpec as P

HD = 256
ROT = 64
F32 = jnp.float32
BF16 = jnp.bfloat16
MESH = pl.DeviceIdType.MESH

eps_norm = 1e-05
rope_base = 10000.0
TILE = 512
NN = (((1,), (0,)), ((), ()))
NT = (((1,), (1,)), ((), ()))
TN = (((0,), (0,)), ((), ()))


def dot(left, right, dims):
    return lax.dot_general(left, right, dims, preferred_element_type=F32)


class Copies:
    def __init__(self, send_sem, recv_sem):
        self.send_sem, self.recv_sem = send_sem, recv_sem
        self.made, self.open = {}, {}

    def start(self, name, source, target, device, when=None):
        index = len(self.made)
        copy = pltpu.make_async_remote_copy(
            src_ref=source,
            dst_ref=target,
            send_sem=self.send_sem.at[index],
            recv_sem=self.recv_sem.at[index],
            device_id=device,
            device_id_type=MESH,
        )
        self.made[name] = copy
        self.open[name] = when
        guarded(when, copy.start)

    def came(self, name, when=None):
        guarded(when, self.made[name].wait_recv)

    def sent(self, *names):
        for name in names:
            guarded(self.open.pop(name), self.made[name].wait_send)

    def sent_all(self):
        self.sent(*list(self.open))


def guarded(when, action):
    if when is None:
        action()
    else:
        pl.when(when)(action)


def at(start, size):
    return pl.ds(pl.multiple_of(start, size), size)


def tiles(count, body):
    lax.fori_loop(0, count, lambda i, carry: (body(i), carry)[1], 0)


def step_kernel(
    sizes,
    hid, cot, wq, wu, wd, wn, seg, gain1, bias1, gain2, bias2, qkv_b, up_b, dense_b, down_b,
    out, in_grad, small, g_qkv, g_dense, g_up, g_down,
    X, G, WQ, WU, WD, WN, N, STAT, QKV, ATT, HID, SLOPE, DUP, DAT, OUTP, OZ1, OZ, OY, DZ1, DZ,
    S_dn, S_de, S_up, S_qk, R_dn, R_de, V_dn, V_de, X_dn, X_de, A_de, TMP, NV, COS, SIN, NSUM, SM, SMO, SMR,
    send_sem, recv_sem, local_sem, credit,
):
    blk, wid, cols = sizes
    rows_all = blk * cols
    width = 2 * wid
    heads, units = WQ.shape[1], WU.shape[1]
    hh, uh, dh = heads // 2, units // 2, HD // 2
    r = lax.axis_index("row")
    c = lax.axis_index("col")
    dp = lax.axis_index("dp")
    k = lax.rem(dp, 2)
    hi = lax.rem(lax.div(dp, 2), 2)
    q = k + 2 * hi
    core_dev = {"dp": dp + 1 - 2 * k}
    x_dev = {"dp": dp + 2 - 4 * hi}
    y_dev = {"row": 1 - r}
    c_low, c_high = lax.rem(c, 2), lax.div(c, 2)
    col_of = [c, c + 1 - 2 * c_low, c + 2 - 4 * c_high, 3 - c]
    own, other = pl.ds(0, wid), pl.ds(wid, wid)
    scale = 1.0 / math.sqrt(HD)
    copies = Copies(send_sem, recv_sem)

    barrier = pltpu.get_barrier_semaphore()
    friends = [core_dev, x_dev, y_dev] + [{"col": col_of[s]} for s in (1, 2, 3)]
    for device in friends:
        pl.semaphore_signal(barrier, inc=1, device_id=device, device_id_type=MESH)

    local = []

    def fetch(source, target):
        copy = pltpu.make_async_copy(source, target, local_sem.at[len(local)])
        copy.start()
        local.append(copy)
        return copy

    fetch_x = fetch(hid, X.at[at(c * blk, blk), own])
    fetch_g = fetch(cot, G.at[at(c * blk, blk), own])
    fetch_u = fetch(wu.at[:, at(r * units, units)], WU.at[own, :])
    fetch_q = fetch(wq.at[:, at(r * heads, heads)], WQ.at[own, :])
    fetch_n = fetch(wn.at[at(r * units, units), :], WN.at[:, own])
    fetch_d = fetch(wd.at[at(r * HD, HD), :], WD.at[:, own])
    pl.semaphore_wait(barrier, len(friends))

    def rows(b):
        return at(b * blk, blk)

    def chain_send(tag, step, buf, columns, first=None):
        for word, move, edge in (("u", 1, c < cols - 1), ("d", -1, c >= 1)):
            block = c - move * (step - 1)
            valid = edge & (block >= 0) & (block <= cols - 1)
            source = first if first is not None else buf.at[rows(block), columns]
            copies.start(
                f"{tag}{word}{step}", source, buf.at[rows(block), columns], {"col": c + move}, valid
            )

    def chain_wait(tag, step):
        copies.came(f"{tag}u{step}", c >= step)
        copies.came(f"{tag}d{step}", c + step <= cols - 1)

    def row_send(name, s):
        b = col_of[s]
        copies.start(name, X.at[rows(b), own], X.at[rows(b), other], y_dev)

    q2 = q + 2 - 4 * hi

    def weight(name, source, full, row0, size, columns, spread):
        share = q if spread else k

        def place(index):
            return full.at[at(row0 + index * size, size), columns]

        copies.start(f"{name}y", source(at(share * size, size)), place(share), y_dev)

        def pass_on():
            copies.came(f"{name}y")
            if spread:
                copies.start(f"{name}x", place(q), place(q), x_dev)
            copies.start(f"{name}c", place(share), place(share), core_dev)

        def pass_far():
            copies.came(f"{name}x")
            copies.start(f"{name}f", place(q2), place(q2), core_dev)

        def done():
            copies.came(f"{name}c")
            if spread:
                copies.came(f"{name}f")

        return pass_on, pass_far, done

    everything = slice(None)
    chain_send("x", 1, X, own, hid)
    copies.start("xy0", hid, X.at[rows(c), other], y_dev)
    for j, vector in enumerate((gain1, bias1, gain2, bias2)):
        copies.start(f"nv{j}", vector, NV.at[pl.ds(j, 1), other], y_dev)
    wu_on, wu_far, wu_done = weight(
        "wu", lambda rs: wu.at[rs, at((1 - r) * units, units)], WU, wid, wid // 4, everything, True
    )

    seg_row = seg[...].astype(F32)
    seg_col = jnp.transpose(jnp.broadcast_to(seg_row, (128, rows_all)))
    STAT[:, 3:4] = seg_col[:, 0:1]
    for j, vector in enumerate((gain1, bias1, gain2, bias2)):
        NV[j : j + 1, own] = vector[...]

    def table(i):
        block = at(i * blk, blk)
        starts = jnp.sum(
            (seg_row < STAT[block, 3:4]).astype(F32), axis=1, keepdims=True
        )
        index = lax.broadcasted_iota(jnp.int32, (blk, 1), 0) + i * blk
        lane = lax.broadcasted_iota(jnp.int32, (1, 128), 1)
        turn = jnp.exp(
            lax.rem(lane, ROT // 2).astype(F32) * (-2.0 * math.log(rope_base) / ROT)
        )
        angles = (index.astype(F32) - starts) * turn
        COS[block, :] = jnp.where(lane < ROT, jnp.cos(angles), 1.0)
        SIN[block, :] = jnp.where(
            lane < ROT // 2, -jnp.sin(angles), jnp.where(lane < ROT, jnp.sin(angles), 0.0)
        )

    tiles(cols, table)

    def rotate(head, block, sign):
        first = head[:, :128]
        lane = lax.broadcasted_iota(jnp.int32, first.shape, 1)
        swapped = jnp.where(
            lane < ROT // 2, pltpu.roll(first, 128 - ROT // 2, 1), pltpu.roll(first, ROT // 2, 1)
        )
        turned = first * COS[block, :] + sign * (swapped * SIN[block, :])
        return jnp.concatenate([turned, head[:, 128:]], axis=1)

    sub = 64

    def norm_block(b):
        def part(i):
            rs = at(b * blk + i * sub, sub)
            x = X[rs, :].astype(F32)
            mean = jnp.sum(x, axis=1, keepdims=True) * (1.0 / width)
            square = jnp.sum(x * x, axis=1, keepdims=True) * (1.0 / width)
            inv = lax.rsqrt(square - mean * mean + eps_norm)
            STAT[rs, 0:1] = mean
            STAT[rs, 1:2] = inv
            normal = (x - mean) * inv
            OUTP[rs, :] = (normal * NV[0:1, :] + NV[1:2, :]).astype(BF16)
            N[rs, :] = (normal * NV[2:3, :] + NV[3:4, :]).astype(BF16)

        tiles(blk // sub, part)

    def up_block(b):
        def part(j):
            cs = at(j * TILE, TILE)
            bias = up_b[:, at(r * units + j * TILE, TILE)]
            up = dot(N[rows(b), :], WU[:, cs], NN) + bias
            cdf = 0.5 * (1.0 + lax.erf(up * (1.0 / math.sqrt(2.0))))
            HID[rows(b), cs] = (up * cdf).astype(BF16)
            SLOPE[rows(b), cs] = (
                cdf + up * jnp.exp(-0.5 * up * up) * (1.0 / math.sqrt(2.0 * math.pi))
            ).astype(BF16)

        tiles(units // TILE, part)

    fetch_x.wait()
    fetch_g.wait()
    chain_wait("x", 1)
    chain_send("x", 2, X, own)
    row_send("xy1", 1)
    wu_on()
    chain_wait("x", 2)
    chain_send("x", 3, X, own)
    row_send("xy2", 2)
    chain_send("g", 1, G, own, cot)
    for j in range(4):
        copies.came(f"nv{j}")
    copies.came("xy0")
    norm_block(col_of[0])
    chain_wait("x", 3)
    row_send("xy3", 3)
    copies.start("gy", cot, G.at[rows(c), other], y_dev)
    wq_on, _, wq_done = weight(
        "wq", lambda rs: wq.at[rs, at((1 - r) * heads, heads)], WQ, wid, wid // 2, everything, False
    )

    def rows_of(ref, start, rs):
        return ref.at[at(start + rs.start, rs.size), :]

    wn_on, _, wn_done = weight(
        "wn", lambda rs: rows_of(wn, (1 - r) * units, rs), WN, 0, units // 2, other, False
    )
    wd_on, _, wd_done = weight(
        "wd", lambda rs: rows_of(wd, (1 - r) * HD, rs), WD, 0, HD // 2, other, False
    )
    wu_far()
    copies.came("xy1")
    norm_block(col_of[1])
    fetch_u.wait()
    wu_done()
    up_block(col_of[0])
    up_block(col_of[1])
    chain_wait("g", 1)
    chain_send("g", 2, G, own)
    copies.came("xy2")
    norm_block(col_of[2])
    up_block(col_of[2])
    chain_wait("g", 2)
    chain_send("g", 3, G, own)
    copies.came("xy3")
    norm_block(col_of[3])
    up_block(col_of[3])
    copies.came("gy")
    chain_send("h", 1, G, other)

    def grad_send(name, staged, left, right, n_rows, n_cols, target):
        def part(i):
            cs = at(i * TILE, TILE)
            staged[:, cs] = dot(left(None), right(cs), TN).astype(BF16)

        tiles(n_cols // TILE, part)
        copies.start(name, staged, target, core_dev)

    hid_keep, hid_send = at(k * uh, uh), at((1 - k) * uh, uh)
    att_keep, att_send = at(k * dh, dh), at((1 - k) * dh, dh)

    def out_grad(name, side, left_ref, keep, give, staged, landing):
        base = side * wid

        def give_part(i):
            cs = at(i * TILE, TILE)
            staged[:, cs] = dot(
                left_ref[:, give], G[:, at(base + i * TILE, TILE)], TN
            ).astype(BF16)

        tiles(wid // TILE, give_part)
        copies.start(f"{name}a", staged, landing, core_dev)

    def out_keep(name, side, left_ref, keep, landing):
        base = side * wid
        copies.came(f"{name}a")

        def keep_part(i):
            cs = at(i * TILE, TILE)
            mine = dot(left_ref[:, keep], G[:, at(base + i * TILE, TILE)], TN)
            landing[:, cs] = (mine + landing[:, cs].astype(F32)).astype(BF16)

        tiles(wid // TILE, keep_part)

    halves = {}

    def cross(name, total, n_rows, landing):
        half_rows = n_rows // 2
        give, keep = at((1 - hi) * half_rows, half_rows), at(hi * half_rows, half_rows)
        copies.start(f"{name}x", total.at[give, :], landing, x_dev)
        halves[name] = (total.at[keep, :], landing)

    def crossed(name, target):
        mine, landing = halves[name]
        copies.came(f"{name}x")
        n = landing.shape[0]
        step = min(n, 128)

        def part(i):
            rs = at(i * step, step)
            landing[rs, :] = (mine[rs, :].astype(F32) + landing[rs, :].astype(F32)).astype(BF16)

        tiles(n // step, part)
        copies.start(f"{name}y", landing, target, y_dev)

    def spread_out(name, came, result, here):
        copies.came(f"{name}y")
        copies.start(f"{name}g", came, result.at[here], x_dev)
        copies.start(f"{name}t", came, result.at[here], core_dev)
        fetch(came, result.at[here])

    def pass_quarter(name, result, there):
        copies.came(f"{name}g")
        copies.start(f"{name}f", result.at[there], result.at[there], core_dev)

    def finish(name, total, came, result, here):
        copies.came(f"{name}x")
        n = total.shape[0]
        step = min(n, 128)

        def part(i):
            rs = at(i * step, step)
            came[rs, :] = (total[rs, :].astype(F32) + came[rs, :].astype(F32)).astype(BF16)

        tiles(n // step, part)
        copies.start(f"{name}t", came, result.at[here], core_dev)
        fetch(came, result.at[here])

    wide = slice(None)

    def down_at(side, part=None):
        start, n = side * units + k * uh, uh
        if part is not None:
            start, n = start + part * (uh // 2), uh // 2
        return (at(start, n), wide)

    def dense_at(side, part=None):
        start, n = side * HD + k * dh, dh
        if part is not None:
            start, n = start + part * (dh // 2), dh // 2
        return (at(start, n), wide)

    def up_at(side, part=None):
        taken = wide if part is None else at(part * (wid // 2), wid // 2)
        return (taken, at(side * units + k * uh, uh))

    def qkv_at(side, part=None):
        taken = wide if part is None else at(part * (wid // 2), wid // 2)
        return (taken, at(side * heads + k * hh, hh))

    chain_wait("g", 3)
    out_grad("dn0", 0, HID, hid_keep, hid_send, DUP.at[pl.ds(0, uh), :], S_dn.at[0])
    out_keep("dn0", 0, HID, hid_keep, S_dn.at[0])
    copies.start("dn0x", S_dn.at[0], X_dn, x_dev)

    chain_wait("h", 1)
    chain_send("h", 2, G, other)
    fetch_q.wait()
    wq_on()
    wq_done()

    def qkv_block(i):
        block = at(i * blk, blk)
        for j in range(3):
            bias = qkv_b[:, at(r * heads + j * HD, HD)]
            value = dot(OUTP[block, :], WQ[:, j * HD : (j + 1) * HD], NN) + bias
            if j < 2:
                value = rotate(value, block, 1.0)
            QKV[block, j * HD : (j + 1) * HD] = value.astype(BF16)

    tiles(cols, qkv_block)
    chain_wait("h", 2)
    chain_send("h", 3, G, other)

    def key_range(i):
        low = max(0, i - 2) * blk
        return slice(i * blk, (i + 1) * blk), slice(low, (i + 1) * blk), low

    def block_scores(i):
        mine, span, low = key_range(i)
        n = span.stop - low
        s = dot(QKV[mine, 0:HD], QKV[span, HD : 2 * HD], NT) * scale
        row_id = lax.broadcasted_iota(jnp.int32, (blk, n), 0) + i * blk
        col_id = lax.broadcasted_iota(jnp.int32, (blk, n), 1) + low
        same = STAT[mine, 3:4] == seg_row[:, span]
        return jnp.where(same & (col_id <= row_id), s, -1e30)

    for i in range(cols):
        mine, span, low = key_range(i)
        s = block_scores(i)
        largest = jnp.max(s, axis=1, keepdims=True)
        p = jnp.exp(s - largest)
        total = jnp.sum(p, axis=1, keepdims=True)
        STAT[mine, 2:3] = largest + jnp.log(total)
        p_low = (p / total).astype(BF16)
        ATT[mine, :] = dot(p_low, QKV[span, 2 * HD :], NN).astype(BF16)
    out_grad("de0", 0, ATT, att_keep, att_send, A_de.at[0], S_de.at[0])
    out_keep("de0", 0, ATT, att_keep, S_de.at[0])
    copies.start("de0x", S_de.at[0], X_de, x_dev)
    fetch_n.wait()
    fetch_d.wait()

    def branch_block(b):
        def part(j):
            cs = at(j * TILE, TILE)
            both = dot(ATT[rows(b), :], WD[:, cs], NN) + dot(HID[rows(b), :], WN[:, cs], NN)
            OUTP[rows(b), cs] = both.astype(BF16)

        tiles(width // TILE, part)

    chain_wait("h", 3)
    out_grad("dn1", 1, HID, hid_keep, hid_send, DUP.at[pl.ds(uh, uh), :], S_dn.at[1])
    out_grad("de1", 1, ATT, att_keep, att_send, A_de.at[1], S_de.at[1])
    wn_on()
    out_keep("dn1", 1, HID, hid_keep, S_dn.at[1])
    cross("dn1", S_dn.at[1], uh, V_dn)
    out_keep("de1", 1, ATT, att_keep, S_de.at[1])
    cross("de1", S_de.at[1], dh, V_de)
    wn_done()

    copies.sent("dn0a", "dn1a")

    def up_grad_part(i):
        block = at(i * blk, blk)
        for j in range(units // TILE):
            cs = slice(j * TILE, (j + 1) * TILE)
            back = dot(G[block, :], WN[cs, :], NT)
            DUP[block, cs] = (back * SLOPE[block, cs].astype(F32)).astype(BF16)

    tiles(cols, up_grad_part)
    keep_u, give_u = at(k * uh, uh), at((1 - k) * uh, uh)
    keep_h, give_h = at(k * hh, hh), at((1 - k) * hh, hh)

    def in_give(name, right_ref, give, n, staged, landing):
        for side in (0, 1):

            def part(i):
                rs = at(i * TILE, TILE)
                lefts = N[:, at(side * wid + i * TILE, TILE)]
                staged[side][rs, :] = dot(lefts, right_ref[:, give], TN).astype(BF16)

            tiles(wid // TILE, part)
            copies.start(f"{name}{side}a", staged[side], landing.at[side], core_dev)

    def in_keep(name, side, right_ref, keep, landing):
        copies.came(f"{name}{side}a")

        def part(i):
            rs = at(i * TILE, TILE)
            mine = dot(N[:, at(side * wid + i * TILE, TILE)], right_ref[:, keep], TN)
            landing[side, rs, :] = (mine + landing[side, rs, :].astype(F32)).astype(BF16)

        tiles(wid // TILE, part)

    in_give(
        "up", DUP, give_u, uh, [SLOPE.at[:, pl.ds(0, uh)], SLOPE.at[:, pl.ds(uh, uh)]], S_up
    )
    wd_on()
    wd_done()
    for i in range(cols):
        mine = slice(i * blk, (i + 1) * blk)
        DAT[mine, :] = dot(G[mine, :], WD[...], NT).astype(BF16)
    SM[6:7, :] = jnp.sum(G[:, own].astype(F32), axis=0, keepdims=True)

    copies.sent(*[f"{t}{w}{s}" for t in "gh" for w in "ud" for s in (1, 2, 3)])
    pl.semaphore_signal(credit.at[0], inc=1, device_id=x_dev, device_id_type=MESH)
    pl.semaphore_signal(credit.at[1], inc=1, device_id=y_dev, device_id_type=MESH)
    X_up, low, high = G.at[:, pl.ds(0, uh)], pl.ds(0, wid // 2), pl.ds(wid // 2, wid // 2)
    V_up, R_up = G.at[low, pl.ds(uh, uh)], G.at[high, pl.ds(uh, uh)]
    X_qk = WN.at[:, pl.ds(0, hh)]
    V_qk, R_qk = WN.at[low, pl.ds(hh, hh)], WN.at[high, pl.ds(hh, hh)]

    in_keep("up", 1, DUP, keep_u, S_up)
    pl.semaphore_wait(credit.at[0], 1)
    cross("up1", S_up.at[1], wid, V_up)
    in_keep("up", 0, DUP, keep_u, S_up)
    copies.start("up0x", S_up.at[0], X_up, x_dev)

    crossed("dn1", R_dn)
    for s in (2, 3):
        branch_block(col_of[s])
        copies.start(f"oy{s}", OUTP.at[rows(col_of[s]), other], OY.at[s - 1], y_dev)
    crossed("de1", R_de)
    branch_block(col_of[1])
    copies.start("oz1", OUTP.at[rows(col_of[1]), :], OZ1, {"col": col_of[1]})
    branch_block(col_of[0])
    copies.sent("wnc")
    pl.semaphore_signal(credit.at[2], inc=1, device_id=x_dev, device_id_type=MESH)
    pl.semaphore_signal(credit.at[3], inc=1, device_id=y_dev, device_id_type=MESH)
    pl.semaphore_signal(credit.at[4], inc=1, device_id=y_dev, device_id_type=MESH)

    def again(i):
        rs = at(i * sub, sub)
        normal = (X[rs, :].astype(F32) - STAT[rs, 0:1]) * STAT[rs, 1:2]
        N[rs, :] = (normal * NV[0:1, :] + NV[1:2, :]).astype(BF16)

    tiles(rows_all // sub, again)
    TMP[...] = jnp.zeros_like(TMP)
    for i in range(cols):
        mine, span, low = key_range(i)
        query = QKV[mine, 0:HD]
        p = jnp.exp(block_scores(i) - STAT[mine, 2:3])
        d_p = dot(DAT[mine, :], QKV[span, 2 * HD :], NT)
        delta = jnp.sum(d_p * p, axis=1, keepdims=True)
        d_s = (p * (d_p - delta)).astype(BF16)
        p_low = p.astype(BF16)
        d_query = dot(d_s, QKV[span, HD : 2 * HD], NN) * scale
        QKV[mine, 0:HD] = rotate(d_query, mine, -1.0).astype(BF16)
        for j in range(low // blk, i + 1):
            js = slice(j * blk - low, (j + 1) * blk - low)
            ks, vs = slice(j * HD, (j + 1) * HD), slice((cols + j) * HD, (cols + j + 1) * HD)
            TMP[:, ks] += dot(d_s[:, js], query, TN)
            TMP[:, vs] += dot(p_low[:, js], DAT[mine, :], TN)
    for j in range(cols):
        mine = slice(j * blk, (j + 1) * blk)
        ks, vs = slice(j * HD, (j + 1) * HD), slice((cols + j) * HD, (cols + j + 1) * HD)
        QKV[mine, HD : 2 * HD] = rotate(TMP[:, ks] * scale, mine, -1.0).astype(BF16)
        QKV[mine, 2 * HD :] = TMP[:, vs].astype(BF16)

    copies.sent("up0a", "up1a")
    in_give(
        "qk", QKV, give_h, hh, [SLOPE.at[:, pl.ds(0, hh)], SLOPE.at[:, pl.ds(hh, hh)]], S_qk
    )
    pl.semaphore_wait(credit.at[1], 1)
    crossed("up1", R_up)
    spread_out("dn1", R_dn, g_down, down_at(1 - r, hi))
    in_keep("qk", 1, QKV, keep_h, S_qk)
    pl.semaphore_wait(credit.at[2], 1)
    cross("qk1", S_qk.at[1], wid, V_qk)
    in_keep("qk", 0, QKV, keep_h, S_qk)
    copies.start("qk0x", S_qk.at[0], X_qk, x_dev)
    finish("dn0", S_dn.at[0], X_dn, g_down, down_at(r))
    finish("de0", S_de.at[0], X_de, g_dense, dense_at(r))

    def out_block(s):
        b = col_of[s]
        copies.came(f"oy{s}")

        def part(i):
            rs = at(b * blk + i * sub, sub)
            came = OY[s - 1, at(i * sub, sub), :]
            OUTP[rs, own] = (OUTP[rs, own].astype(F32) + came.astype(F32)).astype(BF16)

        tiles(blk // sub, part)
        copies.start(f"oz{s}", OUTP.at[rows(b), own], OZ.at[s - 2], {"col": b})

    out_block(2)

    NSUM[...] = jnp.zeros_like(NSUM)
    pl.semaphore_wait(credit.at[4], 1)

    def norm_back(b):
        rb = rows(b)
        mean, inv = STAT[rb, 0:1], STAT[rb, 1:2]

        def first(j, carry):
            along, plain = carry
            cs = at(j * TILE, TILE)
            one = dot(QKV[rb, :], WQ[cs, :], NT)
            two = dot(DUP[rb, :], WU[cs, :], NT)
            normal = (X[rb, cs].astype(F32) - mean) * inv
            NSUM[0:1, cs] += jnp.sum(one * normal, axis=0, keepdims=True)
            NSUM[1:2, cs] += jnp.sum(one, axis=0, keepdims=True)
            NSUM[2:3, cs] += jnp.sum(two * normal, axis=0, keepdims=True)
            NSUM[3:4, cs] += jnp.sum(two, axis=0, keepdims=True)
            grad = one * NV[0:1, cs] + two * NV[2:3, cs]
            TMP[:, cs] = grad
            along = along + jnp.sum(grad * normal, axis=1, keepdims=True)
            plain = plain + jnp.sum(grad, axis=1, keepdims=True)
            return along, plain

        zero = jnp.zeros((blk, 1), F32)
        along, plain = lax.fori_loop(0, width // TILE, first, (zero, zero))
        along, plain = along * (1.0 / width), plain * (1.0 / width)

        def second(j):
            cs = at(j * TILE, TILE)
            normal = (X[rb, cs].astype(F32) - mean) * inv
            N[rb, cs] = (inv * (TMP[:, cs] - plain - normal * along)).astype(BF16)

        tiles(width // TILE, second)

    EY = [HID.at[pl.ds(j * blk, blk), :] for j in range(3)]
    pl.semaphore_wait(credit.at[3], 1)
    for s in (2, 3):
        norm_back(col_of[s])
        copies.start(f"ey{s}", N.at[rows(col_of[s]), other], EY[s - 1], y_dev)
        if s == 2:
            spread_out("de1", R_de, g_dense, dense_at(1 - r, hi))
            out_block(3)
        else:
            crossed("qk1", R_qk)
    norm_back(col_of[1])
    copies.start("ez1", N.at[rows(col_of[1]), :], DZ1, {"col": col_of[1]})
    spread_out("up1", R_up, g_up, up_at(1 - r, hi))
    norm_back(col_of[0])

    SM[0:4, :] = NSUM[0:4, own]
    SM[4:5, :] = jnp.sum(DUP[...].astype(F32), axis=0, keepdims=True)
    SM[5:6, 0:heads] = jnp.sum(QKV[...].astype(F32), axis=0, keepdims=True)
    SM[5:6, heads:] = jnp.zeros((1, wid - heads), F32)
    SM[7:8, :] = jnp.zeros((1, wid), F32)
    SMO[0:4, :] = NSUM[0:4, other]
    SMO[4:8, :] = jnp.zeros((4, wid), F32)
    copies.start("s0", SMO, SMR.at[0], y_dev)

    def small_next(j, device, top):
        def action():
            copies.came(f"s{j - 1}")
            copies.sent(f"s{j - 1}")
            SM[0:top, :] = SM[0:top, :] + SMR[j - 1, 0:top, :]
            if device is not None:
                copies.start(f"s{j}", SM, SMR.at[j], device)

        return action

    def mine_at(i):
        return at(c * blk + i * sub, sub)

    def row_rest(buf, came, landing, name):
        copies.came(f"{name}z1")

        def part(i):
            rs = at(i * sub, sub)
            total = buf[mine_at(i), other].astype(F32) + came[rs, other].astype(F32)
            buf[mine_at(i), other] = total.astype(BF16)

        tiles(blk // sub, part)
        copies.start(f"{name}y0", buf.at[rows(c), other], landing, y_dev)

    def total_of(i, buf, near, far_ones, from_row):
        rs = at(i * sub, sub)
        total = buf[mine_at(i), own].astype(F32) + near[rs, own].astype(F32)
        for ref in far_ones:
            total = total + ref[rs, :].astype(F32)
        return total + from_row[rs, :].astype(F32)

    def x_block(s):
        b = col_of[s]
        copies.came(f"ey{s}")

        def part(i):
            rs = at(b * blk + i * sub, sub)
            came = EY[s - 1][at(i * sub, sub), :]
            N[rs, own] = (N[rs, own].astype(F32) + came.astype(F32)).astype(BF16)

        tiles(blk // sub, part)
        copies.start(f"ez{s}", N.at[rows(b), own], DZ.at[s - 2], {"col": b})

    row_rest(OUTP, OZ1, OY.at[0], "o")
    small_next(1, {"col": col_of[1]}, 4)()
    finish("up0", S_up.at[0], X_up, g_up, up_at(r))
    pass_quarter("dn1", g_down, down_at(1 - r, 1 - hi))
    pass_quarter("de1", g_dense, dense_at(1 - r, 1 - hi))
    small_next(2, {"col": col_of[2]}, 4)()
    x_block(2)
    row_rest(N, DZ1, EY[0], "e")
    x_block(3)
    small_next(3, core_dev, 4)()
    spread_out("qk1", R_qk, g_qkv, qkv_at(1 - r, hi))
    small_next(4, x_dev, 8)()
    finish("qk0", S_qk.at[0], X_qk, g_qkv, qkv_at(r))
    small_next(5, None, 8)()
    copies.start("s5", SM, SMR.at[5], y_dev)
    pass_quarter("up1", g_up, up_at(1 - r, 1 - hi))
    for name in ("oz2", "oz3", "oy0"):
        copies.came(name)

    def out_last(i):
        total = total_of(i, OUTP, OZ1, [OZ.at[0], OZ.at[1]], OY.at[0])
        total = total + X[mine_at(i), own].astype(F32)
        out[at(i * sub, sub), :] = (total + (dense_b[...] + down_b[...])).astype(BF16)

    tiles(blk // sub, out_last)
    copies.came("s5")
    small[0:8, :] = SM[...]
    small[8:16, :] = SMR[5]
    for name in ("ez2", "ez3", "ey0"):
        copies.came(name)

    def x_last(i):
        total = total_of(i, N, DZ1, [DZ.at[0], DZ.at[1]], EY[0])
        in_grad[at(i * sub, sub), :] = cot[at(i * sub, sub), :].astype(F32) + total

    tiles(blk // sub, x_last)
    pass_quarter("qk1", g_qkv, qkv_at(1 - r, 1 - hi))
    for name in ("dn0", "de0", "up0", "qk0"):
        copies.came(f"{name}t")
    for name in ("dn1", "de1", "up1", "qk1"):
        copies.came(f"{name}t")
        copies.came(f"{name}f")
    for copy in local[6:]:
        copy.wait()
    copies.sent_all()


def scratch(blk, wid, cols, units, heads):
    tokens, width = blk * cols, 2 * wid
    low = [
        (tokens, width), (tokens, width), (width, heads), (width, units), (HD, width),
        (units, width), (tokens, width),
    ]
    V = pltpu.VMEM
    return (
        [V(shape, BF16) for shape in low]
        + [V((tokens, 128), F32)]
        + [
            V(shape, BF16)
            for shape in (
                (tokens, heads), (tokens, HD), (tokens, units), (tokens, units), (tokens, units),
                (tokens, HD), (tokens, width), (blk, width), (2, blk, wid), (3, blk, wid),
                (blk, width), (2, blk, wid),
                (2, units // 2, wid), (2, HD // 2, wid), (2, wid, units // 2), (2, wid, heads // 2),
                (units // 4, wid), (HD // 4, wid), (units // 4, wid), (HD // 4, wid),
                (units // 2, wid), (HD // 2, wid), (2, HD // 2, wid),
            )
        ]
        + [
            V((blk, width), F32),
            V((8, width), F32),
            V((tokens, 128), F32),
            V((tokens, 128), F32),
            V((8, width), F32),
            V((8, wid), F32),
            V((8, wid), F32),
            V((6, 8, wid), F32),
            pltpu.SemaphoreType.DMA((120,)),
            pltpu.SemaphoreType.DMA((120,)),
            pltpu.SemaphoreType.DMA((20,)),
            pltpu.SemaphoreType.REGULAR((5,)),
        ]
    )


def swap(value, axis, mask):
    size = lax.axis_size(axis)
    return lax.ppermute(value, axis, [(i, i ^ mask) for i in range(size)])


def shards(
    hidden_in,
    segment,
    norm1_gain,
    norm1_bias,
    norm2_gain,
    norm2_bias,
    qkv_weight,
    qkv_bias,
    dense_weight,
    dense_bias,
    up_weight,
    up_bias,
    down_weight,
    down_bias,
    cotangent,
):
    blk, wid = hidden_in.shape
    cols = lax.axis_size("col")
    heads, units = qkv_weight.shape[1] // 2, up_weight.shape[1] // 2
    vectors = [
        v.reshape(1, -1)
        for v in (
            norm1_gain, norm1_bias, norm2_gain, norm2_bias, qkv_bias, up_bias, dense_bias, down_bias,
        )
    ]
    vmem = pl.BlockSpec(memory_space=pltpu.VMEM)
    far = pl.BlockSpec(memory_space=pl.ANY)
    shape = jax.ShapeDtypeStruct
    out, in_grad, small, g_qkv, g_dense, g_up, g_down = pl.pallas_call(
        functools.partial(step_kernel, (blk, wid, cols)),
        out_shape=(
            shape((blk, wid), BF16),
            shape((blk, wid), F32),
            shape((16, wid), F32),
            shape(qkv_weight.shape, BF16),
            shape(dense_weight.shape, BF16),
            shape(up_weight.shape, BF16),
            shape(down_weight.shape, BF16),
        ),
        in_specs=[vmem, vmem] + [far] * 4 + [vmem] * 9,
        out_specs=(vmem,) * 3 + (far,) * 4,
        scratch_shapes=scratch(blk, wid, cols, units, heads),
        compiler_params=pltpu.CompilerParams(
            collective_id=0, has_side_effects=True, vmem_limit_bytes=67043328
        ),
        name="step",
    )(
        hidden_in, cotangent, qkv_weight, up_weight, dense_weight, down_weight, segment, *vectors
    )

    grads = [g.astype(F32) for g in (g_qkv, g_dense, g_up, g_down)]
    mask = 4
    while mask < lax.axis_size("dp"):
        grads = [g + swap(g.astype(BF16), "dp", mask).astype(F32) for g in grads]
        small = small + swap(small, "dp", mask)
        mask *= 2
    row = lax.axis_index("row")

    def both(index):
        first, second = small[index], small[8 + index]
        return jnp.where(row == 0, first, second), jnp.where(row == 0, second, first)

    qkv_bias_grad = jnp.concatenate([part[:heads] for part in both(5)])
    up_bias_grad = jnp.concatenate(both(4))
    return (
        out,
        in_grad,
        small[0],
        small[1],
        small[2],
        small[3],
        grads[0],
        qkv_bias_grad,
        grads[1],
        small[6],
        grads[2],
        up_bias_grad,
        grads[3],
        small[6],
    )


def solution(mesh):
    return jax.shard_map(
        shards,
        mesh=mesh,
        in_specs=(
            P(("dp", "col"), "row"),
            P("dp", None),
            P("row"),
            P("row"),
            P("row"),
            P("row"),
            P("row", "col"),
            P("col"),
            P("col", "row"),
            P("row"),
            P("row", "col"),
            P("col"),
            P("col", "row"),
            P("row"),
            P(("dp", "col"), "row"),
        ),
        out_specs=(
            P(("dp", "col"), "row"),
            P(("dp", "col"), "row"),
            P("row"),
            P("row"),
            P("row"),
            P("row"),
            P("row", "col"),
            P("col"),
            P("col", "row"),
            P("row"),
            P("row", "col"),
            P("col"),
            P("col", "row"),
            P("row"),
        ),
        check_vma=False,
    )
```

```python
import functools
import math

import jax
import jax.numpy as jnp
from jax import lax
from jax.experimental import pallas as pl
from jax.experimental.pallas import tpu as pltpu
from jax.sharding import PartitionSpec as P

HD = 256
ROT = 64
F32 = jnp.float32
BF16 = jnp.bfloat16
MESH = pl.DeviceIdType.MESH

eps_norm = 1e-05
rope_base = 10000.0
TILE = 512
NN = (((1,), (0,)), ((), ()))
NT = (((1,), (1,)), ((), ()))
TN = (((0,), (0,)), ((), ()))


def dot(left, right, dims):
    return lax.dot_general(left, right, dims, preferred_element_type=F32)


class Copies:
    def __init__(self, send_sem, recv_sem):
        self.send_sem, self.recv_sem = send_sem, recv_sem
        self.made, self.open = {}, {}

    def start(self, name, source, target, device, when=None):
        index = len(self.made)
        copy = pltpu.make_async_remote_copy(
            src_ref=source,
            dst_ref=target,
            send_sem=self.send_sem.at[index],
            recv_sem=self.recv_sem.at[index],
            device_id=device,
            device_id_type=MESH,
        )
        self.made[name] = copy
        self.open[name] = when
        guarded(when, copy.start)

    def came(self, name, when=None):
        guarded(when, self.made[name].wait_recv)

    def sent(self, *names):
        for name in names:
            guarded(self.open.pop(name), self.made[name].wait_send)

    def sent_all(self):
        self.sent(*list(self.open))


def guarded(when, action):
    if when is None:
        action()
    else:
        pl.when(when)(action)


def at(start, size):
    return pl.ds(pl.multiple_of(start, size), size)


def tiles(count, body):
    lax.fori_loop(0, count, lambda i, carry: (body(i), carry)[1], 0)


def step_kernel(
    sizes,
    hid, cot, wq, wu, wd, wn, seg, gain1, bias1, gain2, bias2, qkv_b, up_b, dense_b, down_b,
    out, in_grad, small, g_qkv, g_dense, g_up, g_down,
    X, G, WQ, WU, WD, WN, N, STAT, QKV, ATT, HID, SLOPE, DUP, DAT, OUTP, OZ1, OZ, OY, DZ1, DZ,
    S_dn, S_de, S_up, S_qk, R_dn, R_de, V_dn, V_de, X_dn, X_de, A_de, TMP, NV, COS, SIN, NSUM, SMO, SMR, NZ, NQ, BQ, BS, BR,
    send_sem, recv_sem, local_sem, credit,
):
    blk, wid, cols = sizes
    rows_all = blk * cols
    width = 2 * wid
    heads, units = WQ.shape[1], WU.shape[1]
    hh, uh, dh = heads // 2, units // 2, HD // 2
    r = lax.axis_index("row")
    c = lax.axis_index("col")
    dp = lax.axis_index("dp")
    k = lax.rem(dp, 2)
    hi = lax.rem(lax.div(dp, 2), 2)
    q = k + 2 * hi
    core_dev = {"dp": dp + 1 - 2 * k}
    x_dev = {"dp": dp + 2 - 4 * hi}
    far_dev = {"dp": dp + 3 - 2 * k - 4 * hi}
    y_dev = {"row": 1 - r}
    c_low, c_high = lax.rem(c, 2), lax.div(c, 2)
    col_of = [c, c + 1 - 2 * c_low, c + 2 - 4 * c_high, 3 - c]
    own, other = pl.ds(0, wid), pl.ds(wid, wid)
    scale = 1.0 / math.sqrt(HD)
    copies = Copies(send_sem, recv_sem)

    barrier = pltpu.get_barrier_semaphore()
    friends = [core_dev, x_dev, far_dev, y_dev] + [{"col": col_of[s]} for s in (1, 2, 3)]
    for device in friends:
        pl.semaphore_signal(barrier, inc=1, device_id=device, device_id_type=MESH)

    local = []

    def fetch(source, target):
        copy = pltpu.make_async_copy(source, target, local_sem.at[len(local)])
        copy.start()
        local.append(copy)
        return copy

    fetch_x = fetch(hid, X.at[at(c * blk, blk), own])
    fetch_g = fetch(cot, G.at[at(c * blk, blk), own])
    fetch_u = fetch(wu.at[:, at(r * units, units)], WU.at[own, :])
    fetch_q = fetch(wq.at[:, at(r * heads, heads)], WQ.at[own, :])
    fetch_n = fetch(wn.at[at(r * units, units), :], WN.at[:, own])
    fetch_d = fetch(wd.at[at(r * HD, HD), :], WD.at[:, own])
    pl.semaphore_wait(barrier, len(friends))

    def rows(b):
        return at(b * blk, blk)

    def chain_send(tag, step, buf, columns, first=None):
        for word, move, edge in (("u", 1, c < cols - 1), ("d", -1, c >= 1)):
            block = c - move * (step - 1)
            valid = edge & (block >= 0) & (block <= cols - 1)
            source = first if first is not None else buf.at[rows(block), columns]
            copies.start(
                f"{tag}{word}{step}", source, buf.at[rows(block), columns], {"col": c + move}, valid
            )

    def chain_wait(tag, step):
        copies.came(f"{tag}u{step}", c >= step)
        copies.came(f"{tag}d{step}", c + step <= cols - 1)

    def row_send(name, s):
        b = col_of[s]
        copies.start(name, X.at[rows(b), own], X.at[rows(b), other], y_dev)

    q2 = q + 2 - 4 * hi

    def weight(name, source, full, row0, size, columns, spread):
        share = q if spread else k

        def place(index):
            return full.at[at(row0 + index * size, size), columns]

        copies.start(f"{name}y", source(at(share * size, size)), place(share), y_dev)

        def pass_on():
            copies.came(f"{name}y")
            if spread:
                copies.start(f"{name}x", place(q), place(q), x_dev)
            copies.start(f"{name}c", place(share), place(share), core_dev)

        def pass_far():
            copies.came(f"{name}x")
            copies.start(f"{name}f", place(q2), place(q2), core_dev)

        def done():
            copies.came(f"{name}c")
            if spread:
                copies.came(f"{name}f")

        return pass_on, pass_far, done

    everything = slice(None)
    chain_send("x", 1, X, own, hid)
    copies.start("xy0", hid, X.at[rows(c), other], y_dev)
    for j, vector in enumerate((gain1, bias1, gain2, bias2)):
        copies.start(f"nv{j}", vector, NV.at[pl.ds(j, 1), other], y_dev)
    wu_on, wu_far, wu_done = weight(
        "wu", lambda rs: wu.at[rs, at((1 - r) * units, units)], WU, wid, wid // 4, everything, True
    )

    seg_row = seg[...].astype(F32)
    seg_col = jnp.transpose(jnp.broadcast_to(seg_row, (128, rows_all)))
    STAT[:, 3:4] = seg_col[:, 0:1]
    for j, vector in enumerate((gain1, bias1, gain2, bias2)):
        NV[j : j + 1, own] = vector[...]

    def table(i):
        block = at(i * blk, blk)
        starts = jnp.sum(
            (seg_row < STAT[block, 3:4]).astype(F32), axis=1, keepdims=True
        )
        index = lax.broadcasted_iota(jnp.int32, (blk, 1), 0) + i * blk
        lane = lax.broadcasted_iota(jnp.int32, (1, 128), 1)
        turn = jnp.exp(
            lax.rem(lane, ROT // 2).astype(F32) * (-2.0 * math.log(rope_base) / ROT)
        )
        angles = (index.astype(F32) - starts) * turn
        COS[block, :] = jnp.where(lane < ROT, jnp.cos(angles), 1.0)
        SIN[block, :] = jnp.where(
            lane < ROT // 2, -jnp.sin(angles), jnp.where(lane < ROT, jnp.sin(angles), 0.0)
        )

    tiles(cols, table)

    def rotate(head, block, sign):
        first = head[:, :128]
        lane = lax.broadcasted_iota(jnp.int32, first.shape, 1)
        swapped = jnp.where(
            lane < ROT // 2, pltpu.roll(first, 128 - ROT // 2, 1), pltpu.roll(first, ROT // 2, 1)
        )
        turned = first * COS[block, :] + sign * (swapped * SIN[block, :])
        return jnp.concatenate([turned, head[:, 128:]], axis=1)

    sub = 64

    def norm_block(b):
        def part(i):
            rs = at(b * blk + i * sub, sub)
            x = X[rs, :].astype(F32)
            mean = jnp.sum(x, axis=1, keepdims=True) * (1.0 / width)
            square = jnp.sum(x * x, axis=1, keepdims=True) * (1.0 / width)
            inv = lax.rsqrt(square - mean * mean + eps_norm)
            STAT[rs, 0:1] = mean
            STAT[rs, 1:2] = inv
            normal = (x - mean) * inv
            OUTP[rs, :] = (normal * NV[0:1, :] + NV[1:2, :]).astype(BF16)
            N[rs, :] = (normal * NV[2:3, :] + NV[3:4, :]).astype(BF16)

        tiles(blk // sub, part)

    def up_block(b):
        def part(j):
            cs = at(j * TILE, TILE)
            bias = up_b[:, at(r * units + j * TILE, TILE)]
            up = dot(N[rows(b), :], WU[:, cs], NN) + bias
            cdf = 0.5 * (1.0 + lax.erf(up * (1.0 / math.sqrt(2.0))))
            HID[rows(b), cs] = (up * cdf).astype(BF16)
            SLOPE[rows(b), cs] = (
                cdf + up * jnp.exp(-0.5 * up * up) * (1.0 / math.sqrt(2.0 * math.pi))
            ).astype(BF16)

        tiles(units // TILE, part)

    fetch_x.wait()
    fetch_g.wait()
    chain_wait("x", 1)
    chain_send("x", 2, X, own)
    row_send("xy1", 1)
    wu_on()
    chain_wait("x", 2)
    chain_send("x", 3, X, own)
    row_send("xy2", 2)
    chain_send("g", 1, G, own, cot)
    for j in range(4):
        copies.came(f"nv{j}")
    copies.came("xy0")
    norm_block(col_of[0])
    chain_wait("x", 3)
    row_send("xy3", 3)
    copies.start("gy", cot, G.at[rows(c), other], y_dev)
    wq_on, _, wq_done = weight(
        "wq", lambda rs: wq.at[rs, at((1 - r) * heads, heads)], WQ, wid, wid // 2, everything, False
    )

    def rows_of(ref, start, rs):
        return ref.at[at(start + rs.start, rs.size), :]

    wn_on, wn_far, wn_done = weight(
        "wn", lambda rs: rows_of(wn, (1 - r) * units, rs), WN, 0, units // 4, other, True
    )
    wd_on, _, wd_done = weight(
        "wd", lambda rs: rows_of(wd, (1 - r) * HD, rs), WD, 0, HD // 2, other, False
    )
    wu_far()
    copies.came("xy1")
    norm_block(col_of[1])
    fetch_u.wait()
    wu_done()
    up_block(col_of[0])
    up_block(col_of[1])
    chain_wait("g", 1)
    chain_send("g", 2, G, own)
    copies.came("xy2")
    norm_block(col_of[2])
    up_block(col_of[2])
    chain_wait("g", 2)
    chain_send("g", 3, G, own)
    copies.came("xy3")
    norm_block(col_of[3])
    up_block(col_of[3])
    copies.came("gy")
    chain_send("h", 1, G, other)

    def grad_send(name, staged, left, right, n_rows, n_cols, target):
        def part(i):
            cs = at(i * TILE, TILE)
            staged[:, cs] = dot(left(None), right(cs), TN).astype(BF16)

        tiles(n_cols // TILE, part)
        copies.start(name, staged, target, core_dev)

    hid_keep, hid_send = at(k * uh, uh), at((1 - k) * uh, uh)
    att_keep, att_send = at(k * dh, dh), at((1 - k) * dh, dh)

    def out_grad(name, side, left_ref, keep, give, staged, landing):
        base = side * wid

        def give_part(i):
            cs = at(i * TILE, TILE)
            staged[:, cs] = dot(
                left_ref[:, give], G[:, at(base + i * TILE, TILE)], TN
            ).astype(BF16)

        tiles(wid // TILE, give_part)
        copies.start(f"{name}a", staged, landing, core_dev)

    def out_keep(name, side, left_ref, keep, landing):
        base = side * wid
        copies.came(f"{name}a")

        def keep_part(i):
            cs = at(i * TILE, TILE)
            mine = dot(left_ref[:, keep], G[:, at(base + i * TILE, TILE)], TN)
            landing[:, cs] = (mine + landing[:, cs].astype(F32)).astype(BF16)

        tiles(wid // TILE, keep_part)

    halves = {}

    def cross(name, total, n_rows, landing):
        half_rows = n_rows // 2
        give, keep = at((1 - hi) * half_rows, half_rows), at(hi * half_rows, half_rows)
        copies.start(f"{name}x", total.at[give, :], landing, x_dev)
        halves[name] = (total.at[keep, :], landing)

    def crossed(name, target):
        mine, landing = halves[name]
        copies.came(f"{name}x")
        n = landing.shape[0]
        step = min(n, 128)

        def part(i):
            rs = at(i * step, step)
            landing[rs, :] = (mine[rs, :].astype(F32) + landing[rs, :].astype(F32)).astype(BF16)

        tiles(n // step, part)
        copies.start(f"{name}y", landing, target, y_dev)

    def spread_out(name, came, result, here):
        copies.came(f"{name}y")
        copies.start(f"{name}g", came, result.at[here], x_dev)
        copies.start(f"{name}t", came, result.at[here], core_dev)
        fetch(came, result.at[here])

    def pass_quarter(name, result, there):
        copies.came(f"{name}g")
        copies.start(f"{name}f", result.at[there], result.at[there], core_dev)

    def finish(name, total, came, result, here):
        copies.came(f"{name}x")
        n = total.shape[0]
        step = min(n, 128)

        def part(i):
            rs = at(i * step, step)
            came[rs, :] = (total[rs, :].astype(F32) + came[rs, :].astype(F32)).astype(BF16)

        tiles(n // step, part)
        copies.start(f"{name}t", came, result.at[here], core_dev)
        fetch(came, result.at[here])

    wide = slice(None)

    def down_at(side, part=None):
        start, n = side * units + k * uh, uh
        if part is not None:
            start, n = start + part * (uh // 2), uh // 2
        return (at(start, n), wide)

    def dense_at(side, part=None):
        start, n = side * HD + k * dh, dh
        if part is not None:
            start, n = start + part * (dh // 2), dh // 2
        return (at(start, n), wide)

    def up_at(side, part=None):
        taken = wide if part is None else at(part * (wid // 2), wid // 2)
        return (taken, at(side * units + k * uh, uh))

    def qkv_at(side, part=None):
        taken = wide if part is None else at(part * (wid // 2), wid // 2)
        return (taken, at(side * heads + k * hh, hh))

    chain_wait("g", 3)
    out_grad("dn0", 0, HID, hid_keep, hid_send, DUP.at[pl.ds(0, uh), :], S_dn.at[0])
    out_keep("dn0", 0, HID, hid_keep, S_dn.at[0])
    copies.start("dn0x", S_dn.at[0], X_dn, x_dev)

    chain_wait("h", 1)
    chain_send("h", 2, G, other)
    fetch_q.wait()
    wq_on()
    wq_done()

    def qkv_block(i):
        block = at(i * blk, blk)
        for j in range(3):
            bias = qkv_b[:, at(r * heads + j * HD, HD)]
            value = dot(OUTP[block, :], WQ[:, j * HD : (j + 1) * HD], NN) + bias
            if j < 2:
                value = rotate(value, block, 1.0)
            QKV[block, j * HD : (j + 1) * HD] = value.astype(BF16)

    tiles(cols, qkv_block)
    chain_wait("h", 2)
    chain_send("h", 3, G, other)

    def key_range(i):
        low = max(0, i - 2) * blk
        return slice(i * blk, (i + 1) * blk), slice(low, (i + 1) * blk), low

    def block_scores(i):
        mine, span, low = key_range(i)
        n = span.stop - low
        s = dot(QKV[mine, 0:HD], QKV[span, HD : 2 * HD], NT) * scale
        row_id = lax.broadcasted_iota(jnp.int32, (blk, n), 0) + i * blk
        col_id = lax.broadcasted_iota(jnp.int32, (blk, n), 1) + low
        same = STAT[mine, 3:4] == seg_row[:, span]
        return jnp.where(same & (col_id <= row_id), s, -1e30)

    for i in range(cols):
        mine, span, low = key_range(i)
        s = block_scores(i)
        largest = jnp.max(s, axis=1, keepdims=True)
        p = jnp.exp(s - largest)
        total = jnp.sum(p, axis=1, keepdims=True)
        STAT[mine, 2:3] = largest + jnp.log(total)
        p_low = (p / total).astype(BF16)
        ATT[mine, :] = dot(p_low, QKV[span, 2 * HD :], NN).astype(BF16)
    out_grad("de0", 0, ATT, att_keep, att_send, A_de.at[0], S_de.at[0])
    fetch_n.wait()
    fetch_d.wait()

    def branch_block(b, side):
        def part(j):
            cs = at(side * wid + j * TILE, TILE)
            both = dot(ATT[rows(b), :], WD[:, cs], NN) + dot(HID[rows(b), :], WN[:, cs], NN)
            OUTP[rows(b), cs] = both.astype(BF16)

        tiles(wid // TILE, part)

    tiles(cols, lambda b: branch_block(b, 0))
    wn_on()
    out_keep("de0", 0, ATT, att_keep, S_de.at[0])

    chain_wait("h", 3)
    out_grad("dn1", 1, HID, hid_keep, hid_send, DUP.at[pl.ds(uh, uh), :], S_dn.at[1])
    out_grad("de1", 1, ATT, att_keep, att_send, A_de.at[1], S_de.at[1])
    wd_on()
    out_keep("dn1", 1, HID, hid_keep, S_dn.at[1])
    cross("dn1", S_dn.at[1], uh, V_dn)
    out_keep("de1", 1, ATT, att_keep, S_de.at[1])
    cross("de1", S_de.at[1], dh, V_de)
    copies.start("de0x", S_de.at[0], X_de, x_dev)
    wd_done()
    wn_far()
    wn_done()
    for s in (2, 3):
        branch_block(col_of[s], 1)
        copies.start(f"oy{s}", OUTP.at[rows(col_of[s]), other], OY.at[s - 1], y_dev)
    branch_block(col_of[1], 1)
    copies.start("oz1", OUTP.at[rows(col_of[1]), :], OZ1, {"col": col_of[1]})
    branch_block(col_of[0], 1)

    copies.sent("dn0a", "dn1a")

    def up_grad_part(i):
        block = at(i * blk, blk)
        for j in range(units // TILE):
            cs = slice(j * TILE, (j + 1) * TILE)
            back = dot(G[block, :], WN[cs, :], NT)
            DUP[block, cs] = (back * SLOPE[block, cs].astype(F32)).astype(BF16)

    tiles(cols, up_grad_part)
    keep_u, give_u = at(k * uh, uh), at((1 - k) * uh, uh)
    keep_h, give_h = at(k * hh, hh), at((1 - k) * hh, hh)

    def in_give(name, right_ref, give, n, staged, landing):
        for side in (0, 1):

            def part(i):
                rs = at(i * TILE, TILE)
                lefts = N[:, at(side * wid + i * TILE, TILE)]
                staged[side][rs, :] = dot(lefts, right_ref[:, give], TN).astype(BF16)

            tiles(wid // TILE, part)
            copies.start(f"{name}{side}a", staged[side], landing.at[side], core_dev)

    def in_keep(name, side, right_ref, keep, landing):
        copies.came(f"{name}{side}a")

        def part(i):
            rs = at(i * TILE, TILE)
            mine = dot(N[:, at(side * wid + i * TILE, TILE)], right_ref[:, keep], TN)
            landing[side, rs, :] = (mine + landing[side, rs, :].astype(F32)).astype(BF16)

        tiles(wid // TILE, part)

    in_give(
        "up", DUP, give_u, uh, [SLOPE.at[:, pl.ds(0, uh)], SLOPE.at[:, pl.ds(uh, uh)]], S_up
    )
    for i in range(cols):
        mine = slice(i * blk, (i + 1) * blk)
        DAT[mine, :] = dot(G[mine, :], WD[...], NT).astype(BF16)
    BQ[q, 2:3, :] = jnp.sum(G[:, own].astype(F32), axis=0, keepdims=True)

    copies.sent(*[f"{t}{w}{s}" for t in "gh" for w in "ud" for s in (1, 2, 3)])
    pl.semaphore_signal(credit.at[0], inc=1, device_id=x_dev, device_id_type=MESH)
    pl.semaphore_signal(credit.at[1], inc=1, device_id=y_dev, device_id_type=MESH)
    X_up, low, high = G.at[:, pl.ds(0, uh)], pl.ds(0, wid // 2), pl.ds(wid // 2, wid // 2)
    V_up, R_up = G.at[low, pl.ds(uh, uh)], G.at[high, pl.ds(uh, uh)]
    X_qk = WN.at[:, pl.ds(0, hh)]
    V_qk, R_qk = WN.at[low, pl.ds(hh, hh)], WN.at[high, pl.ds(hh, hh)]

    in_keep("up", 1, DUP, keep_u, S_up)
    pl.semaphore_wait(credit.at[0], 1)
    cross("up1", S_up.at[1], wid, V_up)
    in_keep("up", 0, DUP, keep_u, S_up)
    copies.start("up0x", S_up.at[0], X_up, x_dev)

    crossed("dn1", R_dn)
    crossed("de1", R_de)
    copies.sent("wnx", "wnc", "wnf")
    pl.semaphore_signal(credit.at[2], inc=1, device_id=x_dev, device_id_type=MESH)
    pl.semaphore_signal(credit.at[3], inc=1, device_id=y_dev, device_id_type=MESH)
    pl.semaphore_signal(credit.at[4], inc=1, device_id=y_dev, device_id_type=MESH)

    def out_block(s):
        b = col_of[s]
        copies.came(f"oy{s}")

        def part(i):
            rs = at(b * blk + i * sub, sub)
            came = OY[s - 1, at(i * sub, sub), :]
            OUTP[rs, own] = (OUTP[rs, own].astype(F32) + came.astype(F32)).astype(BF16)

        tiles(blk // sub, part)
        copies.start(f"oz{s}", OUTP.at[rows(b), own], OZ.at[s - 2], {"col": b})

    out_block(2)

    def again(i):
        rs = at(i * sub, sub)
        normal = (X[rs, :].astype(F32) - STAT[rs, 0:1]) * STAT[rs, 1:2]
        N[rs, :] = (normal * NV[0:1, :] + NV[1:2, :]).astype(BF16)

    tiles(rows_all // sub, again)
    out_block(3)
    TMP[...] = jnp.zeros_like(TMP)
    for i in range(cols):
        mine, span, low = key_range(i)
        query = QKV[mine, 0:HD]
        p = jnp.exp(block_scores(i) - STAT[mine, 2:3])
        d_p = dot(DAT[mine, :], QKV[span, 2 * HD :], NT)
        delta = jnp.sum(d_p * p, axis=1, keepdims=True)
        d_s = (p * (d_p - delta)).astype(BF16)
        p_low = p.astype(BF16)
        d_query = dot(d_s, QKV[span, HD : 2 * HD], NN) * scale
        QKV[mine, 0:HD] = rotate(d_query, mine, -1.0).astype(BF16)
        for j in range(low // blk, i + 1):
            js = slice(j * blk - low, (j + 1) * blk - low)
            ks, vs = slice(j * HD, (j + 1) * HD), slice((cols + j) * HD, (cols + j + 1) * HD)
            TMP[:, ks] += dot(d_s[:, js], query, TN)
            TMP[:, vs] += dot(p_low[:, js], DAT[mine, :], TN)
    for j in range(cols):
        mine = slice(j * blk, (j + 1) * blk)
        ks, vs = slice(j * HD, (j + 1) * HD), slice((cols + j) * HD, (cols + j + 1) * HD)
        QKV[mine, HD : 2 * HD] = rotate(TMP[:, ks] * scale, mine, -1.0).astype(BF16)
        QKV[mine, 2 * HD :] = TMP[:, vs].astype(BF16)

    copies.sent("up0a", "up1a")
    in_give(
        "qk", QKV, give_h, hh, [SLOPE.at[:, pl.ds(0, hh)], SLOPE.at[:, pl.ds(hh, hh)]], S_qk
    )
    pl.semaphore_wait(credit.at[1], 1)
    crossed("up1", R_up)
    in_keep("qk", 1, QKV, keep_h, S_qk)
    pl.semaphore_wait(credit.at[2], 1)
    cross("qk1", S_qk.at[1], wid, V_qk)
    in_keep("qk", 0, QKV, keep_h, S_qk)
    copies.start("qk0x", S_qk.at[0], X_qk, x_dev)

    def gather_dp(name, slots):
        for word, device in (("c", core_dev), ("x", x_dev), ("d", far_dev)):
            copies.start(f"{name}{word}", slots.at[q], slots.at[q], device)

    def gathered_dp(name, slots):
        for word in "cxd":
            copies.came(f"{name}{word}")
        return slots[0] + slots[1] + slots[2] + slots[3]

    BQ[q, 0:1, :] = jnp.sum(DUP[...].astype(F32), axis=0, keepdims=True)
    BQ[q, 1:2, 0:heads] = jnp.sum(QKV[...].astype(F32), axis=0, keepdims=True)
    BQ[q, 1:2, heads:] = jnp.zeros((1, wid - heads), F32)
    BQ[q, 3:8, :] = jnp.zeros((5, wid), F32)
    gather_dp("b", BQ)

    NSUM[...] = jnp.zeros_like(NSUM)
    pl.semaphore_wait(credit.at[4], 1)

    def norm_back(b):
        rb = rows(b)
        mean, inv = STAT[rb, 0:1], STAT[rb, 1:2]

        def first(j, carry):
            along, plain = carry
            cs = at(j * TILE, TILE)
            one = dot(QKV[rb, :], WQ[cs, :], NT)
            two = dot(DUP[rb, :], WU[cs, :], NT)
            normal = (X[rb, cs].astype(F32) - mean) * inv
            NSUM[0:1, cs] += jnp.sum(one * normal, axis=0, keepdims=True)
            NSUM[1:2, cs] += jnp.sum(one, axis=0, keepdims=True)
            NSUM[2:3, cs] += jnp.sum(two * normal, axis=0, keepdims=True)
            NSUM[3:4, cs] += jnp.sum(two, axis=0, keepdims=True)
            grad = one * NV[0:1, cs] + two * NV[2:3, cs]
            TMP[:, cs] = grad
            along = along + jnp.sum(grad * normal, axis=1, keepdims=True)
            plain = plain + jnp.sum(grad, axis=1, keepdims=True)
            return along, plain

        zero = jnp.zeros((blk, 1), F32)
        along, plain = lax.fori_loop(0, width // TILE, first, (zero, zero))
        along, plain = along * (1.0 / width), plain * (1.0 / width)

        def second(j):
            cs = at(j * TILE, TILE)
            normal = (X[rb, cs].astype(F32) - mean) * inv
            N[rb, cs] = (inv * (TMP[:, cs] - plain - normal * along)).astype(BF16)

        tiles(width // TILE, second)

    EY = [HID.at[pl.ds(j * blk, blk), :] for j in range(3)]
    pl.semaphore_wait(credit.at[3], 1)
    for s in (2, 3):
        norm_back(col_of[s])
        copies.start(f"ey{s}", N.at[rows(col_of[s]), other], EY[s - 1], y_dev)
        if s == 2:
            spread_out("dn1", R_dn, g_down, down_at(1 - r, hi))
        else:
            spread_out("de1", R_de, g_dense, dense_at(1 - r, hi))
    norm_back(col_of[1])
    copies.start("ez1", N.at[rows(col_of[1]), :], DZ1, {"col": col_of[1]})
    norm_back(col_of[0])
    SMO[0:4, :] = NSUM[0:4, other]
    copies.start("sy", SMO, SMR, y_dev)

    def mine_at(i):
        return at(c * blk + i * sub, sub)

    def row_rest(buf, came, landing, name):
        copies.came(f"{name}z1")

        def part(i):
            rs = at(i * sub, sub)
            total = buf[mine_at(i), other].astype(F32) + came[rs, other].astype(F32)
            buf[mine_at(i), other] = total.astype(BF16)

        tiles(blk // sub, part)
        copies.start(f"{name}y0", buf.at[rows(c), other], landing, y_dev)

    def total_of(i, buf, near, far_ones, from_row):
        rs = at(i * sub, sub)
        total = buf[mine_at(i), own].astype(F32) + near[rs, own].astype(F32)
        for ref in far_ones:
            total = total + ref[rs, :].astype(F32)
        return total + from_row[rs, :].astype(F32)

    def x_block(s):
        b = col_of[s]
        copies.came(f"ey{s}")

        def part(i):
            rs = at(b * blk + i * sub, sub)
            came = EY[s - 1][at(i * sub, sub), :]
            N[rs, own] = (N[rs, own].astype(F32) + came.astype(F32)).astype(BF16)

        tiles(blk // sub, part)
        copies.start(f"ez{s}", N.at[rows(b), own], DZ.at[s - 2], {"col": b})

    row_rest(OUTP, OZ1, OY.at[0], "o")
    spread_out("up1", R_up, g_up, up_at(1 - r, hi))
    finish("dn0", S_dn.at[0], X_dn, g_down, down_at(r))
    finish("de0", S_de.at[0], X_de, g_dense, dense_at(r))
    finish("up0", S_up.at[0], X_up, g_up, up_at(r))
    crossed("qk1", R_qk)
    x_block(2)
    copies.came("sy")
    NZ[c, 0:4, :] = NSUM[0:4, own] + SMR[0:4, :]
    for s in (1, 2, 3):
        copies.start(f"sz{s}", NZ.at[c], NZ.at[c], {"col": col_of[s]})
    x_block(3)
    row_rest(N, DZ1, EY[0], "e")
    BS[...] = gathered_dp("b", BQ)
    copies.start("by", BS, BR, y_dev)
    finish("qk0", S_qk.at[0], X_qk, g_qkv, qkv_at(r))
    for s in (1, 2, 3):
        copies.came(f"sz{s}")
    NQ[q] = NZ[0] + NZ[1] + NZ[2] + NZ[3]
    gather_dp("n", NQ)
    pass_quarter("dn1", g_down, down_at(1 - r, 1 - hi))
    pass_quarter("de1", g_dense, dense_at(1 - r, 1 - hi))
    spread_out("qk1", R_qk, g_qkv, qkv_at(1 - r, hi))
    for name in ("oz2", "oz3", "oy0"):
        copies.came(name)

    def out_last(i):
        total = total_of(i, OUTP, OZ1, [OZ.at[0], OZ.at[1]], OY.at[0])
        total = total + X[mine_at(i), own].astype(F32)
        out[at(i * sub, sub), :] = (total + (dense_b[...] + down_b[...])).astype(BF16)

    tiles(blk // sub, out_last)
    pass_quarter("up1", g_up, up_at(1 - r, 1 - hi))
    copies.came("by")
    small[0:8, :] = BS[...]
    small[8:16, :] = BR[...]
    small[4:8, :] = gathered_dp("n", NQ)[0:4]
    for name in ("ez2", "ez3", "ey0"):
        copies.came(name)

    def x_last(i):
        total = total_of(i, N, DZ1, [DZ.at[0], DZ.at[1]], EY[0])
        in_grad[at(i * sub, sub), :] = cot[at(i * sub, sub), :].astype(F32) + total

    tiles(blk // sub, x_last)
    pass_quarter("qk1", g_qkv, qkv_at(1 - r, 1 - hi))
    for name in ("dn0", "de0", "up0", "qk0"):
        copies.came(f"{name}t")
    for name in ("dn1", "de1", "up1", "qk1"):
        copies.came(f"{name}t")
        copies.came(f"{name}f")
    for copy in local[6:]:
        copy.wait()
    copies.sent_all()


def scratch(blk, wid, cols, units, heads):
    tokens, width = blk * cols, 2 * wid
    low = [
        (tokens, width), (tokens, width), (width, heads), (width, units), (HD, width),
        (units, width), (tokens, width),
    ]
    V = pltpu.VMEM
    return (
        [V(shape, BF16) for shape in low]
        + [V((tokens, 128), F32)]
        + [
            V(shape, BF16)
            for shape in (
                (tokens, heads), (tokens, HD), (tokens, units), (tokens, units), (tokens, units),
                (tokens, HD), (tokens, width), (blk, width), (2, blk, wid), (3, blk, wid),
                (blk, width), (2, blk, wid),
                (2, units // 2, wid), (2, HD // 2, wid), (2, wid, units // 2), (2, wid, heads // 2),
                (units // 4, wid), (HD // 4, wid), (units // 4, wid), (HD // 4, wid),
                (units // 2, wid), (HD // 2, wid), (2, HD // 2, wid),
            )
        ]
        + [
            V((blk, width), F32),
            V((8, width), F32),
            V((tokens, 128), F32),
            V((tokens, 128), F32),
            V((8, width), F32),
            V((8, wid), F32),
            V((8, wid), F32),
            V((cols, 8, wid), F32),
            V((4, 8, wid), F32),
            V((4, 8, wid), F32),
            V((8, wid), F32),
            V((8, wid), F32),
            pltpu.SemaphoreType.DMA((120,)),
            pltpu.SemaphoreType.DMA((120,)),
            pltpu.SemaphoreType.DMA((20,)),
            pltpu.SemaphoreType.REGULAR((5,)),
        ]
    )


def swap(value, axis, mask):
    size = lax.axis_size(axis)
    return lax.ppermute(value, axis, [(i, i ^ mask) for i in range(size)])


def shards(
    hidden_in,
    segment,
    norm1_gain,
    norm1_bias,
    norm2_gain,
    norm2_bias,
    qkv_weight,
    qkv_bias,
    dense_weight,
    dense_bias,
    up_weight,
    up_bias,
    down_weight,
    down_bias,
    cotangent,
):
    blk, wid = hidden_in.shape
    cols = lax.axis_size("col")
    heads, units = qkv_weight.shape[1] // 2, up_weight.shape[1] // 2
    vectors = [
        v.reshape(1, -1)
        for v in (
            norm1_gain, norm1_bias, norm2_gain, norm2_bias, qkv_bias, up_bias, dense_bias, down_bias,
        )
    ]
    vmem = pl.BlockSpec(memory_space=pltpu.VMEM)
    far = pl.BlockSpec(memory_space=pl.ANY)
    shape = jax.ShapeDtypeStruct
    out, in_grad, small, g_qkv, g_dense, g_up, g_down = pl.pallas_call(
        functools.partial(step_kernel, (blk, wid, cols)),
        out_shape=(
            shape((blk, wid), BF16),
            shape((blk, wid), F32),
            shape((16, wid), F32),
            shape(qkv_weight.shape, BF16),
            shape(dense_weight.shape, BF16),
            shape(up_weight.shape, BF16),
            shape(down_weight.shape, BF16),
        ),
        in_specs=[vmem, vmem] + [far] * 4 + [vmem] * 9,
        out_specs=(vmem,) * 3 + (far,) * 4,
        scratch_shapes=scratch(blk, wid, cols, units, heads),
        compiler_params=pltpu.CompilerParams(
            collective_id=0, has_side_effects=True, vmem_limit_bytes=67043328
        ),
        name="step",
    )(
        hidden_in, cotangent, qkv_weight, up_weight, dense_weight, down_weight, segment, *vectors
    )

    grads = [g.astype(F32) for g in (g_qkv, g_dense, g_up, g_down)]
    mask = 4
    while mask < lax.axis_size("dp"):
        grads = [g + swap(g.astype(BF16), "dp", mask).astype(F32) for g in grads]
        small = small + swap(small, "dp", mask)
        mask *= 2
    row = lax.axis_index("row")

    def both(index):
        first, second = small[index], small[8 + index]
        return jnp.where(row == 0, first, second), jnp.where(row == 0, second, first)

    qkv_bias_grad = jnp.concatenate([part[:heads] for part in both(1)])
    up_bias_grad = jnp.concatenate(both(0))
    return (
        out,
        in_grad,
        small[4],
        small[5],
        small[6],
        small[7],
        grads[0],
        qkv_bias_grad,
        grads[1],
        small[2],
        grads[2],
        up_bias_grad,
        grads[3],
        small[2],
    )


def solution(mesh):
    return jax.shard_map(
        shards,
        mesh=mesh,
        in_specs=(
            P(("dp", "col"), "row"),
            P("dp", None),
            P("row"),
            P("row"),
            P("row"),
            P("row"),
            P("row", "col"),
            P("col"),
            P("col", "row"),
            P("row"),
            P("row", "col"),
            P("col"),
            P("col", "row"),
            P("row"),
            P(("dp", "col"), "row"),
        ),
        out_specs=(
            P(("dp", "col"), "row"),
            P(("dp", "col"), "row"),
            P("row"),
            P("row"),
            P("row"),
            P("row"),
            P("row", "col"),
            P("col"),
            P("col", "row"),
            P("row"),
            P("row", "col"),
            P("col"),
            P("col", "row"),
            P("row"),
        ),
        check_vma=False,
    )
```

```python
import functools
import math

import jax
import jax.numpy as jnp
from jax import lax
from jax.experimental import pallas as pl
from jax.experimental.pallas import tpu as pltpu
from jax.sharding import PartitionSpec as P

HD = 256
ROT = 64
F32 = jnp.float32
BF16 = jnp.bfloat16
MESH = pl.DeviceIdType.MESH

eps_norm = 1e-05
rope_base = 10000.0
TILE = 512
NN = (((1,), (0,)), ((), ()))
NT = (((1,), (1,)), ((), ()))
TN = (((0,), (0,)), ((), ()))


def dot(left, right, dims):
    return lax.dot_general(left, right, dims, preferred_element_type=F32)


class Copies:
    def __init__(self, send_sem, recv_sem):
        self.send_sem, self.recv_sem = send_sem, recv_sem
        self.made, self.open = {}, {}

    def start(self, name, source, target, device, when=None):
        index = len(self.made)
        copy = pltpu.make_async_remote_copy(
            src_ref=source,
            dst_ref=target,
            send_sem=self.send_sem.at[index],
            recv_sem=self.recv_sem.at[index],
            device_id=device,
            device_id_type=MESH,
        )
        self.made[name] = copy
        self.open[name] = when
        guarded(when, copy.start)

    def came(self, name, when=None):
        guarded(when, self.made[name].wait_recv)

    def sent(self, *names):
        for name in names:
            guarded(self.open.pop(name), self.made[name].wait_send)

    def sent_all(self):
        self.sent(*list(self.open))


def guarded(when, action):
    if when is None:
        action()
    else:
        pl.when(when)(action)


def row_of(vector):
    return vector.reshape(1, vector.shape[0])


def at(start, size):
    return pl.ds(pl.multiple_of(start, size), size)


def tiles(count, body):
    lax.fori_loop(0, count, lambda i, carry: (body(i), carry)[1], 0)


def step_kernel(
    sizes,
    hid, cot, wq, wu, wd, wn, seg, gain1, bias1, gain2, bias2, qkv_b, up_b, dense_b, down_b,
    out, in_grad, small, g_qkv, g_dense, g_up, g_down,
    X, G, WQ, WU, WD, WN, N, STAT, QKV, ATT, HID, SLOPE, DUP, DAT, OUTP, OZ1, OZ2, OZ3, OY, DZ1, DZ, COT,
    S_dn, S_de, S_up, S_qk, R_dn, R_de, V_dn, V_de, X_dn, X_de, A_de, TMP, NV, COS, SIN, NSUM, SMO, SMR, NZ, NQ, BQ, BS, BR,
    send_sem, recv_sem, local_sem, credit,
):
    blk, wid, cols = sizes
    rows_all = blk * cols
    width = 2 * wid
    heads, units = WQ.shape[1], WU.shape[1]
    hh, uh, dh = heads // 2, units // 2, HD // 2
    r = lax.axis_index("row")
    c = lax.axis_index("col")
    dp = lax.axis_index("dp")
    k = lax.rem(dp, 2)
    hi = lax.rem(lax.div(dp, 2), 2)
    q = k + 2 * hi
    core_dev = {"dp": dp + 1 - 2 * k}
    x_dev = {"dp": dp + 2 - 4 * hi}
    far_dev = {"dp": dp + 3 - 2 * k - 4 * hi}
    y_dev = {"row": 1 - r}
    c_low, c_high = lax.rem(c, 2), lax.div(c, 2)
    col_of = [c, c + 1 - 2 * c_low, c + 2 - 4 * c_high, 3 - c]
    own, other = pl.ds(0, wid), pl.ds(wid, wid)
    scale = 1.0 / math.sqrt(HD)
    copies = Copies(send_sem, recv_sem)

    barrier = pltpu.get_barrier_semaphore()
    friends = [core_dev, x_dev, far_dev, y_dev] + [{"col": col_of[s]} for s in (1, 2, 3)]
    for device in friends:
        pl.semaphore_signal(barrier, inc=1, device_id=device, device_id_type=MESH)

    local = []

    def fetch(source, target):
        copy = pltpu.make_async_copy(source, target, local_sem.at[len(local)])
        copy.start()
        local.append(copy)
        return copy

    fetch_c = fetch(cot, COT)
    fetch_x = fetch(hid, X.at[at(c * blk, blk), own])
    fetch_g = fetch(cot, G.at[at(c * blk, blk), own])
    fetch_u = fetch(wu.at[:, at(r * units, units)], WU.at[own, :])
    fetch_q = fetch(wq.at[:, at(r * heads, heads)], WQ.at[own, :])
    fetch_n = fetch(wn.at[at(r * units, units), :], WN.at[:, own])
    fetch_d = fetch(wd.at[at(r * HD, HD), :], WD.at[:, own])
    pl.semaphore_wait(barrier, len(friends))

    def rows(b):
        return at(b * blk, blk)

    def chain_send(tag, step, buf, columns, first=None):
        for word, move, edge in (("u", 1, c < cols - 1), ("d", -1, c >= 1)):
            block = c - move * (step - 1)
            valid = edge & (block >= 0) & (block <= cols - 1)
            source = first if first is not None else buf.at[rows(block), columns]
            copies.start(
                f"{tag}{word}{step}", source, buf.at[rows(block), columns], {"col": c + move}, valid
            )

    def chain_wait(tag, step):
        copies.came(f"{tag}u{step}", c >= step)
        copies.came(f"{tag}d{step}", c + step <= cols - 1)

    def row_send(name, s):
        b = col_of[s]
        copies.start(name, X.at[rows(b), own], X.at[rows(b), other], y_dev)

    q2 = q + 2 - 4 * hi

    def weight(name, source, full, row0, size, columns, spread):
        share = q if spread else k

        def place(index):
            return full.at[at(row0 + index * size, size), columns]

        copies.start(f"{name}y", source(at(share * size, size)), place(share), y_dev)

        def pass_on():
            copies.came(f"{name}y")
            if spread:
                copies.start(f"{name}x", place(q), place(q), x_dev)
            copies.start(f"{name}c", place(share), place(share), core_dev)

        def pass_far():
            copies.came(f"{name}x")
            copies.start(f"{name}f", place(q2), place(q2), core_dev)

        def done():
            copies.came(f"{name}c")
            if spread:
                copies.came(f"{name}f")

        return pass_on, pass_far, done

    everything = slice(None)
    chain_send("x", 1, X, own, hid)
    copies.start("xy0", hid, X.at[rows(c), other], y_dev)
    for j, vector in enumerate((gain1, bias1, gain2, bias2)):
        NV[j : j + 1, own] = row_of(vector[...])
    NV[4:8, own] = jnp.zeros((4, wid), F32)
    copies.start("nv", NV.at[:, own], NV.at[:, other], y_dev)
    wu_on, wu_far, wu_done = weight(
        "wu", lambda rs: wu.at[rs, at((1 - r) * units, units)], WU, wid, wid // 4, everything, True
    )

    seg_row = seg[...].astype(F32)
    seg_col = jnp.transpose(jnp.broadcast_to(seg_row, (128, rows_all)))
    STAT[:, 3:4] = seg_col[:, 0:1]

    def table(i):
        block = at(i * blk, blk)
        starts = jnp.sum(
            (seg_row < STAT[block, 3:4]).astype(F32), axis=1, keepdims=True
        )
        index = lax.broadcasted_iota(jnp.int32, (blk, 1), 0) + i * blk
        lane = lax.broadcasted_iota(jnp.int32, (1, 128), 1)
        turn = jnp.exp(
            lax.rem(lane, ROT // 2).astype(F32) * (-2.0 * math.log(rope_base) / ROT)
        )
        angles = (index.astype(F32) - starts) * turn
        COS[block, :] = jnp.where(lane < ROT, jnp.cos(angles), 1.0)
        SIN[block, :] = jnp.where(
            lane < ROT // 2, -jnp.sin(angles), jnp.where(lane < ROT, jnp.sin(angles), 0.0)
        )

    tiles(cols, table)

    def rotate(head, block, sign):
        first = head[:, :128]
        lane = lax.broadcasted_iota(jnp.int32, first.shape, 1)
        swapped = jnp.where(
            lane < ROT // 2, pltpu.roll(first, 128 - ROT // 2, 1), pltpu.roll(first, ROT // 2, 1)
        )
        turned = first * COS[block, :] + sign * (swapped * SIN[block, :])
        return jnp.concatenate([turned, head[:, 128:]], axis=1)

    sub = 64

    def norm_block(b):
        def part(i):
            rs = at(b * blk + i * sub, sub)
            x = X[rs, :].astype(F32)
            mean = jnp.sum(x, axis=1, keepdims=True) * (1.0 / width)
            square = jnp.sum(x * x, axis=1, keepdims=True) * (1.0 / width)
            inv = lax.rsqrt(square - mean * mean + eps_norm)
            STAT[rs, 0:1] = mean
            STAT[rs, 1:2] = inv
            normal = (x - mean) * inv
            OUTP[rs, :] = (normal * NV[0:1, :] + NV[1:2, :]).astype(BF16)
            N[rs, :] = (normal * NV[2:3, :] + NV[3:4, :]).astype(BF16)

        tiles(blk // sub, part)

    def up_block(b):
        def part(j):
            cs = at(j * TILE, TILE)
            bias = row_of(up_b[at(r * units + j * TILE, TILE)])
            up = dot(N[rows(b), :], WU[:, cs], NN) + bias
            cdf = 0.5 * (1.0 + lax.erf(up * (1.0 / math.sqrt(2.0))))
            HID[rows(b), cs] = (up * cdf).astype(BF16)
            SLOPE[rows(b), cs] = (
                cdf + up * jnp.exp(-0.5 * up * up) * (1.0 / math.sqrt(2.0 * math.pi))
            ).astype(BF16)

        tiles(units // TILE, part)

    fetch_c.wait()
    fetch_x.wait()
    fetch_g.wait()
    chain_wait("x", 1)
    chain_send("x", 2, X, own)
    row_send("xy1", 1)
    wu_on()
    chain_wait("x", 2)
    chain_send("x", 3, X, own)
    row_send("xy2", 2)
    chain_send("g", 1, G, own, cot)
    copies.came("nv")
    copies.came("xy0")
    norm_block(col_of[0])
    chain_wait("x", 3)
    row_send("xy3", 3)
    copies.start("gy", cot, G.at[rows(c), other], y_dev)
    wq_on, _, wq_done = weight(
        "wq", lambda rs: wq.at[rs, at((1 - r) * heads, heads)], WQ, wid, wid // 2, everything, False
    )

    def rows_of(ref, start, rs):
        return ref.at[at(start + rs.start, rs.size), :]

    wn_on, _, wn_done = weight(
        "wn", lambda rs: rows_of(wn, (1 - r) * units, rs), WN, 0, units // 2, other, False
    )
    wd_on, _, wd_done = weight(
        "wd", lambda rs: rows_of(wd, (1 - r) * HD, rs), WD, 0, HD // 2, other, False
    )
    wu_far()
    copies.came("xy1")
    norm_block(col_of[1])
    fetch_u.wait()
    wu_done()
    up_block(col_of[0])
    up_block(col_of[1])
    chain_wait("g", 1)
    chain_send("g", 2, G, own)
    copies.came("xy2")
    norm_block(col_of[2])
    up_block(col_of[2])
    chain_wait("g", 2)
    chain_send("g", 3, G, own)
    copies.came("xy3")
    norm_block(col_of[3])
    up_block(col_of[3])
    copies.came("gy")
    chain_send("h", 1, G, other)

    def grad_send(name, staged, left, right, n_rows, n_cols, target):
        def part(i):
            cs = at(i * TILE, TILE)
            staged[:, cs] = dot(left(None), right(cs), TN).astype(BF16)

        tiles(n_cols // TILE, part)
        copies.start(name, staged, target, core_dev)

    hid_keep, hid_send = at(k * uh, uh), at((1 - k) * uh, uh)
    att_keep, att_send = at(k * dh, dh), at((1 - k) * dh, dh)

    def out_grad(name, side, left_ref, keep, give, staged, landing):
        base = side * wid

        def give_part(i):
            cs = at(i * TILE, TILE)
            staged[:, cs] = dot(
                left_ref[:, give], G[:, at(base + i * TILE, TILE)], TN
            ).astype(BF16)

        tiles(wid // TILE, give_part)
        copies.start(f"{name}a", staged, landing, core_dev)

    def out_keep(name, side, left_ref, keep, landing):
        base = side * wid
        copies.came(f"{name}a")

        def keep_part(i):
            cs = at(i * TILE, TILE)
            mine = dot(left_ref[:, keep], G[:, at(base + i * TILE, TILE)], TN)
            landing[:, cs] = (mine + landing[:, cs].astype(F32)).astype(BF16)

        tiles(wid // TILE, keep_part)

    halves = {}

    def cross(name, total, n_rows, landing):
        half_rows = n_rows // 2
        give, keep = at((1 - hi) * half_rows, half_rows), at(hi * half_rows, half_rows)
        copies.start(f"{name}x", total.at[give, :], landing, x_dev)
        halves[name] = (total.at[keep, :], landing)

    def crossed(name, target):
        mine, landing = halves[name]
        copies.came(f"{name}x")
        n = landing.shape[0]
        step = min(n, 128)

        def part(i):
            rs = at(i * step, step)
            landing[rs, :] = (mine[rs, :].astype(F32) + landing[rs, :].astype(F32)).astype(BF16)

        tiles(n // step, part)
        copies.start(f"{name}y", landing, target, y_dev)

    def spread_out(name, came, result, here):
        copies.came(f"{name}y")
        copies.start(f"{name}g", came, result.at[here], x_dev)
        copies.start(f"{name}t", came, result.at[here], core_dev)
        fetch(came, result.at[here])

    def pass_quarter(name, result, there):
        copies.came(f"{name}g")
        copies.start(f"{name}f", result.at[there], result.at[there], core_dev)

    def finish(name, total, came, result, here):
        copies.came(f"{name}x")
        n = total.shape[0]
        step = min(n, 128)

        def part(i):
            rs = at(i * step, step)
            came[rs, :] = (total[rs, :].astype(F32) + came[rs, :].astype(F32)).astype(BF16)

        tiles(n // step, part)
        copies.start(f"{name}t", came, result.at[here], core_dev)
        fetch(came, result.at[here])

    wide = slice(None)

    def down_at(side, part=None):
        start, n = side * units + k * uh, uh
        if part is not None:
            start, n = start + part * (uh // 2), uh // 2
        return (at(start, n), wide)

    def dense_at(side, part=None):
        start, n = side * HD + k * dh, dh
        if part is not None:
            start, n = start + part * (dh // 2), dh // 2
        return (at(start, n), wide)

    def up_at(side, part=None):
        taken = wide if part is None else at(part * (wid // 2), wid // 2)
        return (taken, at(side * units + k * uh, uh))

    def qkv_at(side, part=None):
        taken = wide if part is None else at(part * (wid // 2), wid // 2)
        return (taken, at(side * heads + k * hh, hh))

    chain_wait("g", 3)
    out_grad("dn0", 0, HID, hid_keep, hid_send, DUP.at[pl.ds(0, uh), :], S_dn.at[0])
    out_keep("dn0", 0, HID, hid_keep, S_dn.at[0])
    copies.start("dn0x", S_dn.at[0], X_dn, x_dev)

    chain_wait("h", 1)
    chain_send("h", 2, G, other)
    fetch_q.wait()
    wq_on()
    wq_done()

    def qkv_block(i):
        block = at(i * blk, blk)
        for j in range(3):
            bias = row_of(qkv_b[at(r * heads + j * HD, HD)])
            value = dot(OUTP[block, :], WQ[:, j * HD : (j + 1) * HD], NN) + bias
            if j < 2:
                value = rotate(value, block, 1.0)
            QKV[block, j * HD : (j + 1) * HD] = value.astype(BF16)

    tiles(cols, qkv_block)
    chain_wait("h", 2)
    chain_send("h", 3, G, other)

    def key_range(i):
        low = max(0, i - 2) * blk
        return slice(i * blk, (i + 1) * blk), slice(low, (i + 1) * blk), low

    def block_scores(i):
        mine, span, low = key_range(i)
        n = span.stop - low
        s = dot(QKV[mine, 0:HD], QKV[span, HD : 2 * HD], NT) * scale
        row_id = lax.broadcasted_iota(jnp.int32, (blk, n), 0) + i * blk
        col_id = lax.broadcasted_iota(jnp.int32, (blk, n), 1) + low
        same = STAT[mine, 3:4] == seg_row[:, span]
        return jnp.where(same & (col_id <= row_id), s, -1e30)

    for i in range(cols):
        mine, span, low = key_range(i)
        s = block_scores(i)
        largest = jnp.max(s, axis=1, keepdims=True)
        p = jnp.exp(s - largest)
        total = jnp.sum(p, axis=1, keepdims=True)
        STAT[mine, 2:3] = largest + jnp.log(total)
        p_low = (p / total).astype(BF16)
        ATT[mine, :] = dot(p_low, QKV[span, 2 * HD :], NN).astype(BF16)
    out_grad("de0", 0, ATT, att_keep, att_send, A_de.at[0], S_de.at[0])
    fetch_n.wait()
    fetch_d.wait()

    def branch_block(b, side):
        def part(j):
            cs = at(side * wid + j * TILE, TILE)
            both = dot(ATT[rows(b), :], WD[:, cs], NN) + dot(HID[rows(b), :], WN[:, cs], NN)
            OUTP[rows(b), cs] = both.astype(BF16)

        tiles(wid // TILE, part)

    branch_block(col_of[2], 0)
    copies.start("oa2", OUTP.at[rows(col_of[2]), own], OZ2.at[:, own], {"col": col_of[2]})
    out_keep("de0", 0, ATT, att_keep, S_de.at[0])
    copies.start("de0x", S_de.at[0], X_de, x_dev)
    for s in (3, 1, 0):
        branch_block(col_of[s], 0)

    chain_wait("h", 3)
    out_grad("dn1", 1, HID, hid_keep, hid_send, DUP.at[pl.ds(uh, uh), :], S_dn.at[1])
    out_grad("de1", 1, ATT, att_keep, att_send, A_de.at[1], S_de.at[1])
    out_keep("dn1", 1, HID, hid_keep, S_dn.at[1])
    cross("dn1", S_dn.at[1], uh, V_dn)
    out_keep("de1", 1, ATT, att_keep, S_de.at[1])
    cross("de1", S_de.at[1], dh, V_de)
    wn_on()
    wn_done()

    copies.sent("dn0a", "dn1a")

    def up_grad_part(i):
        block = at(i * blk, blk)
        for j in range(units // TILE):
            cs = slice(j * TILE, (j + 1) * TILE)
            back = dot(G[block, :], WN[cs, :], NT)
            DUP[block, cs] = (back * SLOPE[block, cs].astype(F32)).astype(BF16)

    tiles(cols, up_grad_part)
    keep_u, give_u = at(k * uh, uh), at((1 - k) * uh, uh)
    keep_h, give_h = at(k * hh, hh), at((1 - k) * hh, hh)

    def in_give(name, right_ref, give, n, staged, landing):
        for side in (0, 1):

            def part(i):
                rs = at(i * TILE, TILE)
                lefts = N[:, at(side * wid + i * TILE, TILE)]
                staged[side][rs, :] = dot(lefts, right_ref[:, give], TN).astype(BF16)

            tiles(wid // TILE, part)
            copies.start(f"{name}{side}a", staged[side], landing.at[side], core_dev)

    def in_keep(name, side, right_ref, keep, landing):
        copies.came(f"{name}{side}a")

        def part(i):
            rs = at(i * TILE, TILE)
            mine = dot(N[:, at(side * wid + i * TILE, TILE)], right_ref[:, keep], TN)
            landing[side, rs, :] = (mine + landing[side, rs, :].astype(F32)).astype(BF16)

        tiles(wid // TILE, part)

    in_give(
        "up", DUP, give_u, uh, [SLOPE.at[:, pl.ds(0, uh)], SLOPE.at[:, pl.ds(uh, uh)]], S_up
    )
    wd_on()
    wd_done()
    for i in range(cols):
        mine = slice(i * blk, (i + 1) * blk)
        DAT[mine, :] = dot(G[mine, :], WD[...], NT).astype(BF16)
    BQ[q, 2:3, :] = jnp.sum(G[:, own].astype(F32), axis=0, keepdims=True)

    copies.sent(*[f"{t}{w}{s}" for t in "gh" for w in "ud" for s in (1, 2, 3)])
    pl.semaphore_signal(credit.at[0], inc=1, device_id=x_dev, device_id_type=MESH)
    pl.semaphore_signal(credit.at[1], inc=1, device_id=y_dev, device_id_type=MESH)
    X_up, low, high = G.at[:, pl.ds(0, uh)], pl.ds(0, wid // 2), pl.ds(wid // 2, wid // 2)
    V_up, R_up = G.at[low, pl.ds(uh, uh)], G.at[high, pl.ds(uh, uh)]
    X_qk = WN.at[:, pl.ds(0, hh)]
    V_qk, R_qk = WN.at[low, pl.ds(hh, hh)], WN.at[high, pl.ds(hh, hh)]

    crossed("dn1", R_dn)
    in_keep("up", 1, DUP, keep_u, S_up)
    pl.semaphore_wait(credit.at[0], 1)
    cross("up1", S_up.at[1], wid, V_up)
    in_keep("up", 0, DUP, keep_u, S_up)
    copies.start("up0x", S_up.at[0], X_up, x_dev)

    branch_block(col_of[3], 1)
    copies.start("oy3", OUTP.at[rows(col_of[3]), other], OY.at[1], y_dev)
    branch_block(col_of[2], 1)
    copies.start("ob2", OUTP.at[rows(col_of[2]), other], OZ2.at[:, other], {"col": col_of[2]})
    branch_block(col_of[1], 1)
    copies.start("oz1", OUTP.at[rows(col_of[1]), :], OZ1, {"col": col_of[1]})
    branch_block(col_of[0], 1)
    crossed("de1", R_de)
    copies.sent("wnc")
    pl.semaphore_signal(credit.at[2], inc=1, device_id=x_dev, device_id_type=MESH)
    pl.semaphore_signal(credit.at[3], inc=1, device_id=y_dev, device_id_type=MESH)
    pl.semaphore_signal(credit.at[4], inc=1, device_id=y_dev, device_id_type=MESH)

    def out_block():
        b = col_of[3]
        copies.came("oy3")

        def part(i):
            rs = at(b * blk + i * sub, sub)
            came = OY[1, at(i * sub, sub), :]
            OUTP[rs, own] = (OUTP[rs, own].astype(F32) + came.astype(F32)).astype(BF16)

        tiles(blk // sub, part)
        copies.start("oz3", OUTP.at[rows(b), own], OZ3, {"col": b})

    def again(i):
        rs = at(i * sub, sub)
        normal = (X[rs, :].astype(F32) - STAT[rs, 0:1]) * STAT[rs, 1:2]
        N[rs, :] = (normal * NV[0:1, :] + NV[1:2, :]).astype(BF16)

    tiles(rows_all // sub, again)
    TMP[...] = jnp.zeros_like(TMP)
    for i in range(cols):
        mine, span, low = key_range(i)
        query = QKV[mine, 0:HD]
        p = jnp.exp(block_scores(i) - STAT[mine, 2:3])
        d_p = dot(DAT[mine, :], QKV[span, 2 * HD :], NT)
        delta = jnp.sum(d_p * p, axis=1, keepdims=True)
        d_s = (p * (d_p - delta)).astype(BF16)
        p_low = p.astype(BF16)
        d_query = dot(d_s, QKV[span, HD : 2 * HD], NN) * scale
        QKV[mine, 0:HD] = rotate(d_query, mine, -1.0).astype(BF16)
        for j in range(low // blk, i + 1):
            js = slice(j * blk - low, (j + 1) * blk - low)
            ks, vs = slice(j * HD, (j + 1) * HD), slice((cols + j) * HD, (cols + j + 1) * HD)
            TMP[:, ks] += dot(d_s[:, js], query, TN)
            TMP[:, vs] += dot(p_low[:, js], DAT[mine, :], TN)
    for j in range(cols):
        mine = slice(j * blk, (j + 1) * blk)
        ks, vs = slice(j * HD, (j + 1) * HD), slice((cols + j) * HD, (cols + j + 1) * HD)
        QKV[mine, HD : 2 * HD] = rotate(TMP[:, ks] * scale, mine, -1.0).astype(BF16)
        QKV[mine, 2 * HD :] = TMP[:, vs].astype(BF16)

    copies.sent("up0a", "up1a")
    in_give(
        "qk", QKV, give_h, hh, [SLOPE.at[:, pl.ds(0, hh)], SLOPE.at[:, pl.ds(hh, hh)]], S_qk
    )
    pl.semaphore_wait(credit.at[1], 1)
    crossed("up1", R_up)
    in_keep("qk", 1, QKV, keep_h, S_qk)
    pl.semaphore_wait(credit.at[2], 1)
    cross("qk1", S_qk.at[1], wid, V_qk)
    in_keep("qk", 0, QKV, keep_h, S_qk)
    copies.start("qk0x", S_qk.at[0], X_qk, x_dev)

    def gather_dp(name, slots):
        for word, device in (("c", core_dev), ("x", x_dev), ("d", far_dev)):
            copies.start(f"{name}{word}", slots.at[q], slots.at[q], device)

    def gathered_dp(name, slots):
        for word in "cxd":
            copies.came(f"{name}{word}")
        return slots[0] + slots[1] + slots[2] + slots[3]

    BQ[q, 0:1, :] = jnp.sum(DUP[...].astype(F32), axis=0, keepdims=True)
    BQ[q, 1:2, 0:heads] = jnp.sum(QKV[...].astype(F32), axis=0, keepdims=True)
    BQ[q, 1:2, heads:] = jnp.zeros((1, wid - heads), F32)
    BQ[q, 3:8, :] = jnp.zeros((5, wid), F32)
    gather_dp("b", BQ)

    NSUM[...] = jnp.zeros_like(NSUM)
    pl.semaphore_wait(credit.at[4], 1)

    def norm_back(b):
        rb = rows(b)
        mean, inv = STAT[rb, 0:1], STAT[rb, 1:2]

        def first(j, carry):
            along, plain = carry
            cs = at(j * TILE, TILE)
            one = dot(QKV[rb, :], WQ[cs, :], NT)
            two = dot(DUP[rb, :], WU[cs, :], NT)
            normal = (X[rb, cs].astype(F32) - mean) * inv
            NSUM[0:1, cs] += jnp.sum(one * normal, axis=0, keepdims=True)
            NSUM[1:2, cs] += jnp.sum(one, axis=0, keepdims=True)
            NSUM[2:3, cs] += jnp.sum(two * normal, axis=0, keepdims=True)
            NSUM[3:4, cs] += jnp.sum(two, axis=0, keepdims=True)
            grad = one * NV[0:1, cs] + two * NV[2:3, cs]
            TMP[:, cs] = grad
            along = along + jnp.sum(grad * normal, axis=1, keepdims=True)
            plain = plain + jnp.sum(grad, axis=1, keepdims=True)
            return along, plain

        zero = jnp.zeros((blk, 1), F32)
        along, plain = lax.fori_loop(0, width // TILE, first, (zero, zero))
        along, plain = along * (1.0 / width), plain * (1.0 / width)

        def second(j):
            cs = at(j * TILE, TILE)
            normal = (X[rb, cs].astype(F32) - mean) * inv
            N[rb, cs] = (inv * (TMP[:, cs] - plain - normal * along)).astype(BF16)

        tiles(width // TILE, second)

    EY = [HID.at[pl.ds(j * blk, blk), :] for j in range(3)]
    pl.semaphore_wait(credit.at[3], 1)
    for s in (2, 3):
        norm_back(col_of[s])
        copies.start(f"ey{s}", N.at[rows(col_of[s]), other], EY[s - 1], y_dev)
        if s == 2:
            out_block()
            spread_out("dn1", R_dn, g_down, down_at(1 - r, hi))
        else:
            spread_out("de1", R_de, g_dense, dense_at(1 - r, hi))
    norm_back(col_of[1])
    copies.start("ez1", N.at[rows(col_of[1]), :], DZ1, {"col": col_of[1]})
    norm_back(col_of[0])
    SMO[0:4, :] = NSUM[0:4, other]
    copies.start("sy", SMO, SMR, y_dev)

    def mine_at(i):
        return at(c * blk + i * sub, sub)

    def row_rest(buf, names, whole, landing, name):
        for arrival in names:
            copies.came(arrival)

        def part(i):
            rs = at(i * sub, sub)
            total = buf[mine_at(i), other].astype(F32)
            for ref in whole:
                total = total + ref[rs, other].astype(F32)
            buf[mine_at(i), other] = total.astype(BF16)

        tiles(blk // sub, part)
        copies.start(name, buf.at[rows(c), other], landing, y_dev)

    def total_of(i, buf, whole, parts):
        rs = at(i * sub, sub)
        total = buf[mine_at(i), own].astype(F32)
        for ref in whole:
            total = total + ref[rs, own].astype(F32)
        for ref in parts:
            total = total + ref[rs, :].astype(F32)
        return total

    def x_block(s):
        b = col_of[s]
        copies.came(f"ey{s}")

        def part(i):
            rs = at(b * blk + i * sub, sub)
            came = EY[s - 1][at(i * sub, sub), :]
            N[rs, own] = (N[rs, own].astype(F32) + came.astype(F32)).astype(BF16)

        tiles(blk // sub, part)
        copies.start(f"ez{s}", N.at[rows(b), own], DZ.at[s - 2], {"col": b})

    row_rest(OUTP, ("oz1", "oa2", "ob2"), (OZ1, OZ2), OY.at[0], "oy0")
    spread_out("up1", R_up, g_up, up_at(1 - r, hi))
    finish("dn0", S_dn.at[0], X_dn, g_down, down_at(r))
    finish("de0", S_de.at[0], X_de, g_dense, dense_at(r))
    finish("up0", S_up.at[0], X_up, g_up, up_at(r))
    crossed("qk1", R_qk)
    x_block(2)
    copies.came("sy")
    NZ[c, 0:4, :] = NSUM[0:4, own] + SMR[0:4, :]
    for s in (1, 2, 3):
        copies.start(f"sz{s}", NZ.at[c], NZ.at[c], {"col": col_of[s]})
    x_block(3)
    row_rest(N, ("ez1",), (DZ1,), EY[0], "ey0")
    BS[...] = gathered_dp("b", BQ)
    copies.start("by", BS, BR, y_dev)
    finish("qk0", S_qk.at[0], X_qk, g_qkv, qkv_at(r))
    for s in (1, 2, 3):
        copies.came(f"sz{s}")
    NQ[q] = NZ[0] + NZ[1] + NZ[2] + NZ[3]
    gather_dp("n", NQ)
    pass_quarter("dn1", g_down, down_at(1 - r, 1 - hi))
    pass_quarter("de1", g_dense, dense_at(1 - r, 1 - hi))
    spread_out("qk1", R_qk, g_qkv, qkv_at(1 - r, hi))
    for name in ("oz3", "oy0"):
        copies.came(name)

    def out_last(i):
        total = total_of(i, OUTP, (OZ1, OZ2), (OZ3, OY.at[0]))
        total = total + X[mine_at(i), own].astype(F32)
        out[at(i * sub, sub), :] = (total + row_of(dense_b[...] + down_b[...])).astype(BF16)

    tiles(blk // sub, out_last)
    pass_quarter("up1", g_up, up_at(1 - r, 1 - hi))
    copies.came("by")
    small[0:8, :] = BS[...]
    small[8:16, :] = BR[...]
    small[4:8, :] = gathered_dp("n", NQ)[0:4]
    for name in ("ez2", "ez3", "ey0"):
        copies.came(name)

    def x_last(i):
        total = total_of(i, N, (DZ1,), (DZ.at[0], DZ.at[1], EY[0]))
        in_grad[at(i * sub, sub), :] = COT[at(i * sub, sub), :].astype(F32) + total

    tiles(blk // sub, x_last)
    pass_quarter("qk1", g_qkv, qkv_at(1 - r, 1 - hi))
    for name in ("dn0", "de0", "up0", "qk0"):
        copies.came(f"{name}t")
    for name in ("dn1", "de1", "up1", "qk1"):
        copies.came(f"{name}t")
        copies.came(f"{name}f")
    for copy in local[7:]:
        copy.wait()
    copies.sent_all()


def scratch(blk, wid, cols, units, heads):
    tokens, width = blk * cols, 2 * wid
    low = [
        (tokens, width), (tokens, width), (width, heads), (width, units), (HD, width),
        (units, width), (tokens, width),
    ]
    V = pltpu.VMEM
    return (
        [V(shape, BF16) for shape in low]
        + [V((tokens, 128), F32)]
        + [
            V(shape, BF16)
            for shape in (
                (tokens, heads), (tokens, HD), (tokens, units), (tokens, units), (tokens, units),
                (tokens, HD), (tokens, width), (blk, width), (blk, width), (blk, wid),
                (2, blk, wid), (blk, width), (2, blk, wid), (blk, wid),
                (2, units // 2, wid), (2, HD // 2, wid), (2, wid, units // 2), (2, wid, heads // 2),
                (units // 4, wid), (HD // 4, wid), (units // 4, wid), (HD // 4, wid),
                (units // 2, wid), (HD // 2, wid), (2, HD // 2, wid),
            )
        ]
        + [
            V((blk, width), F32),
            V((8, width), F32),
            V((tokens, 128), F32),
            V((tokens, 128), F32),
            V((8, width), F32),
            V((8, wid), F32),
            V((8, wid), F32),
            V((cols, 8, wid), F32),
            V((4, 8, wid), F32),
            V((4, 8, wid), F32),
            V((8, wid), F32),
            V((8, wid), F32),
            pltpu.SemaphoreType.DMA((120,)),
            pltpu.SemaphoreType.DMA((120,)),
            pltpu.SemaphoreType.DMA((20,)),
            pltpu.SemaphoreType.REGULAR((5,)),
        ]
    )


def widen_kernel(*refs):
    given, results = refs[:7], refs[7:]
    small = given[6]
    for source, target in zip(given[:6], results[:6]):
        target[...] = source[...].astype(target.dtype)

    @pl.when(pl.program_id(0) == 0)
    def _():
        gain1, bias1, gain2, bias2, qkv_sum, dense_sum, up_sum, down_sum = results[6:]
        for j, ref in enumerate((gain1, bias1, gain2, bias2)):
            ref[...] = small[4 + j]
        dense_sum[...] = small[2]
        down_sum[...] = small[2]
        r = lax.axis_index("row")
        for ref, index in ((up_sum, 0), (qkv_sum, 1)):
            n = ref.shape[0] // 2
            ref[at(r * n, n)] = small[index, 0:n]
            ref[at((1 - r) * n, n)] = small[8 + index, 0:n]


def swap(value, axis, mask):
    size = lax.axis_size(axis)
    return lax.ppermute(value, axis, [(i, i ^ mask) for i in range(size)])


def shards(
    hidden_in,
    segment,
    norm1_gain,
    norm1_bias,
    norm2_gain,
    norm2_bias,
    qkv_weight,
    qkv_bias,
    dense_weight,
    dense_bias,
    up_weight,
    up_bias,
    down_weight,
    down_bias,
    cotangent,
):
    blk, wid = hidden_in.shape
    cols = lax.axis_size("col")
    heads, units = qkv_weight.shape[1] // 2, up_weight.shape[1] // 2
    vectors = (
        norm1_gain, norm1_bias, norm2_gain, norm2_bias, qkv_bias, up_bias, dense_bias, down_bias,
    )
    vmem = pl.BlockSpec(memory_space=pltpu.VMEM)
    far = pl.BlockSpec(memory_space=pl.ANY)
    shape = jax.ShapeDtypeStruct
    out, in_grad, small, g_qkv, g_dense, g_up, g_down = pl.pallas_call(
        functools.partial(step_kernel, (blk, wid, cols)),
        out_shape=(
            shape((blk, wid), BF16),
            shape((blk, wid), F32),
            shape((16, wid), F32),
            shape(qkv_weight.shape, BF16),
            shape(dense_weight.shape, BF16),
            shape(up_weight.shape, BF16),
            shape(down_weight.shape, BF16),
        ),
        in_specs=[far] * 6 + [vmem] * 9,
        out_specs=(vmem,) * 3 + (far,) * 4,
        scratch_shapes=scratch(blk, wid, cols, units, heads),
        compiler_params=pltpu.CompilerParams(
            collective_id=0, has_side_effects=True, vmem_limit_bytes=67043328
        ),
        name="step",
    )(
        hidden_in, cotangent, qkv_weight, up_weight, dense_weight, down_weight, segment, *vectors
    )

    grads = (g_qkv, g_dense, g_up, g_down)
    mask = 4
    while mask < lax.axis_size("dp"):
        grads = tuple(
            (g.astype(F32) + swap(g, "dp", mask).astype(F32)).astype(BF16) for g in grads
        )
        small = small + swap(small, "dp", mask)
        mask *= 2
    steps = 4

    def cut(array):
        rows, columns = array.shape
        return pl.BlockSpec((rows // steps, columns), lambda i: (i, 0))

    def whole(n):
        return pl.BlockSpec((n,), lambda i: (0,))

    lengths = [wid] * 4 + [2 * heads, wid, 2 * units, wid]
    widened = pl.pallas_call(
        widen_kernel,
        grid=(steps,),
        out_shape=[shape(out.shape, BF16), shape(in_grad.shape, F32)]
        + [shape(g.shape, F32) for g in grads]
        + [shape((n,), F32) for n in lengths],
        in_specs=[cut(out), cut(in_grad)]
        + [cut(g) for g in grads]
        + [pl.BlockSpec(small.shape, lambda i: (0, 0))],
        out_specs=[cut(out), cut(in_grad)] + [cut(g) for g in grads] + [whole(n) for n in lengths],
        compiler_params=pltpu.CompilerParams(vmem_limit_bytes=60 << 20),
        name="widen",
    )(out, in_grad, *grads, small)
    out, in_grad, d_qkv, d_dense, d_up, d_down, *sums = widened
    return (
        out,
        in_grad,
        sums[0],
        sums[1],
        sums[2],
        sums[3],
        d_qkv,
        sums[4],
        d_dense,
        sums[5],
        d_up,
        sums[6],
        d_down,
        sums[7],
    )


def solution(mesh):
    return jax.shard_map(
        shards,
        mesh=mesh,
        in_specs=(
            P(("dp", "col"), "row"),
            P("dp", None),
            P("row"),
            P("row"),
            P("row"),
            P("row"),
            P("row", "col"),
            P("col"),
            P("col", "row"),
            P("row"),
            P("row", "col"),
            P("col"),
            P("col", "row"),
            P("row"),
            P(("dp", "col"), "row"),
        ),
        out_specs=(
            P(("dp", "col"), "row"),
            P(("dp", "col"), "row"),
            P("row"),
            P("row"),
            P("row"),
            P("row"),
            P("row", "col"),
            P("col"),
            P("col", "row"),
            P("row"),
            P("row", "col"),
            P("col"),
            P("col", "row"),
            P("row"),
        ),
        check_vma=False,
    )
```

```python
import functools
import math

import jax
import jax.numpy as jnp
from jax import lax
from jax.experimental import pallas as pl
from jax.experimental.pallas import tpu as pltpu
from jax.sharding import PartitionSpec as P

HD = 256
ROT = 64
F32 = jnp.float32
BF16 = jnp.bfloat16
MESH = pl.DeviceIdType.MESH

eps_norm = 1e-05
rope_base = 10000.0
TILE = 512
NN = (((1,), (0,)), ((), ()))
NT = (((1,), (1,)), ((), ()))
TN = (((0,), (0,)), ((), ()))


def dot(left, right, dims):
    return lax.dot_general(left, right, dims, preferred_element_type=F32)


class Copies:
    def __init__(self, send_sem, recv_sem):
        self.send_sem, self.recv_sem = send_sem, recv_sem
        self.made, self.open = {}, {}

    def start(self, name, source, target, device, when=None):
        index = len(self.made)
        copy = pltpu.make_async_remote_copy(
            src_ref=source,
            dst_ref=target,
            send_sem=self.send_sem.at[index],
            recv_sem=self.recv_sem.at[index],
            device_id=device,
            device_id_type=MESH,
        )
        self.made[name] = copy
        self.open[name] = when
        guarded(when, copy.start)

    def came(self, name, when=None):
        guarded(when, self.made[name].wait_recv)

    def sent(self, *names):
        for name in names:
            guarded(self.open.pop(name), self.made[name].wait_send)

    def sent_all(self):
        self.sent(*list(self.open))


def guarded(when, action):
    if when is None:
        action()
    else:
        pl.when(when)(action)


def row_of(vector):
    return vector.reshape(1, vector.shape[0])


def at(start, size):
    return pl.ds(pl.multiple_of(start, size), size)


def tiles(count, body):
    lax.fori_loop(0, count, lambda i, carry: (body(i), carry)[1], 0)


def step_kernel(
    sizes,
    hid, cot, wq, wu, wd, wn, seg, gain1, bias1, gain2, bias2, qkv_b, up_b, dense_b, down_b,
    out, in_grad, small, g_qkv, g_dense, g_up, g_down,
    X, G, WQ, WU, WD, WN, N, STAT, QKV, ATT, HID, SLOPE, DUP, DAT, OUTP, OZ1, OZ2, OZ3, OY, DZ1, DZ, COT,
    S_dn, S_de, S_up, S_qk, R_dn, R_de, V_dn, V_de, X_dn, X_de, A_de, TMP, NV, COS, SIN, NSUM, SMO, SMR, NZ, NQ, BQ, BS, BR,
    send_sem, recv_sem, local_sem, credit,
):
    blk, wid, cols = sizes
    rows_all = blk * cols
    width = 2 * wid
    heads, units = WQ.shape[1], WU.shape[1]
    hh, uh, dh = heads // 2, units // 2, HD // 2
    r = lax.axis_index("row")
    c = lax.axis_index("col")
    dp = lax.axis_index("dp")
    k = lax.rem(dp, 2)
    hi = lax.rem(lax.div(dp, 2), 2)
    q = k + 2 * hi
    core_dev = {"dp": dp + 1 - 2 * k}
    x_dev = {"dp": dp + 2 - 4 * hi}
    far_dev = {"dp": dp + 3 - 2 * k - 4 * hi}
    y_dev = {"row": 1 - r}
    c_low, c_high = lax.rem(c, 2), lax.div(c, 2)
    col_of = [c, c + 1 - 2 * c_low, c + 2 - 4 * c_high, 3 - c]
    own, other = pl.ds(0, wid), pl.ds(wid, wid)
    scale = 1.0 / math.sqrt(HD)
    copies = Copies(send_sem, recv_sem)

    barrier = pltpu.get_barrier_semaphore()
    for device in (core_dev, x_dev, y_dev):
        pl.semaphore_signal(barrier, inc=1, device_id=device, device_id_type=MESH)
    for move, inside in ((1, c < cols - 1), (-1, c >= 1)):

        @pl.when(inside)
        def _():
            pl.semaphore_signal(
                barrier, inc=1, device_id={"col": c + move}, device_id_type=MESH
            )

    local = []

    def fetch(source, target):
        copy = pltpu.make_async_copy(source, target, local_sem.at[len(local)])
        copy.start()
        local.append(copy)
        return copy

    fetch_c = fetch(cot, COT)
    fetch_x = fetch(hid, X.at[at(c * blk, blk), own])
    fetch_g = fetch(cot, G.at[at(c * blk, blk), own])
    fetch_u = fetch(wu.at[:, at(r * units, units)], WU.at[own, :])
    fetch_q = fetch(wq.at[:, at(r * heads, heads)], WQ.at[own, :])
    fetch_n = fetch(wn.at[at(r * units, units), :], WN.at[:, own])
    fetch_d = fetch(wd.at[at(r * HD, HD), :], WD.at[:, own])
    pl.semaphore_wait(
        barrier, 3 + (c < cols - 1).astype(jnp.int32) + (c >= 1).astype(jnp.int32)
    )

    def rows(b):
        return at(b * blk, blk)

    def chain_send(tag, step, buf, columns, first=None):
        for word, move, edge in (("u", 1, c < cols - 1), ("d", -1, c >= 1)):
            block = c - move * (step - 1)
            valid = edge & (block >= 0) & (block <= cols - 1)
            source = first if first is not None else buf.at[rows(block), columns]
            copies.start(
                f"{tag}{word}{step}", source, buf.at[rows(block), columns], {"col": c + move}, valid
            )

    def chain_wait(tag, step):
        copies.came(f"{tag}u{step}", c >= step)
        copies.came(f"{tag}d{step}", c + step <= cols - 1)

    def row_send(name, s):
        b = col_of[s]
        copies.start(name, X.at[rows(b), own], X.at[rows(b), other], y_dev)

    q2 = q + 2 - 4 * hi

    def weight(name, source, full, row0, size, columns, spread):
        share = q if spread else k

        def place(index):
            return full.at[at(row0 + index * size, size), columns]

        copies.start(f"{name}y", source(at(share * size, size)), place(share), y_dev)

        def pass_on():
            copies.came(f"{name}y")
            if spread:
                copies.start(f"{name}x", place(q), place(q), x_dev)
            copies.start(f"{name}c", place(share), place(share), core_dev)

        def pass_far():
            copies.came(f"{name}x")
            copies.start(f"{name}f", place(q2), place(q2), core_dev)

        def done():
            copies.came(f"{name}c")
            if spread:
                copies.came(f"{name}f")

        return pass_on, pass_far, done

    everything = slice(None)
    chain_send("x", 1, X, own, hid)
    copies.start("xy0", hid, X.at[rows(c), other], y_dev)
    for j, vector in enumerate((gain1, bias1, gain2, bias2)):
        NV[j : j + 1, own] = row_of(vector[...])
    NV[4:8, own] = jnp.zeros((4, wid), F32)
    copies.start("nv", NV.at[:, own], NV.at[:, other], y_dev)
    wu_on, wu_far, wu_done = weight(
        "wu", lambda rs: wu.at[rs, at((1 - r) * units, units)], WU, wid, wid // 4, everything, True
    )

    seg_row = seg[...].astype(F32)
    seg_col = jnp.transpose(jnp.broadcast_to(seg_row, (128, rows_all)))
    STAT[:, 3:4] = seg_col[:, 0:1]

    def table(i):
        block = at(i * blk, blk)
        starts = jnp.sum(
            (seg_row < STAT[block, 3:4]).astype(F32), axis=1, keepdims=True
        )
        index = lax.broadcasted_iota(jnp.int32, (blk, 1), 0) + i * blk
        lane = lax.broadcasted_iota(jnp.int32, (1, 128), 1)
        turn = jnp.exp(
            lax.rem(lane, ROT // 2).astype(F32) * (-2.0 * math.log(rope_base) / ROT)
        )
        angles = (index.astype(F32) - starts) * turn
        COS[block, :] = jnp.where(lane < ROT, jnp.cos(angles), 1.0)
        SIN[block, :] = jnp.where(
            lane < ROT // 2, -jnp.sin(angles), jnp.where(lane < ROT, jnp.sin(angles), 0.0)
        )

    tiles(cols, table)

    def rotate(head, block, sign):
        first = head[:, :128]
        lane = lax.broadcasted_iota(jnp.int32, first.shape, 1)
        swapped = jnp.where(
            lane < ROT // 2, pltpu.roll(first, 128 - ROT // 2, 1), pltpu.roll(first, ROT // 2, 1)
        )
        turned = first * COS[block, :] + sign * (swapped * SIN[block, :])
        return jnp.concatenate([turned, head[:, 128:]], axis=1)

    sub = 64

    def norm_block(b):
        def part(i):
            rs = at(b * blk + i * sub, sub)
            x = X[rs, :].astype(F32)
            mean = jnp.sum(x, axis=1, keepdims=True) * (1.0 / width)
            square = jnp.sum(x * x, axis=1, keepdims=True) * (1.0 / width)
            inv = lax.rsqrt(square - mean * mean + eps_norm)
            STAT[rs, 0:1] = mean
            STAT[rs, 1:2] = inv
            normal = (x - mean) * inv
            OUTP[rs, :] = (normal * NV[0:1, :] + NV[1:2, :]).astype(BF16)
            N[rs, :] = (normal * NV[2:3, :] + NV[3:4, :]).astype(BF16)

        tiles(blk // sub, part)

    def up_block(b):
        def part(j):
            cs = at(j * TILE, TILE)
            bias = row_of(up_b[at(r * units + j * TILE, TILE)])
            up = dot(N[rows(b), :], WU[:, cs], NN) + bias
            cdf = 0.5 * (1.0 + lax.erf(up * (1.0 / math.sqrt(2.0))))
            HID[rows(b), cs] = (up * cdf).astype(BF16)
            SLOPE[rows(b), cs] = (
                cdf + up * jnp.exp(-0.5 * up * up) * (1.0 / math.sqrt(2.0 * math.pi))
            ).astype(BF16)

        tiles(units // TILE, part)

    fetch_c.wait()
    fetch_x.wait()
    fetch_g.wait()
    chain_wait("x", 1)
    chain_send("x", 2, X, own)
    row_send("xy1", 1)
    chain_wait("x", 2)
    chain_send("x", 3, X, own)
    row_send("xy2", 2)
    chain_send("g", 1, G, own, cot)
    wu_on()
    copies.came("nv")
    copies.came("xy0")
    norm_block(col_of[0])
    chain_wait("x", 3)
    row_send("xy3", 3)
    copies.start("gy", cot, G.at[rows(c), other], y_dev)
    wq_on, _, wq_done = weight(
        "wq", lambda rs: wq.at[rs, at((1 - r) * heads, heads)], WQ, wid, wid // 2, everything, False
    )

    def rows_of(ref, start, rs):
        return ref.at[at(start + rs.start, rs.size), :]

    wn_on, _, wn_done = weight(
        "wn", lambda rs: rows_of(wn, (1 - r) * units, rs), WN, 0, units // 2, other, False
    )
    wd_on, _, wd_done = weight(
        "wd", lambda rs: rows_of(wd, (1 - r) * HD, rs), WD, 0, HD // 2, other, False
    )
    wu_far()
    copies.came("xy1")
    norm_block(col_of[1])
    fetch_u.wait()
    wu_done()
    up_block(col_of[0])
    up_block(col_of[1])
    chain_wait("g", 1)
    chain_send("g", 2, G, own)
    copies.came("xy2")
    norm_block(col_of[2])
    up_block(col_of[2])
    chain_wait("g", 2)
    chain_send("g", 3, G, own)
    copies.came("xy3")
    norm_block(col_of[3])
    up_block(col_of[3])
    copies.came("gy")
    chain_send("h", 1, G, other)

    def grad_send(name, staged, left, right, n_rows, n_cols, target):
        def part(i):
            cs = at(i * TILE, TILE)
            staged[:, cs] = dot(left(None), right(cs), TN).astype(BF16)

        tiles(n_cols // TILE, part)
        copies.start(name, staged, target, core_dev)

    hid_keep, hid_send = at(k * uh, uh), at((1 - k) * uh, uh)
    att_keep, att_send = at(k * dh, dh), at((1 - k) * dh, dh)

    def out_grad(name, side, left_ref, keep, give, staged, landing):
        base = side * wid

        def give_part(i):
            cs = at(i * TILE, TILE)
            staged[:, cs] = dot(
                left_ref[:, give], G[:, at(base + i * TILE, TILE)], TN
            ).astype(BF16)

        tiles(wid // TILE, give_part)
        copies.start(f"{name}a", staged, landing, core_dev)

    def out_keep(name, side, left_ref, keep, landing):
        base = side * wid
        copies.came(f"{name}a")

        def keep_part(i):
            cs = at(i * TILE, TILE)
            mine = dot(left_ref[:, keep], G[:, at(base + i * TILE, TILE)], TN)
            landing[:, cs] = (mine + landing[:, cs].astype(F32)).astype(BF16)

        tiles(wid // TILE, keep_part)

    halves = {}

    def cross(name, total, n_rows, landing):
        half_rows = n_rows // 2
        give, keep = at((1 - hi) * half_rows, half_rows), at(hi * half_rows, half_rows)
        copies.start(f"{name}x", total.at[give, :], landing, x_dev)
        halves[name] = (total.at[keep, :], landing)

    def crossed(name, target):
        mine, landing = halves[name]
        copies.came(f"{name}x")
        n = landing.shape[0]
        step = min(n, 128)

        def part(i):
            rs = at(i * step, step)
            landing[rs, :] = (mine[rs, :].astype(F32) + landing[rs, :].astype(F32)).astype(BF16)

        tiles(n // step, part)
        copies.start(f"{name}y", landing, target, y_dev)

    def spread_out(name, came, result, here):
        copies.came(f"{name}y")
        copies.start(f"{name}g", came, result.at[here], x_dev)
        copies.start(f"{name}t", came, result.at[here], core_dev)
        fetch(came, result.at[here])

    def pass_quarter(name, result, there):
        copies.came(f"{name}g")
        copies.start(f"{name}f", result.at[there], result.at[there], core_dev)

    def finish(name, total, came, result, here):
        copies.came(f"{name}x")
        n = total.shape[0]
        step = min(n, 128)

        def part(i):
            rs = at(i * step, step)
            came[rs, :] = (total[rs, :].astype(F32) + came[rs, :].astype(F32)).astype(BF16)

        tiles(n // step, part)
        copies.start(f"{name}t", came, result.at[here], core_dev)
        fetch(came, result.at[here])

    wide = slice(None)

    def down_at(side, part=None):
        start, n = side * units + k * uh, uh
        if part is not None:
            start, n = start + part * (uh // 2), uh // 2
        return (at(start, n), wide)

    def dense_at(side, part=None):
        start, n = side * HD + k * dh, dh
        if part is not None:
            start, n = start + part * (dh // 2), dh // 2
        return (at(start, n), wide)

    def up_at(side, part=None):
        taken = wide if part is None else at(part * (wid // 2), wid // 2)
        return (taken, at(side * units + k * uh, uh))

    def qkv_at(side, part=None):
        taken = wide if part is None else at(part * (wid // 2), wid // 2)
        return (taken, at(side * heads + k * hh, hh))

    chain_wait("g", 3)
    out_grad("dn0", 0, HID, hid_keep, hid_send, DUP.at[pl.ds(0, uh), :], S_dn.at[0])
    out_keep("dn0", 0, HID, hid_keep, S_dn.at[0])
    copies.start("dn0x", S_dn.at[0], X_dn, x_dev)

    chain_wait("h", 1)
    chain_send("h", 2, G, other)
    fetch_q.wait()
    wq_on()
    wq_done()

    def qkv_block(i):
        block = at(i * blk, blk)
        for j in range(3):
            bias = row_of(qkv_b[at(r * heads + j * HD, HD)])
            value = dot(OUTP[block, :], WQ[:, j * HD : (j + 1) * HD], NN) + bias
            if j < 2:
                value = rotate(value, block, 1.0)
            QKV[block, j * HD : (j + 1) * HD] = value.astype(BF16)

    tiles(cols, qkv_block)
    chain_wait("h", 2)
    chain_send("h", 3, G, other)

    def key_range(i):
        low = max(0, i - 2) * blk
        return slice(i * blk, (i + 1) * blk), slice(low, (i + 1) * blk), low

    def block_scores(i):
        mine, span, low = key_range(i)
        n = span.stop - low
        s = dot(QKV[mine, 0:HD], QKV[span, HD : 2 * HD], NT) * scale
        row_id = lax.broadcasted_iota(jnp.int32, (blk, n), 0) + i * blk
        col_id = lax.broadcasted_iota(jnp.int32, (blk, n), 1) + low
        same = STAT[mine, 3:4] == seg_row[:, span]
        return jnp.where(same & (col_id <= row_id), s, -1e30)

    for i in range(cols):
        mine, span, low = key_range(i)
        s = block_scores(i)
        largest = jnp.max(s, axis=1, keepdims=True)
        p = jnp.exp(s - largest)
        total = jnp.sum(p, axis=1, keepdims=True)
        STAT[mine, 2:3] = largest + jnp.log(total)
        p_low = (p / total).astype(BF16)
        ATT[mine, :] = dot(p_low, QKV[span, 2 * HD :], NN).astype(BF16)
    out_grad("de0", 0, ATT, att_keep, att_send, A_de.at[0], S_de.at[0])
    fetch_n.wait()
    fetch_d.wait()

    def branch_block(b, side):
        def part(j):
            cs = at(side * wid + j * TILE, TILE)
            both = dot(ATT[rows(b), :], WD[:, cs], NN) + dot(HID[rows(b), :], WN[:, cs], NN)
            OUTP[rows(b), cs] = both.astype(BF16)

        tiles(wid // TILE, part)

    branch_block(col_of[2], 0)
    out_keep("de0", 0, ATT, att_keep, S_de.at[0])
    copies.start("de0x", S_de.at[0], X_de, x_dev)
    for s in (3, 1, 0):
        branch_block(col_of[s], 0)

    chain_wait("h", 3)
    copies.start("oa1", OUTP.at[rows(col_of[1]), own], OZ1.at[:, own], {"col": col_of[1]})
    out_grad("dn1", 1, HID, hid_keep, hid_send, DUP.at[pl.ds(uh, uh), :], S_dn.at[1])
    out_grad("de1", 1, ATT, att_keep, att_send, A_de.at[1], S_de.at[1])
    wn_on()
    out_keep("dn1", 1, HID, hid_keep, S_dn.at[1])
    cross("dn1", S_dn.at[1], uh, V_dn)
    out_keep("de1", 1, ATT, att_keep, S_de.at[1])
    cross("de1", S_de.at[1], dh, V_de)
    wn_done()
    copies.start("oa2", OUTP.at[rows(col_of[2]), own], OZ2.at[:, own], {"col": col_of[2]})
    wd_on()

    copies.sent("dn0a", "dn1a")

    def up_grad_part(i):
        block = at(i * blk, blk)
        for j in range(units // TILE):
            cs = slice(j * TILE, (j + 1) * TILE)
            back = dot(G[block, :], WN[cs, :], NT)
            DUP[block, cs] = (back * SLOPE[block, cs].astype(F32)).astype(BF16)

    tiles(cols, up_grad_part)
    keep_u, give_u = at(k * uh, uh), at((1 - k) * uh, uh)
    keep_h, give_h = at(k * hh, hh), at((1 - k) * hh, hh)

    def in_give(name, side, right_ref, give, staged, landing):
        def part(i):
            rs = at(i * TILE, TILE)
            lefts = N[:, at(side * wid + i * TILE, TILE)]
            staged[rs, :] = dot(lefts, right_ref[:, give], TN).astype(BF16)

        tiles(wid // TILE, part)
        copies.start(f"{name}{side}a", staged, landing.at[side], core_dev)

    def in_keep(name, side, right_ref, keep, landing):
        copies.came(f"{name}{side}a")

        def part(i):
            rs = at(i * TILE, TILE)
            mine = dot(N[:, at(side * wid + i * TILE, TILE)], right_ref[:, keep], TN)
            landing[side, rs, :] = (mine + landing[side, rs, :].astype(F32)).astype(BF16)

        tiles(wid // TILE, part)

    wd_done()
    branch_block(col_of[3], 1)
    copies.start("oy3", OUTP.at[rows(col_of[3]), other], OY.at[1], y_dev)
    in_give("up", 1, DUP, give_u, SLOPE.at[:, pl.ds(uh, uh)], S_up)
    for i in range(cols):
        mine = slice(i * blk, (i + 1) * blk)
        DAT[mine, :] = dot(G[mine, :], WD[...], NT).astype(BF16)
    BQ[q, 2:3, :] = jnp.sum(G[:, own].astype(F32), axis=0, keepdims=True)

    copies.sent(*[f"{t}{w}{s}" for t in "gh" for w in "ud" for s in (1, 2, 3)])
    pl.semaphore_signal(credit.at[0], inc=1, device_id=x_dev, device_id_type=MESH)
    pl.semaphore_signal(credit.at[1], inc=1, device_id=y_dev, device_id_type=MESH)
    X_up, low, high = G.at[:, pl.ds(0, uh)], pl.ds(0, wid // 2), pl.ds(wid // 2, wid // 2)
    V_up, R_up = G.at[low, pl.ds(uh, uh)], G.at[high, pl.ds(uh, uh)]
    X_qk = WN.at[:, pl.ds(0, hh)]
    V_qk, R_qk = WN.at[low, pl.ds(hh, hh)], WN.at[high, pl.ds(hh, hh)]

    in_keep("up", 1, DUP, keep_u, S_up)
    pl.semaphore_wait(credit.at[0], 1)
    cross("up1", S_up.at[1], wid, V_up)
    crossed("dn1", R_dn)
    in_give("up", 0, DUP, give_u, SLOPE.at[:, pl.ds(0, uh)], S_up)
    branch_block(col_of[2], 1)
    copies.start("ob2", OUTP.at[rows(col_of[2]), other], OZ2.at[:, other], {"col": col_of[2]})
    in_keep("up", 0, DUP, keep_u, S_up)
    copies.start("up0x", S_up.at[0], X_up, x_dev)

    branch_block(col_of[1], 1)
    copies.start("ob1", OUTP.at[rows(col_of[1]), other], OZ1.at[:, other], {"col": col_of[1]})
    branch_block(col_of[0], 1)
    crossed("de1", R_de)
    copies.sent("wnc")
    pl.semaphore_signal(credit.at[2], inc=1, device_id=x_dev, device_id_type=MESH)
    pl.semaphore_signal(credit.at[3], inc=1, device_id=y_dev, device_id_type=MESH)
    pl.semaphore_signal(credit.at[4], inc=1, device_id=y_dev, device_id_type=MESH)

    def out_block():
        b = col_of[3]
        copies.came("oy3")

        def part(i):
            rs = at(b * blk + i * sub, sub)
            came = OY[1, at(i * sub, sub), :]
            OUTP[rs, own] = (OUTP[rs, own].astype(F32) + came.astype(F32)).astype(BF16)

        tiles(blk // sub, part)
        copies.start("oz3", OUTP.at[rows(b), own], OZ3, {"col": b})

    def again(i):
        rs = at(i * sub, sub)
        normal = (X[rs, :].astype(F32) - STAT[rs, 0:1]) * STAT[rs, 1:2]
        N[rs, :] = (normal * NV[0:1, :] + NV[1:2, :]).astype(BF16)

    tiles(rows_all // sub, again)
    TMP[...] = jnp.zeros_like(TMP)
    for i in range(cols):
        mine, span, low = key_range(i)
        query = QKV[mine, 0:HD]
        p = jnp.exp(block_scores(i) - STAT[mine, 2:3])
        d_p = dot(DAT[mine, :], QKV[span, 2 * HD :], NT)
        delta = jnp.sum(d_p * p, axis=1, keepdims=True)
        d_s = (p * (d_p - delta)).astype(BF16)
        p_low = p.astype(BF16)
        d_query = dot(d_s, QKV[span, HD : 2 * HD], NN) * scale
        QKV[mine, 0:HD] = rotate(d_query, mine, -1.0).astype(BF16)
        for j in range(low // blk, i + 1):
            js = slice(j * blk - low, (j + 1) * blk - low)
            ks, vs = slice(j * HD, (j + 1) * HD), slice((cols + j) * HD, (cols + j + 1) * HD)
            TMP[:, ks] += dot(d_s[:, js], query, TN)
            TMP[:, vs] += dot(p_low[:, js], DAT[mine, :], TN)
    for j in range(cols):
        mine = slice(j * blk, (j + 1) * blk)
        ks, vs = slice(j * HD, (j + 1) * HD), slice((cols + j) * HD, (cols + j + 1) * HD)
        QKV[mine, HD : 2 * HD] = rotate(TMP[:, ks] * scale, mine, -1.0).astype(BF16)
        QKV[mine, 2 * HD :] = TMP[:, vs].astype(BF16)

    copies.sent("up0a", "up1a")
    in_give("qk", 1, QKV, give_h, SLOPE.at[:, pl.ds(hh, hh)], S_qk)
    in_give("qk", 0, QKV, give_h, SLOPE.at[:, pl.ds(0, hh)], S_qk)
    pl.semaphore_wait(credit.at[1], 1)
    crossed("up1", R_up)
    in_keep("qk", 1, QKV, keep_h, S_qk)
    pl.semaphore_wait(credit.at[2], 1)
    cross("qk1", S_qk.at[1], wid, V_qk)
    in_keep("qk", 0, QKV, keep_h, S_qk)
    copies.start("qk0x", S_qk.at[0], X_qk, x_dev)

    def gather_dp(name, slots):
        for word, device in (("c", core_dev), ("x", x_dev), ("d", far_dev)):
            copies.start(f"{name}{word}", slots.at[q], slots.at[q], device)

    def gathered_dp(name, slots):
        for word in "cxd":
            copies.came(f"{name}{word}")
        return slots[0] + slots[1] + slots[2] + slots[3]

    BQ[q, 0:1, :] = jnp.sum(DUP[...].astype(F32), axis=0, keepdims=True)
    BQ[q, 1:2, 0:heads] = jnp.sum(QKV[...].astype(F32), axis=0, keepdims=True)
    BQ[q, 1:2, heads:] = jnp.zeros((1, wid - heads), F32)
    BQ[q, 3:8, :] = jnp.zeros((5, wid), F32)
    gather_dp("b", BQ)

    NSUM[...] = jnp.zeros_like(NSUM)
    pl.semaphore_wait(credit.at[4], 1)

    def norm_back(b):
        rb = rows(b)
        mean, inv = STAT[rb, 0:1], STAT[rb, 1:2]

        def first(j, carry):
            along, plain = carry
            cs = at(j * TILE, TILE)
            one = dot(QKV[rb, :], WQ[cs, :], NT)
            two = dot(DUP[rb, :], WU[cs, :], NT)
            normal = (X[rb, cs].astype(F32) - mean) * inv
            NSUM[0:1, cs] += jnp.sum(one * normal, axis=0, keepdims=True)
            NSUM[1:2, cs] += jnp.sum(one, axis=0, keepdims=True)
            NSUM[2:3, cs] += jnp.sum(two * normal, axis=0, keepdims=True)
            NSUM[3:4, cs] += jnp.sum(two, axis=0, keepdims=True)
            grad = one * NV[0:1, cs] + two * NV[2:3, cs]
            TMP[:, cs] = grad
            along = along + jnp.sum(grad * normal, axis=1, keepdims=True)
            plain = plain + jnp.sum(grad, axis=1, keepdims=True)
            return along, plain

        zero = jnp.zeros((blk, 1), F32)
        along, plain = lax.fori_loop(0, width // TILE, first, (zero, zero))
        along, plain = along * (1.0 / width), plain * (1.0 / width)

        def second(j):
            cs = at(j * TILE, TILE)
            normal = (X[rb, cs].astype(F32) - mean) * inv
            N[rb, cs] = (inv * (TMP[:, cs] - plain - normal * along)).astype(BF16)

        tiles(width // TILE, second)

    EY = [HID.at[pl.ds(j * blk, blk), :] for j in range(3)]
    pl.semaphore_wait(credit.at[3], 1)
    for s in (2, 3):
        norm_back(col_of[s])
        copies.start(f"ey{s}", N.at[rows(col_of[s]), other], EY[s - 1], y_dev)
        if s == 2:
            out_block()
            spread_out("dn1", R_dn, g_down, down_at(1 - r, hi))
        else:
            spread_out("de1", R_de, g_dense, dense_at(1 - r, hi))
    norm_back(col_of[1])
    copies.start(
        "ezb", N.at[rows(col_of[1]), other], DZ1.at[:, other], {"col": col_of[1]}
    )
    norm_back(col_of[0])
    SMO[0:4, :] = NSUM[0:4, other]
    copies.start("sy", SMO, SMR, y_dev)

    def mine_at(i):
        return at(c * blk + i * sub, sub)

    def row_rest(buf, names, whole, landing, name):
        for arrival in names:
            copies.came(arrival)

        def part(i):
            rs = at(i * sub, sub)
            total = buf[mine_at(i), other].astype(F32)
            for ref in whole:
                total = total + ref[rs, other].astype(F32)
            buf[mine_at(i), other] = total.astype(BF16)

        tiles(blk // sub, part)
        copies.start(name, buf.at[rows(c), other], landing, y_dev)

    def total_of(i, buf, whole, parts):
        rs = at(i * sub, sub)
        total = buf[mine_at(i), own].astype(F32)
        for ref in whole:
            total = total + ref[rs, own].astype(F32)
        for ref in parts:
            total = total + ref[rs, :].astype(F32)
        return total

    at_end, between = lax.rem(c, 3) == 0, lax.rem(c, 3) != 0

    def x_block(s):
        b = col_of[s]
        copies.came(f"ey{s}")

        def part(i):
            rs = at(b * blk + i * sub, sub)
            came = EY[s - 1][at(i * sub, sub), :]
            N[rs, own] = (N[rs, own].astype(F32) + came.astype(F32)).astype(BF16)

        tiles(blk // sub, part)
        copies.start(
            f"ea{s}", N.at[rows(b), own], DZ.at[s - 2], {"col": col_of[1]}, at_end
        )

    def x_pass(s):
        b = col_of[s]
        copies.came(f"ea{5 - s}", between)

        @pl.when(between)
        def _():
            def part(i):
                rs = at(b * blk + i * sub, sub)
                came = DZ[3 - s, at(i * sub, sub), :]
                N[rs, own] = (N[rs, own].astype(F32) + came.astype(F32)).astype(BF16)

            tiles(blk // sub, part)

        copies.start(f"eb{s}", N.at[rows(b), own], DZ.at[2], {"col": b}, between)

    row_rest(OUTP, ("oa1", "oa2", "ob1", "ob2"), (OZ1, OZ2), OY.at[0], "oy0")
    spread_out("up1", R_up, g_up, up_at(1 - r, hi))
    finish("dn0", S_dn.at[0], X_dn, g_down, down_at(r))
    finish("de0", S_de.at[0], X_de, g_dense, dense_at(r))
    finish("up0", S_up.at[0], X_up, g_up, up_at(r))
    crossed("qk1", R_qk)
    x_block(2)
    copies.came("sy")
    NZ[c, 0:4, :] = NSUM[0:4, own] + SMR[0:4, :]
    for s in (1, 2, 3):
        copies.start(f"sz{s}", NZ.at[c], NZ.at[c], {"col": col_of[s]})
    x_block(3)
    copies.start("eza", N.at[rows(col_of[1]), own], DZ1.at[:, own], {"col": col_of[1]})
    BS[...] = gathered_dp("b", BQ)
    copies.start("by", BS, BR, y_dev)
    row_rest(N, ("ezb",), (DZ1,), EY[0], "ey0")
    x_pass(3)
    finish("qk0", S_qk.at[0], X_qk, g_qkv, qkv_at(r))
    pass_quarter("dn1", g_down, down_at(1 - r, 1 - hi))
    x_pass(2)
    for s in (1, 2, 3):
        copies.came(f"sz{s}")
    NQ[q] = NZ[0] + NZ[1] + NZ[2] + NZ[3]
    gather_dp("n", NQ)
    pass_quarter("de1", g_dense, dense_at(1 - r, 1 - hi))
    spread_out("qk1", R_qk, g_qkv, qkv_at(1 - r, hi))
    for name in ("oz3", "oy0"):
        copies.came(name)

    def out_last(i):
        total = total_of(i, OUTP, (OZ1, OZ2), (OZ3, OY.at[0]))
        total = total + X[mine_at(i), own].astype(F32)
        out[at(i * sub, sub), :] = (total + row_of(dense_b[...] + down_b[...])).astype(BF16)

    tiles(blk // sub, out_last)
    pass_quarter("up1", g_up, up_at(1 - r, 1 - hi))
    copies.came("by")
    small[0:8, :] = BS[...]
    small[8:16, :] = BR[...]
    small[4:8, :] = gathered_dp("n", NQ)[0:4]
    copies.came("eza")
    copies.came("eb2", at_end)
    copies.came("eb3", between)
    copies.came("ey0")

    def x_last(i):
        total = total_of(i, N, (DZ1,), (DZ.at[2], EY[0]))
        in_grad[at(i * sub, sub), :] = COT[at(i * sub, sub), :].astype(F32) + total

    tiles(blk // sub, x_last)
    pass_quarter("qk1", g_qkv, qkv_at(1 - r, 1 - hi))
    for name in ("dn0", "de0", "up0", "qk0"):
        copies.came(f"{name}t")
    for name in ("dn1", "de1", "up1", "qk1"):
        copies.came(f"{name}t")
        copies.came(f"{name}f")
    for copy in local[7:]:
        copy.wait()
    copies.sent_all()


def scratch(blk, wid, cols, units, heads):
    tokens, width = blk * cols, 2 * wid
    low = [
        (tokens, width), (tokens, width), (width, heads), (width, units), (HD, width),
        (units, width), (tokens, width),
    ]
    V = pltpu.VMEM
    return (
        [V(shape, BF16) for shape in low]
        + [V((tokens, 128), F32)]
        + [
            V(shape, BF16)
            for shape in (
                (tokens, heads), (tokens, HD), (tokens, units), (tokens, units), (tokens, units),
                (tokens, HD), (tokens, width), (blk, width), (blk, width), (blk, wid),
                (2, blk, wid), (blk, width), (3, blk, wid), (blk, wid),
                (2, units // 2, wid), (2, HD // 2, wid), (2, wid, units // 2), (2, wid, heads // 2),
                (units // 4, wid), (HD // 4, wid), (units // 4, wid), (HD // 4, wid),
                (units // 2, wid), (HD // 2, wid), (2, HD // 2, wid),
            )
        ]
        + [
            V((blk, width), F32),
            V((8, width), F32),
            V((tokens, 128), F32),
            V((tokens, 128), F32),
            V((8, width), F32),
            V((8, wid), F32),
            V((8, wid), F32),
            V((cols, 8, wid), F32),
            V((4, 8, wid), F32),
            V((4, 8, wid), F32),
            V((8, wid), F32),
            V((8, wid), F32),
            pltpu.SemaphoreType.DMA((120,)),
            pltpu.SemaphoreType.DMA((120,)),
            pltpu.SemaphoreType.DMA((20,)),
            pltpu.SemaphoreType.REGULAR((5,)),
        ]
    )


def widen_kernel(*refs):
    given, results = refs[:7], refs[7:]
    small = given[6]
    for source, target in zip(given[:6], results[:6]):
        target[...] = source[...].astype(target.dtype)

    @pl.when(pl.program_id(0) == 0)
    def _():
        gain1, bias1, gain2, bias2, qkv_sum, dense_sum, up_sum, down_sum = results[6:]
        for j, ref in enumerate((gain1, bias1, gain2, bias2)):
            ref[...] = small[4 + j]
        dense_sum[...] = small[2]
        down_sum[...] = small[2]
        r = lax.axis_index("row")
        for ref, index in ((up_sum, 0), (qkv_sum, 1)):
            n = ref.shape[0] // 2
            ref[at(r * n, n)] = small[index, 0:n]
            ref[at((1 - r) * n, n)] = small[8 + index, 0:n]


def swap(value, axis, mask):
    size = lax.axis_size(axis)
    return lax.ppermute(value, axis, [(i, i ^ mask) for i in range(size)])


def shards(
    hidden_in,
    segment,
    norm1_gain,
    norm1_bias,
    norm2_gain,
    norm2_bias,
    qkv_weight,
    qkv_bias,
    dense_weight,
    dense_bias,
    up_weight,
    up_bias,
    down_weight,
    down_bias,
    cotangent,
):
    blk, wid = hidden_in.shape
    cols = lax.axis_size("col")
    heads, units = qkv_weight.shape[1] // 2, up_weight.shape[1] // 2
    vectors = (
        norm1_gain, norm1_bias, norm2_gain, norm2_bias, qkv_bias, up_bias, dense_bias, down_bias,
    )
    vmem = pl.BlockSpec(memory_space=pltpu.VMEM)
    far = pl.BlockSpec(memory_space=pl.ANY)
    shape = jax.ShapeDtypeStruct
    out, in_grad, small, g_qkv, g_dense, g_up, g_down = pl.pallas_call(
        functools.partial(step_kernel, (blk, wid, cols)),
        out_shape=(
            shape((blk, wid), BF16),
            shape((blk, wid), F32),
            shape((16, wid), F32),
            shape(qkv_weight.shape, BF16),
            shape(dense_weight.shape, BF16),
            shape(up_weight.shape, BF16),
            shape(down_weight.shape, BF16),
        ),
        in_specs=[far] * 6 + [vmem] * 9,
        out_specs=(vmem,) * 3 + (far,) * 4,
        scratch_shapes=scratch(blk, wid, cols, units, heads),
        compiler_params=pltpu.CompilerParams(
            collective_id=0, has_side_effects=True, vmem_limit_bytes=67043328
        ),
        name="step",
    )(
        hidden_in, cotangent, qkv_weight, up_weight, dense_weight, down_weight, segment, *vectors
    )

    grads = (g_qkv, g_dense, g_up, g_down)
    mask = 4
    while mask < lax.axis_size("dp"):
        grads = tuple(
            (g.astype(F32) + swap(g, "dp", mask).astype(F32)).astype(BF16) for g in grads
        )
        small = small + swap(small, "dp", mask)
        mask *= 2
    steps = 4

    def cut(array):
        rows, columns = array.shape
        return pl.BlockSpec((rows // steps, columns), lambda i: (i, 0))

    def whole(n):
        return pl.BlockSpec((n,), lambda i: (0,))

    lengths = [wid] * 4 + [2 * heads, wid, 2 * units, wid]
    widened = pl.pallas_call(
        widen_kernel,
        grid=(steps,),
        out_shape=[shape(out.shape, BF16), shape(in_grad.shape, F32)]
        + [shape(g.shape, F32) for g in grads]
        + [shape((n,), F32) for n in lengths],
        in_specs=[cut(out), cut(in_grad)]
        + [cut(g) for g in grads]
        + [pl.BlockSpec(small.shape, lambda i: (0, 0))],
        out_specs=[cut(out), cut(in_grad)] + [cut(g) for g in grads] + [whole(n) for n in lengths],
        compiler_params=pltpu.CompilerParams(vmem_limit_bytes=60 << 20),
        name="widen",
    )(out, in_grad, *grads, small)
    out, in_grad, d_qkv, d_dense, d_up, d_down, *sums = widened
    return (
        out,
        in_grad,
        sums[0],
        sums[1],
        sums[2],
        sums[3],
        d_qkv,
        sums[4],
        d_dense,
        sums[5],
        d_up,
        sums[6],
        d_down,
        sums[7],
    )


def solution(mesh):
    return jax.shard_map(
        shards,
        mesh=mesh,
        in_specs=(
            P(("dp", "col"), "row"),
            P("dp", None),
            P("row"),
            P("row"),
            P("row"),
            P("row"),
            P("row", "col"),
            P("col"),
            P("col", "row"),
            P("row"),
            P("row", "col"),
            P("col"),
            P("col", "row"),
            P("row"),
            P(("dp", "col"), "row"),
        ),
        out_specs=(
            P(("dp", "col"), "row"),
            P(("dp", "col"), "row"),
            P("row"),
            P("row"),
            P("row"),
            P("row"),
            P("row", "col"),
            P("col"),
            P("col", "row"),
            P("row"),
            P("row", "col"),
            P("col"),
            P("col", "row"),
            P("row"),
        ),
        check_vma=False,
    )
```

```python
import functools
import math

import jax
import jax.numpy as jnp
from jax import lax
from jax.experimental import pallas as pl
from jax.experimental.pallas import tpu as pltpu
from jax.sharding import PartitionSpec as P

HD = 256
ROT = 64
F32 = jnp.float32
BF16 = jnp.bfloat16
MESH = pl.DeviceIdType.MESH

eps_norm = 1e-05
rope_base = 10000.0
TILE = 512
NN = (((1,), (0,)), ((), ()))
NT = (((1,), (1,)), ((), ()))
TN = (((0,), (0,)), ((), ()))


def dot(left, right, dims):
    return lax.dot_general(left, right, dims, preferred_element_type=F32)


class Copies:
    def __init__(self, send_sem, recv_sem):
        self.send_sem, self.recv_sem = send_sem, recv_sem
        self.made, self.open = {}, {}

    def start(self, name, source, target, device, when=None):
        index = len(self.made)
        copy = pltpu.make_async_remote_copy(
            src_ref=source,
            dst_ref=target,
            send_sem=self.send_sem.at[index],
            recv_sem=self.recv_sem.at[index],
            device_id=device,
            device_id_type=MESH,
        )
        self.made[name] = copy
        self.open[name] = when
        guarded(when, copy.start)

    def came(self, name, when=None):
        guarded(when, self.made[name].wait_recv)

    def sent(self, *names):
        for name in names:
            guarded(self.open.pop(name), self.made[name].wait_send)

    def sent_all(self):
        self.sent(*list(self.open))


def guarded(when, action):
    if when is None:
        action()
    else:
        pl.when(when)(action)


def row_of(vector):
    return vector.reshape(1, vector.shape[0])


def at(start, size):
    return pl.ds(pl.multiple_of(start, size), size)


def tiles(count, body):
    lax.fori_loop(0, count, lambda i, carry: (body(i), carry)[1], 0)


def step_kernel(
    sizes,
    hid, cot, wq, wu, wd, wn, seg, gain1, bias1, gain2, bias2, qkv_b, up_b, dense_b, down_b,
    out_hbm, in_grad_hbm, small_hbm, g_qkv, g_dense, g_up, g_down,
    out, in_grad, small, X, G, WQ, WU, WD, WN, N, STAT, QKV, ATT, HID, SLOPE, DUP, DAT, OUTP, OZ1, OZ2, OZ3, OY, DZ1, DZ, COT,
    S_dn, S_de, S_up, S_qk, R_dn, R_de, V_dn, V_de, X_dn, X_de, A_de, TMP, NV, COS, SIN, NSUM, SMO, SMR, NZ, NQ, BQ, BS, BR,
    send_sem, recv_sem, local_sem, credit,
):
    blk, wid, cols = sizes
    rows_all = blk * cols
    width = 2 * wid
    heads, units = WQ.shape[1], WU.shape[1]
    hh, uh, dh = heads // 2, units // 2, HD // 2
    r = lax.axis_index("row")
    c = lax.axis_index("col")
    dp = lax.axis_index("dp")
    k = lax.rem(dp, 2)
    hi = lax.rem(lax.div(dp, 2), 2)
    q = k + 2 * hi
    core_dev = {"dp": dp + 1 - 2 * k}
    x_dev = {"dp": dp + 2 - 4 * hi}
    far_dev = {"dp": dp + 3 - 2 * k - 4 * hi}
    y_dev = {"row": 1 - r}
    c_low, c_high = lax.rem(c, 2), lax.div(c, 2)
    col_of = [c, c + 1 - 2 * c_low, c + 2 - 4 * c_high, 3 - c]
    own, other = pl.ds(0, wid), pl.ds(wid, wid)
    scale = 1.0 / math.sqrt(HD)
    copies = Copies(send_sem, recv_sem)

    barrier = pltpu.get_barrier_semaphore()
    for device in (core_dev, x_dev, y_dev):
        pl.semaphore_signal(barrier, inc=1, device_id=device, device_id_type=MESH)
    for move, inside in ((1, c < cols - 1), (-1, c >= 1)):

        @pl.when(inside)
        def _():
            pl.semaphore_signal(
                barrier, inc=1, device_id={"col": c + move}, device_id_type=MESH
            )

    local = []

    def fetch(source, target):
        copy = pltpu.make_async_copy(source, target, local_sem.at[len(local)])
        copy.start()
        local.append(copy)
        return copy

    fetch_c = fetch(cot, COT)
    fetch_x = fetch(hid, X.at[at(c * blk, blk), own])
    fetch_g = fetch(cot, G.at[at(c * blk, blk), own])
    fetch_u = fetch(wu.at[:, at(r * units, units)], WU.at[own, :])
    fetch_q = fetch(wq.at[:, at(r * heads, heads)], WQ.at[own, :])
    fetch_n = fetch(wn.at[at(r * units, units), :], WN.at[:, own])
    fetch_d = fetch(wd.at[at(r * HD, HD), :], WD.at[:, own])
    pl.semaphore_wait(
        barrier, 3 + (c < cols - 1).astype(jnp.int32) + (c >= 1).astype(jnp.int32)
    )

    def rows(b):
        return at(b * blk, blk)

    def chain_send(tag, step, buf, columns, first=None):
        for word, move, edge in (("u", 1, c < cols - 1), ("d", -1, c >= 1)):
            block = c - move * (step - 1)
            valid = edge & (block >= 0) & (block <= cols - 1)
            source = first if first is not None else buf.at[rows(block), columns]
            copies.start(
                f"{tag}{word}{step}", source, buf.at[rows(block), columns], {"col": c + move}, valid
            )

    def chain_wait(tag, step):
        copies.came(f"{tag}u{step}", c >= step)
        copies.came(f"{tag}d{step}", c + step <= cols - 1)

    def row_send(name, s):
        b = col_of[s]
        copies.start(name, X.at[rows(b), own], X.at[rows(b), other], y_dev)

    q2 = q + 2 - 4 * hi

    def weight(name, source, full, row0, size, columns, spread):
        share = q if spread else k

        def place(index):
            return full.at[at(row0 + index * size, size), columns]

        copies.start(f"{name}y", source(at(share * size, size)), place(share), y_dev)

        def pass_on():
            copies.came(f"{name}y")
            if spread:
                copies.start(f"{name}x", place(q), place(q), x_dev)
            copies.start(f"{name}c", place(share), place(share), core_dev)

        def pass_far():
            copies.came(f"{name}x")
            copies.start(f"{name}f", place(q2), place(q2), core_dev)

        def done():
            copies.came(f"{name}c")
            if spread:
                copies.came(f"{name}f")

        return pass_on, pass_far, done

    everything = slice(None)
    chain_send("x", 1, X, own, hid)
    copies.start("xy0", hid, X.at[rows(c), other], y_dev)
    for j, vector in enumerate((gain1, bias1, gain2, bias2)):
        NV[j : j + 1, own] = row_of(vector[...])
    NV[4:8, own] = jnp.zeros((4, wid), F32)
    copies.start("nv", NV.at[:, own], NV.at[:, other], y_dev)
    wu_on, wu_far, wu_done = weight(
        "wu", lambda rs: wu.at[rs, at((1 - r) * units, units)], WU, wid, wid // 4, everything, True
    )

    seg_row = seg[...].astype(F32)
    seg_col = jnp.transpose(jnp.broadcast_to(seg_row, (128, rows_all)))
    STAT[:, 3:4] = seg_col[:, 0:1]

    def table(i):
        block = at(i * blk, blk)
        starts = jnp.sum(
            (seg_row < STAT[block, 3:4]).astype(F32), axis=1, keepdims=True
        )
        index = lax.broadcasted_iota(jnp.int32, (blk, 1), 0) + i * blk
        lane = lax.broadcasted_iota(jnp.int32, (1, 128), 1)
        turn = jnp.exp(
            lax.rem(lane, ROT // 2).astype(F32) * (-2.0 * math.log(rope_base) / ROT)
        )
        angles = (index.astype(F32) - starts) * turn
        COS[block, :] = jnp.where(lane < ROT, jnp.cos(angles), 1.0)
        SIN[block, :] = jnp.where(
            lane < ROT // 2, -jnp.sin(angles), jnp.where(lane < ROT, jnp.sin(angles), 0.0)
        )

    tiles(cols, table)

    def rotate(head, block, sign):
        first = head[:, :128]
        lane = lax.broadcasted_iota(jnp.int32, first.shape, 1)
        swapped = jnp.where(
            lane < ROT // 2, pltpu.roll(first, 128 - ROT // 2, 1), pltpu.roll(first, ROT // 2, 1)
        )
        turned = first * COS[block, :] + sign * (swapped * SIN[block, :])
        return jnp.concatenate([turned, head[:, 128:]], axis=1)

    sub = 64

    def norm_block(b):
        def part(i):
            rs = at(b * blk + i * sub, sub)
            x = X[rs, :].astype(F32)
            mean = jnp.sum(x, axis=1, keepdims=True) * (1.0 / width)
            square = jnp.sum(x * x, axis=1, keepdims=True) * (1.0 / width)
            inv = lax.rsqrt(square - mean * mean + eps_norm)
            STAT[rs, 0:1] = mean
            STAT[rs, 1:2] = inv
            normal = (x - mean) * inv
            OUTP[rs, :] = (normal * NV[0:1, :] + NV[1:2, :]).astype(BF16)
            N[rs, :] = (normal * NV[2:3, :] + NV[3:4, :]).astype(BF16)

        tiles(blk // sub, part)

    def up_block(b):
        def part(j):
            cs = at(j * TILE, TILE)
            bias = row_of(up_b[at(r * units + j * TILE, TILE)])
            up = dot(N[rows(b), :], WU[:, cs], NN) + bias
            cdf = 0.5 * (1.0 + lax.erf(up * (1.0 / math.sqrt(2.0))))
            HID[rows(b), cs] = (up * cdf).astype(BF16)
            SLOPE[rows(b), cs] = (
                cdf + up * jnp.exp(-0.5 * up * up) * (1.0 / math.sqrt(2.0 * math.pi))
            ).astype(BF16)

        tiles(units // TILE, part)

    fetch_c.wait()
    fetch_x.wait()
    fetch_g.wait()
    chain_wait("x", 1)
    chain_send("x", 2, X, own)
    row_send("xy1", 1)
    chain_wait("x", 2)
    chain_send("x", 3, X, own)
    row_send("xy2", 2)
    chain_send("g", 1, G, own, cot)
    wu_on()
    copies.came("nv")
    copies.came("xy0")
    norm_block(col_of[0])
    chain_wait("x", 3)
    row_send("xy3", 3)
    copies.start("gy", cot, G.at[rows(c), other], y_dev)
    wq_on, _, wq_done = weight(
        "wq", lambda rs: wq.at[rs, at((1 - r) * heads, heads)], WQ, wid, wid // 2, everything, False
    )

    def rows_of(ref, start, rs):
        return ref.at[at(start + rs.start, rs.size), :]

    wn_on, _, wn_done = weight(
        "wn", lambda rs: rows_of(wn, (1 - r) * units, rs), WN, 0, units // 2, other, False
    )
    wd_on, _, wd_done = weight(
        "wd", lambda rs: rows_of(wd, (1 - r) * HD, rs), WD, 0, HD // 2, other, False
    )
    wu_far()
    copies.came("xy1")
    norm_block(col_of[1])
    fetch_u.wait()
    wu_done()
    up_block(col_of[0])
    up_block(col_of[1])
    chain_wait("g", 1)
    chain_send("g", 2, G, own)
    copies.came("xy2")
    norm_block(col_of[2])
    up_block(col_of[2])
    chain_wait("g", 2)
    chain_send("g", 3, G, own)
    copies.came("xy3")
    norm_block(col_of[3])
    up_block(col_of[3])
    copies.came("gy")
    chain_send("h", 1, G, other)

    def grad_send(name, staged, left, right, n_rows, n_cols, target):
        def part(i):
            cs = at(i * TILE, TILE)
            staged[:, cs] = dot(left(None), right(cs), TN).astype(BF16)

        tiles(n_cols // TILE, part)
        copies.start(name, staged, target, core_dev)

    hid_keep, hid_send = at(k * uh, uh), at((1 - k) * uh, uh)
    att_keep, att_send = at(k * dh, dh), at((1 - k) * dh, dh)

    def out_grad(name, side, left_ref, keep, give, staged, landing):
        base = side * wid

        def give_part(i):
            cs = at(i * TILE, TILE)
            staged[:, cs] = dot(
                left_ref[:, give], G[:, at(base + i * TILE, TILE)], TN
            ).astype(BF16)

        tiles(wid // TILE, give_part)
        copies.start(f"{name}a", staged, landing, core_dev)

    def out_keep(name, side, left_ref, keep, landing):
        base = side * wid
        copies.came(f"{name}a")

        def keep_part(i):
            cs = at(i * TILE, TILE)
            mine = dot(left_ref[:, keep], G[:, at(base + i * TILE, TILE)], TN)
            landing[:, cs] = (mine + landing[:, cs].astype(F32)).astype(BF16)

        tiles(wid // TILE, keep_part)

    down_tiles = [slice(i * TILE, (i + 1) * TILE) for i in range(wid // TILE)]

    def down_give(side, staged):
        for i, cs in enumerate(down_tiles):
            part = dot(HID[:, hid_send], G[:, side * wid + i * TILE : side * wid + (i + 1) * TILE], TN)
            staged[:, cs] = part.astype(BF16)
            copies.start(f"dn{side}a{i}", staged.at[:, cs], S_dn.at[side, :, cs], core_dev)

    def down_keep(side):
        half_rows = uh // 2
        give = at((1 - hi) * half_rows, half_rows)
        for i, cs in enumerate(down_tiles):
            copies.came(f"dn{side}a{i}")
            mine = dot(HID[:, hid_keep], G[:, side * wid + i * TILE : side * wid + (i + 1) * TILE], TN)
            S_dn[side, :, cs] = (mine + S_dn[side, :, cs].astype(F32)).astype(BF16)
            if side == 0:
                copies.start(f"dn0x{i}", S_dn.at[0, :, cs], X_dn.at[:, cs], x_dev)
            else:
                copies.start(f"dn1x{i}", S_dn.at[1, give, cs], V_dn.at[:, cs], x_dev)

    halves = {}

    def cross(name, total, n_rows, landing):
        half_rows = n_rows // 2
        give, keep = at((1 - hi) * half_rows, half_rows), at(hi * half_rows, half_rows)
        copies.start(f"{name}x", total.at[give, :], landing, x_dev)
        halves[name] = (total.at[keep, :], landing)

    def crossed(name, target, parts=("",)):
        mine, landing = halves[name]
        for word in parts:
            copies.came(f"{name}x{word}")
        n = landing.shape[0]
        step = min(n, 128)

        def part(i):
            rs = at(i * step, step)
            landing[rs, :] = (mine[rs, :].astype(F32) + landing[rs, :].astype(F32)).astype(BF16)

        tiles(n // step, part)
        copies.start(f"{name}y", landing, target, y_dev)

    def spread_out(name, came, result, here):
        copies.came(f"{name}y")
        copies.start(f"{name}g", came, result.at[here], x_dev)
        copies.start(f"{name}t", came, result.at[here], core_dev)
        fetch(came, result.at[here])

    def pass_quarter(name, result, there):
        copies.came(f"{name}g")
        copies.start(f"{name}f", result.at[there], result.at[there], core_dev)

    def finish(name, total, came, result, here, parts=("",)):
        for word in parts:
            copies.came(f"{name}x{word}")
        n = total.shape[0]
        step = min(n, 128)

        def part(i):
            rs = at(i * step, step)
            came[rs, :] = (total[rs, :].astype(F32) + came[rs, :].astype(F32)).astype(BF16)

        tiles(n // step, part)
        copies.start(f"{name}t", came, result.at[here], core_dev)
        fetch(came, result.at[here])

    wide = slice(None)

    def down_at(side, part=None):
        start, n = side * units + k * uh, uh
        if part is not None:
            start, n = start + part * (uh // 2), uh // 2
        return (at(start, n), wide)

    def dense_at(side, part=None):
        start, n = side * HD + k * dh, dh
        if part is not None:
            start, n = start + part * (dh // 2), dh // 2
        return (at(start, n), wide)

    def up_at(side, part=None):
        taken = wide if part is None else at(part * (wid // 2), wid // 2)
        return (taken, at(side * units + k * uh, uh))

    def qkv_at(side, part=None):
        taken = wide if part is None else at(part * (wid // 2), wid // 2)
        return (taken, at(side * heads + k * hh, hh))

    chain_wait("g", 3)
    both_tiles = tuple(range(len(down_tiles)))
    down_give(0, DUP.at[pl.ds(0, uh), :])
    down_keep(0)

    chain_wait("h", 1)
    chain_send("h", 2, G, other)
    fetch_q.wait()
    wq_on()
    wq_done()

    def qkv_block(i):
        block = at(i * blk, blk)
        for j in range(3):
            bias = row_of(qkv_b[at(r * heads + j * HD, HD)])
            value = dot(OUTP[block, :], WQ[:, j * HD : (j + 1) * HD], NN) + bias
            if j < 2:
                value = rotate(value, block, 1.0)
            QKV[block, j * HD : (j + 1) * HD] = value.astype(BF16)

    tiles(cols, qkv_block)
    chain_wait("h", 2)
    chain_send("h", 3, G, other)

    def key_range(i):
        low = max(0, i - 2) * blk
        return slice(i * blk, (i + 1) * blk), slice(low, (i + 1) * blk), low

    def block_scores(i):
        mine, span, low = key_range(i)
        n = span.stop - low
        s = dot(QKV[mine, 0:HD], QKV[span, HD : 2 * HD], NT) * scale
        row_id = lax.broadcasted_iota(jnp.int32, (blk, n), 0) + i * blk
        col_id = lax.broadcasted_iota(jnp.int32, (blk, n), 1) + low
        same = STAT[mine, 3:4] == seg_row[:, span]
        return jnp.where(same & (col_id <= row_id), s, -1e30)

    for i in range(cols):
        mine, span, low = key_range(i)
        s = block_scores(i)
        largest = jnp.max(s, axis=1, keepdims=True)
        p = jnp.exp(s - largest)
        total = jnp.sum(p, axis=1, keepdims=True)
        STAT[mine, 2:3] = largest + jnp.log(total)
        p_low = (p / total).astype(BF16)
        ATT[mine, :] = dot(p_low, QKV[span, 2 * HD :], NN).astype(BF16)
    out_grad("de0", 0, ATT, att_keep, att_send, A_de.at[0], S_de.at[0])
    fetch_n.wait()
    fetch_d.wait()

    def branch_block(b, side):
        def part(j):
            cs = at(side * wid + j * TILE, TILE)
            both = dot(ATT[rows(b), :], WD[:, cs], NN) + dot(HID[rows(b), :], WN[:, cs], NN)
            OUTP[rows(b), cs] = both.astype(BF16)

        tiles(wid // TILE, part)

    branch_block(col_of[2], 0)
    out_keep("de0", 0, ATT, att_keep, S_de.at[0])
    copies.start("de0x", S_de.at[0], X_de, x_dev)
    for s in (3, 1, 0):
        branch_block(col_of[s], 0)

    chain_wait("h", 3)
    at_end, between = lax.rem(c, 3) == 0, lax.rem(c, 3) != 0

    def own_near(name, when):
        copies.start(
            name, OUTP.at[rows(col_of[1]), own], OZ1.at[:, own], {"col": col_of[1]}, when
        )

    own_near("oa1", at_end)
    down_give(1, DUP.at[pl.ds(uh, uh), :])
    out_grad("de1", 1, ATT, att_keep, att_send, A_de.at[1], S_de.at[1])
    wn_on()
    down_keep(1)
    halves["dn1"] = (S_dn.at[1, at(hi * (uh // 2), uh // 2), :], V_dn)
    out_keep("de1", 1, ATT, att_keep, S_de.at[1])
    cross("de1", S_de.at[1], dh, V_de)
    own_near("oc1", between)
    wn_done()
    copies.start("oa2", OUTP.at[rows(col_of[2]), own], OZ2.at[:, own], {"col": col_of[2]})
    wd_on()

    copies.sent(*[f"dn{side}a{i}" for side in (0, 1) for i in both_tiles])

    def up_grad_part(i):
        block = at(i * blk, blk)
        for j in range(units // TILE):
            cs = slice(j * TILE, (j + 1) * TILE)
            back = dot(G[block, :], WN[cs, :], NT)
            DUP[block, cs] = (back * SLOPE[block, cs].astype(F32)).astype(BF16)

    tiles(cols, up_grad_part)
    keep_u, give_u = at(k * uh, uh), at((1 - k) * uh, uh)
    keep_h, give_h = at(k * hh, hh), at((1 - k) * hh, hh)

    def in_give(name, side, right_ref, give, staged, landing):
        def part(i):
            rs = at(i * TILE, TILE)
            lefts = N[:, at(side * wid + i * TILE, TILE)]
            staged[rs, :] = dot(lefts, right_ref[:, give], TN).astype(BF16)

        tiles(wid // TILE, part)
        copies.start(f"{name}{side}a", staged, landing.at[side], core_dev)

    def in_keep(name, side, right_ref, keep, landing, crossing=None):
        copies.came(f"{name}{side}a")
        n = wid // 2

        def part(i):
            rs = at(i * n, n)
            mine = dot(N[:, at(side * wid + i * n, n)], right_ref[:, keep], TN)
            landing[side, rs, :] = (mine + landing[side, rs, :].astype(F32)).astype(BF16)

        if crossing is None:
            tiles(2, part)
        else:
            part(1 - hi)
            crossing()
            part(hi)

    wd_done()
    branch_block(col_of[3], 1)
    copies.start("oy3", OUTP.at[rows(col_of[3]), other], OY.at[1], y_dev)
    in_give("up", 1, DUP, give_u, SLOPE.at[:, pl.ds(uh, uh)], S_up)
    for i in range(cols):
        mine = slice(i * blk, (i + 1) * blk)
        DAT[mine, :] = dot(G[mine, :], WD[...], NT).astype(BF16)
    BQ[q, 2:3, :] = jnp.sum(G[:, own].astype(F32), axis=0, keepdims=True)

    copies.sent(*[f"{t}{w}{s}" for t in "gh" for w in "ud" for s in (1, 2, 3)])
    pl.semaphore_signal(credit.at[0], inc=1, device_id=x_dev, device_id_type=MESH)
    pl.semaphore_signal(credit.at[1], inc=1, device_id=y_dev, device_id_type=MESH)
    X_up, low, high = G.at[:, pl.ds(0, uh)], pl.ds(0, wid // 2), pl.ds(wid // 2, wid // 2)
    V_up, R_up = G.at[low, pl.ds(uh, uh)], G.at[high, pl.ds(uh, uh)]
    X_qk = WN.at[:, pl.ds(0, hh)]
    V_qk, R_qk = WN.at[low, pl.ds(hh, hh)], WN.at[high, pl.ds(hh, hh)]

    pl.semaphore_wait(credit.at[0], 1)
    in_keep("up", 1, DUP, keep_u, S_up, lambda: cross("up1", S_up.at[1], wid, V_up))
    crossed("dn1", R_dn, both_tiles)
    in_give("up", 0, DUP, give_u, SLOPE.at[:, pl.ds(0, uh)], S_up)
    branch_block(col_of[2], 1)
    copies.start("ob2", OUTP.at[rows(col_of[2]), other], OZ2.at[:, other], {"col": col_of[2]})
    in_keep("up", 0, DUP, keep_u, S_up)
    copies.start("up0x", S_up.at[0], X_up, x_dev)

    branch_block(col_of[1], 1)
    copies.start("ob1", OUTP.at[rows(col_of[1]), other], OZ1.at[:, other], {"col": col_of[1]})
    branch_block(col_of[0], 1)
    crossed("de1", R_de)
    copies.sent("wnc")
    pl.semaphore_signal(credit.at[2], inc=1, device_id=x_dev, device_id_type=MESH)
    pl.semaphore_signal(credit.at[3], inc=1, device_id=y_dev, device_id_type=MESH)
    pl.semaphore_signal(credit.at[4], inc=1, device_id=y_dev, device_id_type=MESH)

    def out_block():
        b = col_of[3]
        copies.came("oy3")

        def part(i):
            rs = at(b * blk + i * sub, sub)
            came = OY[1, at(i * sub, sub), :]
            OUTP[rs, own] = (OUTP[rs, own].astype(F32) + came.astype(F32)).astype(BF16)

        tiles(blk // sub, part)
        copies.start("oz3", OUTP.at[rows(b), own], OZ3, {"col": b})

    def again(i):
        rs = at(i * sub, sub)
        normal = (X[rs, :].astype(F32) - STAT[rs, 0:1]) * STAT[rs, 1:2]
        N[rs, :] = (normal * NV[0:1, :] + NV[1:2, :]).astype(BF16)

    tiles(rows_all // sub, again)
    TMP[...] = jnp.zeros_like(TMP)
    for i in range(cols):
        mine, span, low = key_range(i)
        query = QKV[mine, 0:HD]
        p = jnp.exp(block_scores(i) - STAT[mine, 2:3])
        d_p = dot(DAT[mine, :], QKV[span, 2 * HD :], NT)
        delta = jnp.sum(d_p * p, axis=1, keepdims=True)
        d_s = (p * (d_p - delta)).astype(BF16)
        p_low = p.astype(BF16)
        d_query = dot(d_s, QKV[span, HD : 2 * HD], NN) * scale
        QKV[mine, 0:HD] = rotate(d_query, mine, -1.0).astype(BF16)
        for j in range(low // blk, i + 1):
            js = slice(j * blk - low, (j + 1) * blk - low)
            ks, vs = slice(j * HD, (j + 1) * HD), slice((cols + j) * HD, (cols + j + 1) * HD)
            TMP[:, ks] += dot(d_s[:, js], query, TN)
            TMP[:, vs] += dot(p_low[:, js], DAT[mine, :], TN)
    for j in range(cols):
        mine = slice(j * blk, (j + 1) * blk)
        ks, vs = slice(j * HD, (j + 1) * HD), slice((cols + j) * HD, (cols + j + 1) * HD)
        QKV[mine, HD : 2 * HD] = rotate(TMP[:, ks] * scale, mine, -1.0).astype(BF16)
        QKV[mine, 2 * HD :] = TMP[:, vs].astype(BF16)

    copies.sent("up0a", "up1a")
    in_give("qk", 1, QKV, give_h, SLOPE.at[:, pl.ds(hh, hh)], S_qk)
    in_give("qk", 0, QKV, give_h, SLOPE.at[:, pl.ds(0, hh)], S_qk)
    pl.semaphore_wait(credit.at[1], 1)
    crossed("up1", R_up)
    pl.semaphore_wait(credit.at[2], 1)
    in_keep("qk", 1, QKV, keep_h, S_qk, lambda: cross("qk1", S_qk.at[1], wid, V_qk))
    in_keep("qk", 0, QKV, keep_h, S_qk)
    copies.start("qk0x", S_qk.at[0], X_qk, x_dev)

    def gather_dp(name, slots):
        for word, device in (("c", core_dev), ("x", x_dev), ("d", far_dev)):
            copies.start(f"{name}{word}", slots.at[q], slots.at[q], device)

    def gathered_dp(name, slots):
        for word in "cxd":
            copies.came(f"{name}{word}")
        return slots[0] + slots[1] + slots[2] + slots[3]

    BQ[q, 0:1, :] = jnp.sum(DUP[...].astype(F32), axis=0, keepdims=True)
    BQ[q, 1:2, 0:heads] = jnp.sum(QKV[...].astype(F32), axis=0, keepdims=True)
    BQ[q, 1:2, heads:] = jnp.zeros((1, wid - heads), F32)
    BQ[q, 3:8, :] = jnp.zeros((5, wid), F32)
    gather_dp("b", BQ)

    NSUM[...] = jnp.zeros_like(NSUM)
    pl.semaphore_wait(credit.at[4], 1)

    def norm_back(b):
        rb = rows(b)
        mean, inv = STAT[rb, 0:1], STAT[rb, 1:2]

        def first(j, carry):
            along, plain = carry
            cs = at(j * TILE, TILE)
            one = dot(QKV[rb, :], WQ[cs, :], NT)
            two = dot(DUP[rb, :], WU[cs, :], NT)
            normal = (X[rb, cs].astype(F32) - mean) * inv
            NSUM[0:1, cs] += jnp.sum(one * normal, axis=0, keepdims=True)
            NSUM[1:2, cs] += jnp.sum(one, axis=0, keepdims=True)
            NSUM[2:3, cs] += jnp.sum(two * normal, axis=0, keepdims=True)
            NSUM[3:4, cs] += jnp.sum(two, axis=0, keepdims=True)
            grad = one * NV[0:1, cs] + two * NV[2:3, cs]
            TMP[:, cs] = grad
            along = along + jnp.sum(grad * normal, axis=1, keepdims=True)
            plain = plain + jnp.sum(grad, axis=1, keepdims=True)
            return along, plain

        zero = jnp.zeros((blk, 1), F32)
        along, plain = lax.fori_loop(0, width // TILE, first, (zero, zero))
        along, plain = along * (1.0 / width), plain * (1.0 / width)

        def second(j):
            cs = at(j * TILE, TILE)
            normal = (X[rb, cs].astype(F32) - mean) * inv
            N[rb, cs] = (inv * (TMP[:, cs] - plain - normal * along)).astype(BF16)

        tiles(width // TILE, second)

    EY = [HID.at[pl.ds(j * blk, blk), :] for j in range(3)]
    pl.semaphore_wait(credit.at[3], 1)
    for s in (2, 3):
        norm_back(col_of[s])
        copies.start(f"ey{s}", N.at[rows(col_of[s]), other], EY[s - 1], y_dev)
        if s == 2:
            out_block()
            spread_out("dn1", R_dn, g_down, down_at(1 - r, hi))
        else:
            spread_out("de1", R_de, g_dense, dense_at(1 - r, hi))
    norm_back(col_of[1])
    copies.start(
        "ezb", N.at[rows(col_of[1]), other], DZ1.at[:, other], {"col": col_of[1]}
    )
    norm_back(col_of[0])
    SMO[0:4, :] = NSUM[0:4, other]
    copies.start("sy", SMO, SMR, y_dev)

    def mine_at(i):
        return at(c * blk + i * sub, sub)

    def row_rest(buf, names, whole, landing, name):
        for arrival, when in names:
            copies.came(arrival, when)

        def part(i):
            rs = at(i * sub, sub)
            total = buf[mine_at(i), other].astype(F32)
            for ref in whole:
                total = total + ref[rs, other].astype(F32)
            buf[mine_at(i), other] = total.astype(BF16)

        tiles(blk // sub, part)
        copies.start(name, buf.at[rows(c), other], landing, y_dev)

    def total_of(i, buf, whole, parts):
        rs = at(i * sub, sub)
        total = buf[mine_at(i), own].astype(F32)
        for ref in whole:
            total = total + ref[rs, own].astype(F32)
        for ref in parts:
            total = total + ref[rs, :].astype(F32)
        return total

    def x_block(s):
        b = col_of[s]
        copies.came(f"ey{s}")

        def part(i):
            rs = at(b * blk + i * sub, sub)
            came = EY[s - 1][at(i * sub, sub), :]
            N[rs, own] = (N[rs, own].astype(F32) + came.astype(F32)).astype(BF16)

        tiles(blk // sub, part)
        copies.start(
            f"ea{s}", N.at[rows(b), own], DZ.at[s - 2], {"col": col_of[1]}, at_end
        )

    def x_pass(s):
        b = col_of[s]
        copies.came(f"ea{5 - s}", between)

        @pl.when(between)
        def _():
            def part(i):
                rs = at(b * blk + i * sub, sub)
                came = DZ[3 - s, at(i * sub, sub), :]
                N[rs, own] = (N[rs, own].astype(F32) + came.astype(F32)).astype(BF16)

            tiles(blk // sub, part)

        copies.start(f"eb{s}", N.at[rows(b), own], DZ.at[2], {"col": b}, between)

    row_rest(
        OUTP,
        (("oa1", between), ("oc1", at_end), ("oa2", None), ("ob1", None), ("ob2", None)),
        (OZ1, OZ2),
        OY.at[0],
        "oy0",
    )
    spread_out("up1", R_up, g_up, up_at(1 - r, hi))
    finish("dn0", S_dn.at[0], X_dn, g_down, down_at(r), both_tiles)
    finish("de0", S_de.at[0], X_de, g_dense, dense_at(r))
    finish("up0", S_up.at[0], X_up, g_up, up_at(r))
    crossed("qk1", R_qk)
    x_block(2)
    copies.came("sy")
    NZ[c, 0:4, :] = NSUM[0:4, own] + SMR[0:4, :]
    for s in (1, 2, 3):
        copies.start(f"sz{s}", NZ.at[c], NZ.at[c], {"col": col_of[s]})
    x_block(3)
    copies.start("eza", N.at[rows(col_of[1]), own], DZ1.at[:, own], {"col": col_of[1]})
    BS[...] = gathered_dp("b", BQ)
    copies.start("by", BS, BR, y_dev)
    row_rest(N, (("ezb", None),), (DZ1,), EY[0], "ey0")
    x_pass(3)
    finish("qk0", S_qk.at[0], X_qk, g_qkv, qkv_at(r))
    pass_quarter("dn1", g_down, down_at(1 - r, 1 - hi))
    x_pass(2)
    for s in (1, 2, 3):
        copies.came(f"sz{s}")
    NQ[q] = NZ[0] + NZ[1] + NZ[2] + NZ[3]
    gather_dp("n", NQ)
    pass_quarter("de1", g_dense, dense_at(1 - r, 1 - hi))
    spread_out("qk1", R_qk, g_qkv, qkv_at(1 - r, hi))
    for name in ("oz3", "oy0"):
        copies.came(name)

    def out_last(i):
        total = total_of(i, OUTP, (OZ1, OZ2), (OZ3, OY.at[0]))
        total = total + X[mine_at(i), own].astype(F32)
        out[at(i * sub, sub), :] = (total + row_of(dense_b[...] + down_b[...])).astype(BF16)

    tiles(blk // sub, out_last)
    fetch(out, out_hbm)
    pass_quarter("up1", g_up, up_at(1 - r, 1 - hi))
    copies.came("by")
    small[0:8, :] = BS[...]
    small[8:16, :] = BR[...]
    small[4:8, :] = gathered_dp("n", NQ)[0:4]
    fetch(small, small_hbm)
    copies.came("eza")
    copies.came("eb2", at_end)
    copies.came("eb3", between)
    copies.came("ey0")

    def x_last(i):
        total = total_of(i, N, (DZ1,), (DZ.at[2], EY[0]))
        in_grad[at(i * sub, sub), :] = COT[at(i * sub, sub), :].astype(F32) + total

    tiles(blk // sub, x_last)
    fetch(in_grad, in_grad_hbm)
    pass_quarter("qk1", g_qkv, qkv_at(1 - r, 1 - hi))
    for name in ("dn0", "de0", "up0", "qk0"):
        copies.came(f"{name}t")
    for name in ("dn1", "de1", "up1", "qk1"):
        copies.came(f"{name}t")
        copies.came(f"{name}f")
    for copy in local[7:]:
        copy.wait()
    copies.sent_all()


def scratch(blk, wid, cols, units, heads):
    tokens, width = blk * cols, 2 * wid
    low = [
        (tokens, width), (tokens, width), (width, heads), (width, units), (HD, width),
        (units, width), (tokens, width),
    ]
    V = pltpu.VMEM
    return (
        [V((blk, wid), BF16), V((blk, wid), F32), V((16, wid), F32)]
        + [V(shape, BF16) for shape in low]
        + [V((tokens, 128), F32)]
        + [
            V(shape, BF16)
            for shape in (
                (tokens, heads), (tokens, HD), (tokens, units), (tokens, units), (tokens, units),
                (tokens, HD), (tokens, width), (blk, width), (blk, width), (blk, wid),
                (2, blk, wid), (blk, width), (3, blk, wid), (blk, wid),
                (2, units // 2, wid), (2, HD // 2, wid), (2, wid, units // 2), (2, wid, heads // 2),
                (units // 4, wid), (HD // 4, wid), (units // 4, wid), (HD // 4, wid),
                (units // 2, wid), (HD // 2, wid), (2, HD // 2, wid),
            )
        ]
        + [
            V((blk, width), F32),
            V((8, width), F32),
            V((tokens, 128), F32),
            V((tokens, 128), F32),
            V((8, width), F32),
            V((8, wid), F32),
            V((8, wid), F32),
            V((cols, 8, wid), F32),
            V((4, 8, wid), F32),
            V((4, 8, wid), F32),
            V((8, wid), F32),
            V((8, wid), F32),
            pltpu.SemaphoreType.DMA((120,)),
            pltpu.SemaphoreType.DMA((120,)),
            pltpu.SemaphoreType.DMA((20,)),
            pltpu.SemaphoreType.REGULAR((5,)),
        ]
    )


def widen_kernel(*refs):
    given, results = refs[:7], refs[7:]
    small = given[6]
    for source, target in zip(given[:6], results[:6]):
        target[...] = source[...].astype(target.dtype)

    @pl.when(pl.program_id(0) == 0)
    def _():
        gain1, bias1, gain2, bias2, qkv_sum, dense_sum, up_sum, down_sum = results[6:]
        for j, ref in enumerate((gain1, bias1, gain2, bias2)):
            ref[...] = small[4 + j]
        dense_sum[...] = small[2]
        down_sum[...] = small[2]
        r = lax.axis_index("row")
        for ref, index in ((up_sum, 0), (qkv_sum, 1)):
            n = ref.shape[0] // 2
            ref[at(r * n, n)] = small[index, 0:n]
            ref[at((1 - r) * n, n)] = small[8 + index, 0:n]


def swap(value, axis, mask):
    size = lax.axis_size(axis)
    return lax.ppermute(value, axis, [(i, i ^ mask) for i in range(size)])


def shards(
    hidden_in,
    segment,
    norm1_gain,
    norm1_bias,
    norm2_gain,
    norm2_bias,
    qkv_weight,
    qkv_bias,
    dense_weight,
    dense_bias,
    up_weight,
    up_bias,
    down_weight,
    down_bias,
    cotangent,
):
    blk, wid = hidden_in.shape
    cols = lax.axis_size("col")
    heads, units = qkv_weight.shape[1] // 2, up_weight.shape[1] // 2
    vectors = (
        norm1_gain, norm1_bias, norm2_gain, norm2_bias, qkv_bias, up_bias, dense_bias, down_bias,
    )
    vmem = pl.BlockSpec(memory_space=pltpu.VMEM)
    far = pl.BlockSpec(memory_space=pl.ANY)
    shape = jax.ShapeDtypeStruct
    out, in_grad, small, g_qkv, g_dense, g_up, g_down = pl.pallas_call(
        functools.partial(step_kernel, (blk, wid, cols)),
        out_shape=(
            shape((blk, wid), BF16),
            shape((blk, wid), F32),
            shape((16, wid), F32),
            shape(qkv_weight.shape, BF16),
            shape(dense_weight.shape, BF16),
            shape(up_weight.shape, BF16),
            shape(down_weight.shape, BF16),
        ),
        in_specs=[far] * 6 + [vmem] * 9,
        out_specs=(far,) * 7,
        scratch_shapes=scratch(blk, wid, cols, units, heads),
        compiler_params=pltpu.CompilerParams(
            collective_id=0, has_side_effects=True, vmem_limit_bytes=67043328
        ),
        name="step",
    )(
        hidden_in, cotangent, qkv_weight, up_weight, dense_weight, down_weight, segment, *vectors
    )

    grads = (g_qkv, g_dense, g_up, g_down)
    mask = 4
    while mask < lax.axis_size("dp"):
        grads = tuple(
            (g.astype(F32) + swap(g, "dp", mask).astype(F32)).astype(BF16) for g in grads
        )
        small = small + swap(small, "dp", mask)
        mask *= 2
    steps = 4

    def cut(array):
        rows, columns = array.shape
        return pl.BlockSpec((rows // steps, columns), lambda i: (i, 0))

    def whole(n):
        return pl.BlockSpec((n,), lambda i: (0,))

    lengths = [wid] * 4 + [2 * heads, wid, 2 * units, wid]
    widened = pl.pallas_call(
        widen_kernel,
        grid=(steps,),
        out_shape=[shape(out.shape, BF16), shape(in_grad.shape, F32)]
        + [shape(g.shape, F32) for g in grads]
        + [shape((n,), F32) for n in lengths],
        in_specs=[cut(out), cut(in_grad)]
        + [cut(g) for g in grads]
        + [pl.BlockSpec(small.shape, lambda i: (0, 0))],
        out_specs=[cut(out), cut(in_grad)] + [cut(g) for g in grads] + [whole(n) for n in lengths],
        compiler_params=pltpu.CompilerParams(vmem_limit_bytes=60 << 20),
        name="widen",
    )(out, in_grad, *grads, small)
    out, in_grad, d_qkv, d_dense, d_up, d_down, *sums = widened
    return (
        out,
        in_grad,
        sums[0],
        sums[1],
        sums[2],
        sums[3],
        d_qkv,
        sums[4],
        d_dense,
        sums[5],
        d_up,
        sums[6],
        d_down,
        sums[7],
    )


def solution(mesh):
    return jax.shard_map(
        shards,
        mesh=mesh,
        in_specs=(
            P(("dp", "col"), "row"),
            P("dp", None),
            P("row"),
            P("row"),
            P("row"),
            P("row"),
            P("row", "col"),
            P("col"),
            P("col", "row"),
            P("row"),
            P("row", "col"),
            P("col"),
            P("col", "row"),
            P("row"),
            P(("dp", "col"), "row"),
        ),
        out_specs=(
            P(("dp", "col"), "row"),
            P(("dp", "col"), "row"),
            P("row"),
            P("row"),
            P("row"),
            P("row"),
            P("row", "col"),
            P("col"),
            P("col", "row"),
            P("row"),
            P("row", "col"),
            P("col"),
            P("col", "row"),
            P("row"),
        ),
        check_vma=False,
    )
```

```python
import functools
import math

import jax
import jax.numpy as jnp
from jax import lax
from jax.experimental import pallas as pl
from jax.experimental.pallas import tpu as pltpu
from jax.sharding import PartitionSpec as P

HD = 256
ROT = 64
F32 = jnp.float32
BF16 = jnp.bfloat16
MESH = pl.DeviceIdType.MESH

eps_norm = 1e-05
rope_base = 10000.0
TILE = 512
NN = (((1,), (0,)), ((), ()))
NT = (((1,), (1,)), ((), ()))
TN = (((0,), (0,)), ((), ()))


def dot(left, right, dims):
    return lax.dot_general(left, right, dims, preferred_element_type=F32)


class Copies:
    def __init__(self, send_sem, recv_sem):
        self.send_sem, self.recv_sem = send_sem, recv_sem
        self.made, self.open = {}, {}

    def start(self, name, source, target, device, when=None):
        index = len(self.made)
        copy = pltpu.make_async_remote_copy(
            src_ref=source,
            dst_ref=target,
            send_sem=self.send_sem.at[index],
            recv_sem=self.recv_sem.at[index],
            device_id=device,
            device_id_type=MESH,
        )
        self.made[name] = copy
        self.open[name] = when
        guarded(when, copy.start)

    def came(self, name, when=None):
        guarded(when, self.made[name].wait_recv)

    def sent(self, *names):
        for name in names:
            guarded(self.open.pop(name), self.made[name].wait_send)

    def sent_all(self):
        self.sent(*list(self.open))


def guarded(when, action):
    if when is None:
        action()
    else:
        pl.when(when)(action)


def row_of(vector):
    return vector.reshape(1, vector.shape[0])


def at(start, size):
    return pl.ds(pl.multiple_of(start, size), size)


def tiles(count, body):
    lax.fori_loop(0, count, lambda i, carry: (body(i), carry)[1], 0)


def step_kernel(
    sizes,
    hid, cot, wq, wu, wd, wn, seg, gain1, bias1, gain2, bias2, qkv_b, up_b, dense_b, down_b,
    out_hbm, in_grad_hbm, small_hbm, g_qkv, g_dense, g_up, g_down,
    out, in_grad, small, X, G, WQ, WU, WD, WN, N, STAT, QKV, ATT, HID, SLOPE, DUP, DAT, OUTP, OZ1, OZ2, OZ3, OY, DZ1, DZ, COT,
    S_dn, S_de, S_up, S_qk, R_dn, R_de, V_dn, V_de, V_up, X_dn, X_de, A_de, TMP, NV, COS, SIN, NSUM, SMO, SMR, NZ, NQ, BQ, BS, BR,
    send_sem, recv_sem, local_sem, credit,
):
    blk, wid, cols = sizes
    rows_all = blk * cols
    width = 2 * wid
    heads, units = WQ.shape[1], WU.shape[1]
    hh, uh, dh = heads // 2, units // 2, HD // 2
    r = lax.axis_index("row")
    c = lax.axis_index("col")
    dp = lax.axis_index("dp")
    k = lax.rem(dp, 2)
    hi = lax.rem(lax.div(dp, 2), 2)
    q = k + 2 * hi
    core_dev = {"dp": dp + 1 - 2 * k}
    x_dev = {"dp": dp + 2 - 4 * hi}
    far_dev = {"dp": dp + 3 - 2 * k - 4 * hi}
    y_dev = {"row": 1 - r}
    c_low, c_high = lax.rem(c, 2), lax.div(c, 2)
    col_of = [c, c + 1 - 2 * c_low, c + 2 - 4 * c_high, 3 - c]
    own, other = pl.ds(0, wid), pl.ds(wid, wid)
    scale = 1.0 / math.sqrt(HD)
    copies = Copies(send_sem, recv_sem)

    barrier = pltpu.get_barrier_semaphore()
    for device in (core_dev, x_dev, y_dev):
        pl.semaphore_signal(barrier, inc=1, device_id=device, device_id_type=MESH)
    for move, inside in ((1, c < cols - 1), (-1, c >= 1)):

        @pl.when(inside)
        def _():
            pl.semaphore_signal(
                barrier, inc=1, device_id={"col": c + move}, device_id_type=MESH
            )

    local = []

    def fetch(source, target):
        copy = pltpu.make_async_copy(source, target, local_sem.at[len(local)])
        copy.start()
        local.append(copy)
        return copy

    fetch_c = fetch(cot, COT)
    fetch_x = fetch(hid, X.at[at(c * blk, blk), own])
    fetch_g = fetch(cot, G.at[at(c * blk, blk), own])
    fetch_u = fetch(wu.at[:, at(r * units, units)], WU.at[own, :])
    fetch_q = fetch(wq.at[:, at(r * heads, heads)], WQ.at[own, :])
    fetch_n = fetch(wn.at[at(r * units, units), :], WN.at[:, own])
    fetch_d = fetch(wd.at[at(r * HD, HD), :], WD.at[:, own])
    pl.semaphore_wait(
        barrier, 3 + (c < cols - 1).astype(jnp.int32) + (c >= 1).astype(jnp.int32)
    )

    def rows(b):
        return at(b * blk, blk)

    def chain_send(tag, step, buf, columns, first=None):
        for word, move, edge in (("u", 1, c < cols - 1), ("d", -1, c >= 1)):
            block = c - move * (step - 1)
            valid = edge & (block >= 0) & (block <= cols - 1)
            source = first if first is not None else buf.at[rows(block), columns]
            copies.start(
                f"{tag}{word}{step}", source, buf.at[rows(block), columns], {"col": c + move}, valid
            )

    def chain_wait(tag, step):
        copies.came(f"{tag}u{step}", c >= step)
        copies.came(f"{tag}d{step}", c + step <= cols - 1)

    def row_send(name, s):
        b = col_of[s]
        copies.start(name, X.at[rows(b), own], X.at[rows(b), other], y_dev)

    q2 = q + 2 - 4 * hi

    def weight(name, source, full, row0, size, columns, spread):
        share = q if spread else k

        def place(index):
            return full.at[at(row0 + index * size, size), columns]

        copies.start(f"{name}y", source(at(share * size, size)), place(share), y_dev)

        def pass_on():
            copies.came(f"{name}y")
            if spread:
                copies.start(f"{name}x", place(q), place(q), x_dev)
            copies.start(f"{name}c", place(share), place(share), core_dev)

        def pass_far():
            copies.came(f"{name}x")
            copies.start(f"{name}f", place(q2), place(q2), core_dev)

        def done():
            copies.came(f"{name}c")
            if spread:
                copies.came(f"{name}f")

        return pass_on, pass_far, done

    everything = slice(None)
    chain_send("x", 1, X, own, hid)
    copies.start("xy0", hid, X.at[rows(c), other], y_dev)
    for j, vector in enumerate((gain1, bias1, gain2, bias2)):
        NV[j : j + 1, own] = row_of(vector[...])
    NV[4:8, own] = jnp.zeros((4, wid), F32)
    copies.start("nv", NV.at[:, own], NV.at[:, other], y_dev)
    wu_on, wu_far, wu_done = weight(
        "wu", lambda rs: wu.at[rs, at((1 - r) * units, units)], WU, wid, wid // 4, everything, True
    )

    seg_row = seg[...].astype(F32)
    seg_col = jnp.transpose(jnp.broadcast_to(seg_row, (128, rows_all)))
    STAT[:, 3:4] = seg_col[:, 0:1]

    def table(i):
        block = at(i * blk, blk)
        starts = jnp.sum(
            (seg_row < STAT[block, 3:4]).astype(F32), axis=1, keepdims=True
        )
        index = lax.broadcasted_iota(jnp.int32, (blk, 1), 0) + i * blk
        lane = lax.broadcasted_iota(jnp.int32, (1, 128), 1)
        turn = jnp.exp(
            lax.rem(lane, ROT // 2).astype(F32) * (-2.0 * math.log(rope_base) / ROT)
        )
        angles = (index.astype(F32) - starts) * turn
        COS[block, :] = jnp.where(lane < ROT, jnp.cos(angles), 1.0)
        SIN[block, :] = jnp.where(
            lane < ROT // 2, -jnp.sin(angles), jnp.where(lane < ROT, jnp.sin(angles), 0.0)
        )

    tiles(cols, table)

    def rotate(head, block, sign):
        first = head[:, :128]
        lane = lax.broadcasted_iota(jnp.int32, first.shape, 1)
        swapped = jnp.where(
            lane < ROT // 2, pltpu.roll(first, 128 - ROT // 2, 1), pltpu.roll(first, ROT // 2, 1)
        )
        turned = first * COS[block, :] + sign * (swapped * SIN[block, :])
        return jnp.concatenate([turned, head[:, 128:]], axis=1)

    sub = 64

    def norm_block(b):
        def part(i):
            rs = at(b * blk + i * sub, sub)
            x = X[rs, :].astype(F32)
            mean = jnp.sum(x, axis=1, keepdims=True) * (1.0 / width)
            square = jnp.sum(x * x, axis=1, keepdims=True) * (1.0 / width)
            inv = lax.rsqrt(square - mean * mean + eps_norm)
            STAT[rs, 0:1] = mean
            STAT[rs, 1:2] = inv
            normal = (x - mean) * inv
            OUTP[rs, :] = (normal * NV[0:1, :] + NV[1:2, :]).astype(BF16)
            N[rs, :] = (normal * NV[2:3, :] + NV[3:4, :]).astype(BF16)

        tiles(blk // sub, part)

    def up_block(b):
        def part(j):
            cs = at(j * TILE, TILE)
            bias = row_of(up_b[at(r * units + j * TILE, TILE)])
            up = dot(N[rows(b), :], WU[:, cs], NN) + bias
            cdf = 0.5 * (1.0 + lax.erf(up * (1.0 / math.sqrt(2.0))))
            HID[rows(b), cs] = (up * cdf).astype(BF16)
            SLOPE[rows(b), cs] = (
                cdf + up * jnp.exp(-0.5 * up * up) * (1.0 / math.sqrt(2.0 * math.pi))
            ).astype(BF16)

        tiles(units // TILE, part)

    fetch_c.wait()
    fetch_x.wait()
    fetch_g.wait()
    chain_wait("x", 1)
    chain_send("x", 2, X, own)
    row_send("xy1", 1)
    chain_wait("x", 2)
    chain_send("x", 3, X, own)
    row_send("xy2", 2)
    chain_send("g", 1, G, own, cot)
    wu_on()
    copies.came("nv")
    copies.came("xy0")
    norm_block(col_of[0])
    chain_wait("x", 3)
    row_send("xy3", 3)
    copies.start("gy", cot, G.at[rows(c), other], y_dev)
    wq_on, _, wq_done = weight(
        "wq", lambda rs: wq.at[rs, at((1 - r) * heads, heads)], WQ, wid, wid // 2, everything, False
    )

    def rows_of(ref, start, rs):
        return ref.at[at(start + rs.start, rs.size), :]

    wn_on, _, wn_done = weight(
        "wn", lambda rs: rows_of(wn, (1 - r) * units, rs), WN, 0, units // 2, other, False
    )
    wd_on, _, wd_done = weight(
        "wd", lambda rs: rows_of(wd, (1 - r) * HD, rs), WD, 0, HD // 2, other, False
    )
    wu_far()
    copies.came("xy1")
    norm_block(col_of[1])
    fetch_u.wait()
    wu_done()
    up_block(col_of[0])
    up_block(col_of[1])
    chain_wait("g", 1)
    chain_send("g", 2, G, own)
    copies.came("xy2")
    norm_block(col_of[2])
    up_block(col_of[2])
    chain_wait("g", 2)
    chain_send("g", 3, G, own)
    copies.came("xy3")
    norm_block(col_of[3])
    up_block(col_of[3])
    copies.came("gy")
    near_part, far_part = pl.ds(wid, wid // 2), pl.ds(wid + wid // 2, wid // 2)
    chain_send("h", 1, G, near_part)
    chain_send("i", 1, G, far_part)

    def grad_send(name, staged, left, right, n_rows, n_cols, target):
        def part(i):
            cs = at(i * TILE, TILE)
            staged[:, cs] = dot(left(None), right(cs), TN).astype(BF16)

        tiles(n_cols // TILE, part)
        copies.start(name, staged, target, core_dev)

    hid_keep, hid_send = at(k * uh, uh), at((1 - k) * uh, uh)
    att_keep, att_send = at(k * dh, dh), at((1 - k) * dh, dh)

    def out_grad(name, side, left_ref, keep, give, staged, landing):
        base = side * wid

        def give_part(i):
            cs = at(i * TILE, TILE)
            staged[:, cs] = dot(
                left_ref[:, give], G[:, at(base + i * TILE, TILE)], TN
            ).astype(BF16)

        tiles(wid // TILE, give_part)
        copies.start(f"{name}a", staged, landing, core_dev)

    def out_keep(name, side, left_ref, keep, landing):
        base = side * wid
        copies.came(f"{name}a")

        def keep_part(i):
            cs = at(i * TILE, TILE)
            mine = dot(left_ref[:, keep], G[:, at(base + i * TILE, TILE)], TN)
            landing[:, cs] = (mine + landing[:, cs].astype(F32)).astype(BF16)

        tiles(wid // TILE, keep_part)

    down_tiles = [slice(i * TILE, (i + 1) * TILE) for i in range(wid // TILE)]

    def down_give(side, staged, which):
        for i in which:
            cs = down_tiles[i]
            part = dot(HID[:, hid_send], G[:, side * wid + i * TILE : side * wid + (i + 1) * TILE], TN)
            staged[:, cs] = part.astype(BF16)
            copies.start(f"dn{side}a{i}", staged.at[:, cs], S_dn.at[side, :, cs], core_dev)

    def down_keep(side, which):
        half_rows = uh // 2
        give = at((1 - hi) * half_rows, half_rows)
        for i in which:
            cs = down_tiles[i]
            copies.came(f"dn{side}a{i}")
            mine = dot(HID[:, hid_keep], G[:, side * wid + i * TILE : side * wid + (i + 1) * TILE], TN)
            S_dn[side, :, cs] = (mine + S_dn[side, :, cs].astype(F32)).astype(BF16)
            if side == 0:
                copies.start(f"dn0x{i}", S_dn.at[0, :, cs], X_dn.at[:, cs], x_dev)
            else:
                copies.start(f"dn1x{i}", S_dn.at[1, give, cs], V_dn.at[:, cs], x_dev)

    halves = {}

    def cross(name, total, n_rows, landing):
        half_rows = n_rows // 2
        give, keep = at((1 - hi) * half_rows, half_rows), at(hi * half_rows, half_rows)
        copies.start(f"{name}x", total.at[give, :], landing, x_dev)
        halves[name] = (total.at[keep, :], landing)

    def crossed(name, target, parts=("",)):
        mine, landing = halves[name]
        for word in parts:
            copies.came(f"{name}x{word}")
        n = landing.shape[0]
        step = min(n, 128)

        def part(i):
            rs = at(i * step, step)
            landing[rs, :] = (mine[rs, :].astype(F32) + landing[rs, :].astype(F32)).astype(BF16)

        tiles(n // step, part)
        copies.start(f"{name}y", landing, target, y_dev)

    def spread_out(name, came, result, here):
        copies.came(f"{name}y")
        copies.start(f"{name}g", came, result.at[here], x_dev)
        copies.start(f"{name}t", came, result.at[here], core_dev)
        fetch(came, result.at[here])

    def pass_quarter(name, result, there):
        copies.came(f"{name}g")
        copies.start(f"{name}f", result.at[there], result.at[there], core_dev)

    def finish(name, total, came, result, here, parts=("",)):
        for word in parts:
            copies.came(f"{name}x{word}")
        n = total.shape[0]
        step = min(n, 128)

        def part(i):
            rs = at(i * step, step)
            came[rs, :] = (total[rs, :].astype(F32) + came[rs, :].astype(F32)).astype(BF16)

        tiles(n // step, part)
        copies.start(f"{name}t", came, result.at[here], core_dev)
        fetch(came, result.at[here])

    wide = slice(None)

    def down_at(side, part=None):
        start, n = side * units + k * uh, uh
        if part is not None:
            start, n = start + part * (uh // 2), uh // 2
        return (at(start, n), wide)

    def dense_at(side, part=None):
        start, n = side * HD + k * dh, dh
        if part is not None:
            start, n = start + part * (dh // 2), dh // 2
        return (at(start, n), wide)

    def up_at(side, part=None):
        taken = wide if part is None else at(part * (wid // 2), wid // 2)
        return (taken, at(side * units + k * uh, uh))

    def qkv_at(side, part=None):
        taken = wide if part is None else at(part * (wid // 2), wid // 2)
        return (taken, at(side * heads + k * hh, hh))

    chain_wait("g", 3)
    both_tiles = tuple(range(len(down_tiles)))
    down_give(0, DUP.at[pl.ds(0, uh), :], both_tiles)
    down_keep(0, both_tiles)
    give_u, keep_u = at((1 - k) * uh, uh), at(k * uh, uh)

    def hidden_back(i, side):
        block = at(i * blk, blk)
        TMP[:, at(i * uh, uh)] = dot(
            G[block, side * wid : (side + 1) * wid], WN[give_u, side * wid : (side + 1) * wid], NT
        )


    chain_wait("h", 1)
    chain_send("h", 2, G, near_part)
    fetch_n.wait()
    tiles(cols, lambda i: hidden_back(i, 0))
    chain_wait("i", 1)
    chain_send("i", 2, G, far_part)
    fetch_q.wait()
    wq_on()
    chain_wait("h", 2)
    chain_send("h", 3, G, near_part)
    wq_done()

    def qkv_block(i):
        block = at(i * blk, blk)
        for j in range(3):
            bias = row_of(qkv_b[at(r * heads + j * HD, HD)])
            value = dot(OUTP[block, :], WQ[:, j * HD : (j + 1) * HD], NN) + bias
            if j < 2:
                value = rotate(value, block, 1.0)
            QKV[block, j * HD : (j + 1) * HD] = value.astype(BF16)

    tiles(cols, qkv_block)
    chain_wait("i", 2)
    chain_send("i", 3, G, far_part)

    def key_range(i):
        low = max(0, i - 2) * blk
        return slice(i * blk, (i + 1) * blk), slice(low, (i + 1) * blk), low

    def block_scores(i):
        mine, span, low = key_range(i)
        n = span.stop - low
        s = dot(QKV[mine, 0:HD], QKV[span, HD : 2 * HD], NT) * scale
        row_id = lax.broadcasted_iota(jnp.int32, (blk, n), 0) + i * blk
        col_id = lax.broadcasted_iota(jnp.int32, (blk, n), 1) + low
        same = STAT[mine, 3:4] == seg_row[:, span]
        return jnp.where(same & (col_id <= row_id), s, -1e30)

    for i in range(cols):
        mine, span, low = key_range(i)
        s = block_scores(i)
        largest = jnp.max(s, axis=1, keepdims=True)
        p = jnp.exp(s - largest)
        total = jnp.sum(p, axis=1, keepdims=True)
        STAT[mine, 2:3] = largest + jnp.log(total)
        p_low = (p / total).astype(BF16)
        ATT[mine, :] = dot(p_low, QKV[span, 2 * HD :], NN).astype(BF16)
    out_grad("de0", 0, ATT, att_keep, att_send, A_de.at[0], S_de.at[0])
    fetch_d.wait()

    def branch_block(b, side):
        def part(j):
            cs = at(side * wid + j * TILE, TILE)
            both = dot(ATT[rows(b), :], WD[:, cs], NN) + dot(HID[rows(b), :], WN[:, cs], NN)
            OUTP[rows(b), cs] = both.astype(BF16)

        tiles(wid // TILE, part)

    branch_block(col_of[2], 0)
    out_keep("de0", 0, ATT, att_keep, S_de.at[0])
    copies.start("de0x", S_de.at[0], X_de, x_dev)
    branch_block(col_of[3], 0)

    chain_wait("h", 3)
    down_give(1, DUP.at[pl.ds(uh, uh), :], both_tiles[:1])
    at_end, between = lax.rem(c, 3) == 0, lax.rem(c, 3) != 0

    def own_near(name, when):
        copies.start(
            name, OUTP.at[rows(col_of[1]), own], OZ1.at[:, own], {"col": col_of[1]}, when
        )

    for s in (1, 0):
        branch_block(col_of[s], 0)
    down_keep(1, both_tiles[:1])
    chain_wait("i", 3)
    own_near("oa1", at_end)
    down_give(1, DUP.at[pl.ds(uh, uh), :], both_tiles[1:])
    out_grad("de1", 1, ATT, att_keep, att_send, A_de.at[1], S_de.at[1])
    wn_on()
    down_keep(1, both_tiles[1:])
    halves["dn1"] = (S_dn.at[1, at(hi * (uh // 2), uh // 2), :], V_dn)
    out_keep("de1", 1, ATT, att_keep, S_de.at[1])
    cross("de1", S_de.at[1], dh, V_de)
    own_near("oc1", between)
    wn_done()
    copies.start("oa2", OUTP.at[rows(col_of[2]), own], OZ2.at[:, own], {"col": col_of[2]})

    copies.sent(*[f"dn{side}a{i}" for side in (0, 1) for i in both_tiles])

    def up_grad_give(i):
        block = at(i * blk, blk)
        back = TMP[:, at(i * uh, uh)] + dot(G[block, other], WN[give_u, other], NT)
        DUP[block, give_u] = (back * SLOPE[block, give_u].astype(F32)).astype(BF16)

    def up_grad_keep(i):
        block = at(i * blk, blk)
        back = dot(G[block, :], WN[keep_u, :], NT)
        DUP[block, keep_u] = (back * SLOPE[block, keep_u].astype(F32)).astype(BF16)

    tiles(cols, up_grad_give)
    keep_h, give_h = at(k * hh, hh), at((1 - k) * hh, hh)

    def in_give(name, side, right_ref, give, staged, landing):
        def part(i):
            rs = at(i * TILE, TILE)
            lefts = N[:, at(side * wid + i * TILE, TILE)]
            staged[rs, :] = dot(lefts, right_ref[:, give], TN).astype(BF16)

        tiles(wid // TILE, part)
        copies.start(f"{name}{side}a", staged, landing.at[side], core_dev)

    def in_keep(name, side, right_ref, keep, landing, crossing=None):
        copies.came(f"{name}{side}a")
        n = wid // 2

        def part(i):
            rs = at(i * n, n)
            mine = dot(N[:, at(side * wid + i * n, n)], right_ref[:, keep], TN)
            landing[side, rs, :] = (mine + landing[side, rs, :].astype(F32)).astype(BF16)

        if crossing is None:
            tiles(2, part)
        else:
            part(1 - hi)
            crossing()
            part(hi)

    in_give("up", 1, DUP, give_u, SLOPE.at[:, give_u], S_up)
    tiles(cols, up_grad_keep)
    wd_on()
    in_keep("up", 1, DUP, keep_u, S_up, lambda: cross("up1", S_up.at[1], wid, V_up))
    wd_done()
    branch_block(col_of[3], 1)
    copies.start("oy3", OUTP.at[rows(col_of[3]), other], OY.at[1], y_dev)
    for i in range(cols):
        mine = slice(i * blk, (i + 1) * blk)
        DAT[mine, :] = dot(G[mine, :], WD[...], NT).astype(BF16)
    BQ[q, 2:3, :] = jnp.sum(G[:, own].astype(F32), axis=0, keepdims=True)

    copies.sent(*[f"{t}{w}{s}" for t in "ghi" for w in "ud" for s in (1, 2, 3)])
    pl.semaphore_signal(credit.at[0], inc=1, device_id=x_dev, device_id_type=MESH)
    pl.semaphore_signal(credit.at[1], inc=1, device_id=y_dev, device_id_type=MESH)
    low, high = pl.ds(0, wid // 2), pl.ds(wid // 2, wid // 2)
    X_up, R_up = G.at[:, pl.ds(0, uh)], G.at[high, pl.ds(uh, uh)]
    X_qk = WN.at[:, pl.ds(0, hh)]
    V_qk, R_qk = WN.at[low, pl.ds(hh, hh)], WN.at[high, pl.ds(hh, hh)]

    in_give("up", 0, DUP, give_u, SLOPE.at[:, keep_u], S_up)
    crossed("dn1", R_dn, both_tiles)
    branch_block(col_of[2], 1)
    copies.start("ob2", OUTP.at[rows(col_of[2]), other], OZ2.at[:, other], {"col": col_of[2]})
    in_keep("up", 0, DUP, keep_u, S_up)
    pl.semaphore_wait(credit.at[0], 1)
    copies.start("up0x", S_up.at[0], X_up, x_dev)

    branch_block(col_of[1], 1)
    copies.start("ob1", OUTP.at[rows(col_of[1]), other], OZ1.at[:, other], {"col": col_of[1]})
    branch_block(col_of[0], 1)
    crossed("de1", R_de)
    copies.sent("wnc")
    pl.semaphore_signal(credit.at[2], inc=1, device_id=x_dev, device_id_type=MESH)
    pl.semaphore_signal(credit.at[3], inc=1, device_id=y_dev, device_id_type=MESH)
    pl.semaphore_signal(credit.at[4], inc=1, device_id=y_dev, device_id_type=MESH)

    def out_block():
        b = col_of[3]
        copies.came("oy3")

        def part(i):
            rs = at(b * blk + i * sub, sub)
            came = OY[1, at(i * sub, sub), :]
            OUTP[rs, own] = (OUTP[rs, own].astype(F32) + came.astype(F32)).astype(BF16)

        tiles(blk // sub, part)
        copies.start("oz3", OUTP.at[rows(b), own], OZ3, {"col": b})

    def again(i):
        rs = at(i * sub, sub)
        normal = (X[rs, :].astype(F32) - STAT[rs, 0:1]) * STAT[rs, 1:2]
        N[rs, :] = (normal * NV[0:1, :] + NV[1:2, :]).astype(BF16)

    tiles(rows_all // sub, again)
    TMP[...] = jnp.zeros_like(TMP)
    for i in range(cols):
        mine, span, low = key_range(i)
        query = QKV[mine, 0:HD]
        p = jnp.exp(block_scores(i) - STAT[mine, 2:3])
        d_p = dot(DAT[mine, :], QKV[span, 2 * HD :], NT)
        delta = jnp.sum(d_p * p, axis=1, keepdims=True)
        d_s = (p * (d_p - delta)).astype(BF16)
        p_low = p.astype(BF16)
        d_query = dot(d_s, QKV[span, HD : 2 * HD], NN) * scale
        QKV[mine, 0:HD] = rotate(d_query, mine, -1.0).astype(BF16)
        for j in range(low // blk, i + 1):
            js = slice(j * blk - low, (j + 1) * blk - low)
            ks, vs = slice(j * HD, (j + 1) * HD), slice((cols + j) * HD, (cols + j + 1) * HD)
            TMP[:, ks] += dot(d_s[:, js], query, TN)
            TMP[:, vs] += dot(p_low[:, js], DAT[mine, :], TN)
    for j in range(cols):
        mine = slice(j * blk, (j + 1) * blk)
        ks, vs = slice(j * HD, (j + 1) * HD), slice((cols + j) * HD, (cols + j + 1) * HD)
        QKV[mine, HD : 2 * HD] = rotate(TMP[:, ks] * scale, mine, -1.0).astype(BF16)
        QKV[mine, 2 * HD :] = TMP[:, vs].astype(BF16)

    copies.sent("up0a", "up1a")
    in_give("qk", 1, QKV, give_h, SLOPE.at[:, pl.ds(hh, hh)], S_qk)
    in_give("qk", 0, QKV, give_h, SLOPE.at[:, pl.ds(0, hh)], S_qk)
    pl.semaphore_wait(credit.at[1], 1)
    crossed("up1", R_up)
    pl.semaphore_wait(credit.at[2], 1)
    in_keep("qk", 1, QKV, keep_h, S_qk, lambda: cross("qk1", S_qk.at[1], wid, V_qk))
    in_keep("qk", 0, QKV, keep_h, S_qk)
    copies.start("qk0x", S_qk.at[0], X_qk, x_dev)

    def gather_dp(name, slots):
        for word, device in (("c", core_dev), ("x", x_dev), ("d", far_dev)):
            copies.start(f"{name}{word}", slots.at[q], slots.at[q], device)

    def gathered_dp(name, slots):
        for word in "cxd":
            copies.came(f"{name}{word}")
        return slots[0] + slots[1] + slots[2] + slots[3]

    BQ[q, 0:1, :] = jnp.sum(DUP[...].astype(F32), axis=0, keepdims=True)
    BQ[q, 1:2, 0:heads] = jnp.sum(QKV[...].astype(F32), axis=0, keepdims=True)
    BQ[q, 1:2, heads:] = jnp.zeros((1, wid - heads), F32)
    BQ[q, 3:8, :] = jnp.zeros((5, wid), F32)
    gather_dp("b", BQ)

    NSUM[...] = jnp.zeros_like(NSUM)
    pl.semaphore_wait(credit.at[4], 1)

    def norm_back(b):
        rb = rows(b)
        mean, inv = STAT[rb, 0:1], STAT[rb, 1:2]

        def first(j, carry):
            along, plain = carry
            cs = at(j * TILE, TILE)
            one = dot(QKV[rb, :], WQ[cs, :], NT)
            two = dot(DUP[rb, :], WU[cs, :], NT)
            normal = (X[rb, cs].astype(F32) - mean) * inv
            NSUM[0:1, cs] += jnp.sum(one * normal, axis=0, keepdims=True)
            NSUM[1:2, cs] += jnp.sum(one, axis=0, keepdims=True)
            NSUM[2:3, cs] += jnp.sum(two * normal, axis=0, keepdims=True)
            NSUM[3:4, cs] += jnp.sum(two, axis=0, keepdims=True)
            grad = one * NV[0:1, cs] + two * NV[2:3, cs]
            TMP[:, cs] = grad
            along = along + jnp.sum(grad * normal, axis=1, keepdims=True)
            plain = plain + jnp.sum(grad, axis=1, keepdims=True)
            return along, plain

        zero = jnp.zeros((blk, 1), F32)
        along, plain = lax.fori_loop(0, width // TILE, first, (zero, zero))
        along, plain = along * (1.0 / width), plain * (1.0 / width)

        def second(j):
            cs = at(j * TILE, TILE)
            normal = (X[rb, cs].astype(F32) - mean) * inv
            N[rb, cs] = (inv * (TMP[:, cs] - plain - normal * along)).astype(BF16)

        tiles(width // TILE, second)

    EY = [HID.at[pl.ds(j * blk, blk), :] for j in range(3)]
    pl.semaphore_wait(credit.at[3], 1)
    for s in (2, 3):
        norm_back(col_of[s])
        copies.start(f"ey{s}", N.at[rows(col_of[s]), other], EY[s - 1], y_dev)
        if s == 2:
            out_block()
            spread_out("dn1", R_dn, g_down, down_at(1 - r, hi))
        else:
            spread_out("de1", R_de, g_dense, dense_at(1 - r, hi))
    norm_back(col_of[1])
    copies.start(
        "ezb", N.at[rows(col_of[1]), other], DZ1.at[:, other], {"col": col_of[1]}
    )
    norm_back(col_of[0])
    SMO[0:4, :] = NSUM[0:4, other]
    copies.start("sy", SMO, SMR, y_dev)

    def mine_at(i):
        return at(c * blk + i * sub, sub)

    def row_rest(buf, names, whole, landing, name):
        for arrival, when in names:
            copies.came(arrival, when)

        def part(i):
            rs = at(i * sub, sub)
            total = buf[mine_at(i), other].astype(F32)
            for ref in whole:
                total = total + ref[rs, other].astype(F32)
            buf[mine_at(i), other] = total.astype(BF16)

        tiles(blk // sub, part)
        copies.start(name, buf.at[rows(c), other], landing, y_dev)

    def total_of(i, buf, whole, parts):
        rs = at(i * sub, sub)
        total = buf[mine_at(i), own].astype(F32)
        for ref in whole:
            total = total + ref[rs, own].astype(F32)
        for ref in parts:
            total = total + ref[rs, :].astype(F32)
        return total

    def x_block(s):
        b = col_of[s]
        copies.came(f"ey{s}")

        def part(i):
            rs = at(b * blk + i * sub, sub)
            came = EY[s - 1][at(i * sub, sub), :]
            N[rs, own] = (N[rs, own].astype(F32) + came.astype(F32)).astype(BF16)

        tiles(blk // sub, part)
        copies.start(
            f"ea{s}", N.at[rows(b), own], DZ.at[s - 2], {"col": col_of[1]}, at_end
        )

    def x_pass(s):
        b = col_of[s]
        copies.came(f"ea{5 - s}", between)

        @pl.when(between)
        def _():
            def part(i):
                rs = at(b * blk + i * sub, sub)
                came = DZ[3 - s, at(i * sub, sub), :]
                N[rs, own] = (N[rs, own].astype(F32) + came.astype(F32)).astype(BF16)

            tiles(blk // sub, part)

        copies.start(f"eb{s}", N.at[rows(b), own], DZ.at[2], {"col": b}, between)

    row_rest(
        OUTP,
        (("oa1", between), ("oc1", at_end), ("oa2", None), ("ob1", None), ("ob2", None)),
        (OZ1, OZ2),
        OY.at[0],
        "oy0",
    )
    spread_out("up1", R_up, g_up, up_at(1 - r, hi))
    finish("dn0", S_dn.at[0], X_dn, g_down, down_at(r), both_tiles)
    finish("de0", S_de.at[0], X_de, g_dense, dense_at(r))
    finish("up0", S_up.at[0], X_up, g_up, up_at(r))
    crossed("qk1", R_qk)
    x_block(2)
    copies.came("sy")
    NZ[c, 0:4, :] = NSUM[0:4, own] + SMR[0:4, :]
    for s in (1, 2, 3):
        copies.start(f"sz{s}", NZ.at[c], NZ.at[c], {"col": col_of[s]})
    x_block(3)
    copies.start("eza", N.at[rows(col_of[1]), own], DZ1.at[:, own], {"col": col_of[1]})
    BS[...] = gathered_dp("b", BQ)
    copies.start("by", BS, BR, y_dev)
    row_rest(N, (("ezb", None),), (DZ1,), EY[0], "ey0")
    x_pass(3)
    finish("qk0", S_qk.at[0], X_qk, g_qkv, qkv_at(r))
    pass_quarter("dn1", g_down, down_at(1 - r, 1 - hi))
    x_pass(2)
    for s in (1, 2, 3):
        copies.came(f"sz{s}")
    NQ[q] = NZ[0] + NZ[1] + NZ[2] + NZ[3]
    gather_dp("n", NQ)
    pass_quarter("de1", g_dense, dense_at(1 - r, 1 - hi))
    spread_out("qk1", R_qk, g_qkv, qkv_at(1 - r, hi))
    for name in ("oz3", "oy0"):
        copies.came(name)

    def out_last(i):
        total = total_of(i, OUTP, (OZ1, OZ2), (OZ3, OY.at[0]))
        total = total + X[mine_at(i), own].astype(F32)
        out[at(i * sub, sub), :] = (total + row_of(dense_b[...] + down_b[...])).astype(BF16)

    tiles(blk // sub, out_last)
    fetch(out, out_hbm)
    pass_quarter("up1", g_up, up_at(1 - r, 1 - hi))
    copies.came("by")
    small[0:8, :] = BS[...]
    small[8:16, :] = BR[...]
    small[4:8, :] = gathered_dp("n", NQ)[0:4]
    fetch(small, small_hbm)
    copies.came("eza")
    copies.came("eb2", at_end)
    copies.came("eb3", between)
    copies.came("ey0")

    def x_last(i):
        total = total_of(i, N, (DZ1,), (DZ.at[2], EY[0]))
        in_grad[at(i * sub, sub), :] = COT[at(i * sub, sub), :].astype(F32) + total

    tiles(blk // sub, x_last)
    fetch(in_grad, in_grad_hbm)
    pass_quarter("qk1", g_qkv, qkv_at(1 - r, 1 - hi))
    for name in ("dn0", "de0", "up0", "qk0"):
        copies.came(f"{name}t")
    for name in ("dn1", "de1", "up1", "qk1"):
        copies.came(f"{name}t")
        copies.came(f"{name}f")
    for copy in local[7:]:
        copy.wait()
    copies.sent_all()


def scratch(blk, wid, cols, units, heads):
    tokens, width = blk * cols, 2 * wid
    low = [
        (tokens, width), (tokens, width), (width, heads), (width, units), (HD, width),
        (units, width), (tokens, width),
    ]
    V = pltpu.VMEM
    return (
        [V((blk, wid), BF16), V((blk, wid), F32), V((16, wid), F32)]
        + [V(shape, BF16) for shape in low]
        + [V((tokens, 128), F32)]
        + [
            V(shape, BF16)
            for shape in (
                (tokens, heads), (tokens, HD), (tokens, units), (tokens, units), (tokens, units),
                (tokens, HD), (tokens, width), (blk, width), (blk, width), (blk, wid),
                (2, blk, wid), (blk, width), (3, blk, wid), (blk, wid),
                (2, units // 2, wid), (2, HD // 2, wid), (2, wid, units // 2), (2, wid, heads // 2),
                (units // 4, wid), (HD // 4, wid), (units // 4, wid), (HD // 4, wid),
                (wid // 2, units // 2),
                (units // 2, wid), (HD // 2, wid), (2, HD // 2, wid),
            )
        ]
        + [
            V((blk, width), F32),
            V((8, width), F32),
            V((tokens, 128), F32),
            V((tokens, 128), F32),
            V((8, width), F32),
            V((8, wid), F32),
            V((8, wid), F32),
            V((cols, 8, wid), F32),
            V((4, 8, wid), F32),
            V((4, 8, wid), F32),
            V((8, wid), F32),
            V((8, wid), F32),
            pltpu.SemaphoreType.DMA((120,)),
            pltpu.SemaphoreType.DMA((120,)),
            pltpu.SemaphoreType.DMA((20,)),
            pltpu.SemaphoreType.REGULAR((5,)),
        ]
    )


def widen_kernel(*refs):
    given, results = refs[:7], refs[7:]
    small = given[6]
    for source, target in zip(given[:6], results[:6]):
        target[...] = source[...].astype(target.dtype)

    @pl.when(pl.program_id(0) == 0)
    def _():
        gain1, bias1, gain2, bias2, qkv_sum, dense_sum, up_sum, down_sum = results[6:]
        for j, ref in enumerate((gain1, bias1, gain2, bias2)):
            ref[...] = small[4 + j]
        dense_sum[...] = small[2]
        down_sum[...] = small[2]
        r = lax.axis_index("row")
        for ref, index in ((up_sum, 0), (qkv_sum, 1)):
            n = ref.shape[0] // 2
            ref[at(r * n, n)] = small[index, 0:n]
            ref[at((1 - r) * n, n)] = small[8 + index, 0:n]


def swap(value, axis, mask):
    size = lax.axis_size(axis)
    return lax.ppermute(value, axis, [(i, i ^ mask) for i in range(size)])


def shards(
    hidden_in,
    segment,
    norm1_gain,
    norm1_bias,
    norm2_gain,
    norm2_bias,
    qkv_weight,
    qkv_bias,
    dense_weight,
    dense_bias,
    up_weight,
    up_bias,
    down_weight,
    down_bias,
    cotangent,
):
    blk, wid = hidden_in.shape
    cols = lax.axis_size("col")
    heads, units = qkv_weight.shape[1] // 2, up_weight.shape[1] // 2
    vectors = (
        norm1_gain, norm1_bias, norm2_gain, norm2_bias, qkv_bias, up_bias, dense_bias, down_bias,
    )
    vmem = pl.BlockSpec(memory_space=pltpu.VMEM)
    far = pl.BlockSpec(memory_space=pl.ANY)
    shape = jax.ShapeDtypeStruct
    out, in_grad, small, g_qkv, g_dense, g_up, g_down = pl.pallas_call(
        functools.partial(step_kernel, (blk, wid, cols)),
        out_shape=(
            shape((blk, wid), BF16),
            shape((blk, wid), F32),
            shape((16, wid), F32),
            shape(qkv_weight.shape, BF16),
            shape(dense_weight.shape, BF16),
            shape(up_weight.shape, BF16),
            shape(down_weight.shape, BF16),
        ),
        in_specs=[far] * 6 + [vmem] * 9,
        out_specs=(far,) * 7,
        scratch_shapes=scratch(blk, wid, cols, units, heads),
        compiler_params=pltpu.CompilerParams(
            collective_id=0, has_side_effects=True, vmem_limit_bytes=67043328
        ),
        name="step",
    )(
        hidden_in, cotangent, qkv_weight, up_weight, dense_weight, down_weight, segment, *vectors
    )

    grads = (g_qkv, g_dense, g_up, g_down)
    mask = 4
    while mask < lax.axis_size("dp"):
        grads = tuple(
            (g.astype(F32) + swap(g, "dp", mask).astype(F32)).astype(BF16) for g in grads
        )
        small = small + swap(small, "dp", mask)
        mask *= 2
    steps = 4

    def cut(array):
        rows, columns = array.shape
        return pl.BlockSpec((rows // steps, columns), lambda i: (i, 0))

    def whole(n):
        return pl.BlockSpec((n,), lambda i: (0,))

    lengths = [wid] * 4 + [2 * heads, wid, 2 * units, wid]
    widened = pl.pallas_call(
        widen_kernel,
        grid=(steps,),
        out_shape=[shape(out.shape, BF16), shape(in_grad.shape, F32)]
        + [shape(g.shape, F32) for g in grads]
        + [shape((n,), F32) for n in lengths],
        in_specs=[cut(out), cut(in_grad)]
        + [cut(g) for g in grads]
        + [pl.BlockSpec(small.shape, lambda i: (0, 0))],
        out_specs=[cut(out), cut(in_grad)] + [cut(g) for g in grads] + [whole(n) for n in lengths],
        compiler_params=pltpu.CompilerParams(vmem_limit_bytes=60 << 20),
        name="widen",
    )(out, in_grad, *grads, small)
    out, in_grad, d_qkv, d_dense, d_up, d_down, *sums = widened
    return (
        out,
        in_grad,
        sums[0],
        sums[1],
        sums[2],
        sums[3],
        d_qkv,
        sums[4],
        d_dense,
        sums[5],
        d_up,
        sums[6],
        d_down,
        sums[7],
    )


def solution(mesh):
    return jax.shard_map(
        shards,
        mesh=mesh,
        in_specs=(
            P(("dp", "col"), "row"),
            P("dp", None),
            P("row"),
            P("row"),
            P("row"),
            P("row"),
            P("row", "col"),
            P("col"),
            P("col", "row"),
            P("row"),
            P("row", "col"),
            P("col"),
            P("col", "row"),
            P("row"),
            P(("dp", "col"), "row"),
        ),
        out_specs=(
            P(("dp", "col"), "row"),
            P(("dp", "col"), "row"),
            P("row"),
            P("row"),
            P("row"),
            P("row"),
            P("row", "col"),
            P("col"),
            P("col", "row"),
            P("row"),
            P("row", "col"),
            P("col"),
            P("col", "row"),
            P("row"),
        ),
        check_vma=False,
    )
```

```python
import functools
import math

import jax
import jax.numpy as jnp
from jax import lax
from jax.experimental import pallas as pl
from jax.experimental.pallas import tpu as pltpu
from jax.sharding import PartitionSpec as P

HD = 256
ROT = 64
F32 = jnp.float32
BF16 = jnp.bfloat16
MESH = pl.DeviceIdType.MESH

eps_norm = 1e-05
rope_base = 10000.0
TILE = 512
NN = (((1,), (0,)), ((), ()))
NT = (((1,), (1,)), ((), ()))
TN = (((0,), (0,)), ((), ()))


def dot(left, right, dims):
    return lax.dot_general(left, right, dims, preferred_element_type=F32)


class Copies:
    def __init__(self, send_sem, recv_sem):
        self.send_sem, self.recv_sem = send_sem, recv_sem
        self.made, self.open, self.free, self.slot = {}, {}, [], {}
        self.used = 0

    def start(self, name, source, target, device, when=None):
        if self.free:
            slot = self.free.pop(0)
        else:
            slot, self.used = self.used, self.used + 1
        index = len(self.made)
        self.slot[name] = slot
        copy = pltpu.make_async_remote_copy(
            src_ref=source,
            dst_ref=target,
            send_sem=self.send_sem.at[slot],
            recv_sem=self.recv_sem.at[index],
            device_id=device,
            device_id_type=MESH,
        )
        self.made[name] = copy
        self.open[name] = when
        guarded(when, copy.start)

    def came(self, name, when=None):
        guarded(when, self.made[name].wait_recv)

    def sent(self, *names):
        for name in names:
            guarded(self.open.pop(name), self.made[name].wait_send)
            self.free.append(self.slot[name])

    def sent_all(self):
        self.sent(*list(self.open))


def guarded(when, action):
    if when is None:
        action()
    else:
        pl.when(when)(action)


def row_of(vector):
    return vector.reshape(1, vector.shape[0])


def at(start, size):
    return pl.ds(pl.multiple_of(start, size), size)


def tiles(count, body):
    lax.fori_loop(0, count, lambda i, carry: (body(i), carry)[1], 0)


def step_kernel(
    sizes,
    hid, cot, wq, wu, wd, wn, seg, gain1, bias1, gain2, bias2, qkv_b, up_b, dense_b, down_b,
    out, in_grad, small, G, WN, WU, g_dense,
    X, WQ, WD, N, STAT, QKV, ATT, HID, SLOPE, DUP, DAT, OUTP, OZ1, OZ2, OZ3, OY, DZ1, DZ,
    S_dn, S_de, S_up, S_qk, R_dn, R_de, V_dn, V_de, V_up, X_dn, X_de, TMP, NV, COS, SIN, NSUM, SMO, SMR, NZ, NQ, BQ, BS, BR,
    send_sem, recv_sem, local_sem, credit,
):
    blk, wid, cols = sizes
    rows_all = blk * cols
    width = 2 * wid
    heads, units = WQ.shape[1], WU.shape[1]
    hh, uh, dh = heads // 2, units // 2, HD // 2
    r = lax.axis_index("row")
    c = lax.axis_index("col")
    dp = lax.axis_index("dp")
    k = lax.rem(dp, 2)
    hi = lax.rem(lax.div(dp, 2), 2)
    q = k + 2 * hi
    core_dev = {"dp": dp + 1 - 2 * k}
    x_dev = {"dp": dp + 2 - 4 * hi}
    far_dev = {"dp": dp + 3 - 2 * k - 4 * hi}
    y_dev = {"row": 1 - r}
    c_low, c_high = lax.rem(c, 2), lax.div(c, 2)
    col_of = [c, c + 1 - 2 * c_low, c + 2 - 4 * c_high, 3 - c]
    own, other = pl.ds(0, wid), pl.ds(wid, wid)
    scale = 1.0 / math.sqrt(HD)
    copies = Copies(send_sem, recv_sem)

    barrier = pltpu.get_barrier_semaphore()
    for device in (core_dev, x_dev, y_dev):
        pl.semaphore_signal(barrier, inc=1, device_id=device, device_id_type=MESH)
    for move, inside in ((1, c < cols - 1), (-1, c >= 1)):

        @pl.when(inside)
        def _():
            pl.semaphore_signal(
                barrier, inc=1, device_id={"col": c + move}, device_id_type=MESH
            )

    local = []

    def fetch(source, target):
        copy = pltpu.make_async_copy(source, target, local_sem.at[len(local)])
        copy.start()
        local.append(copy)
        return copy

    fetch_x = fetch(hid, X.at[at(c * blk, blk), own])
    fetch_g = fetch(cot, G.at[at(c * blk, blk), own])
    fetch_u = fetch(wu.at[:, at(r * units, units)], WU.at[own, :])
    fetch_q = fetch(wq.at[:, at(r * heads, heads)], WQ.at[own, :])
    fetch_n = fetch(wn.at[at(r * units, units), :], WN.at[:, own])
    fetch_d = fetch(wd.at[at(r * HD, HD), :], WD.at[:, own])
    pl.semaphore_wait(
        barrier, 3 + (c < cols - 1).astype(jnp.int32) + (c >= 1).astype(jnp.int32)
    )

    def rows(b):
        return at(b * blk, blk)

    def chain_send(tag, step, buf, columns, first=None):
        for word, move, edge in (("u", 1, c < cols - 1), ("d", -1, c >= 1)):
            block = c - move * (step - 1)
            valid = edge & (block >= 0) & (block <= cols - 1)
            source = first if first is not None else buf.at[rows(block), columns]
            copies.start(
                f"{tag}{word}{step}", source, buf.at[rows(block), columns], {"col": c + move}, valid
            )

    def chain_wait(tag, step):
        copies.came(f"{tag}u{step}", c >= step)
        copies.came(f"{tag}d{step}", c + step <= cols - 1)

    def row_send(name, s):
        b = col_of[s]
        copies.start(name, X.at[rows(b), own], X.at[rows(b), other], y_dev)

    q2 = q + 2 - 4 * hi

    def weight(name, source, full, row0, size, columns, spread):
        share = q if spread else k

        def place(index):
            return full.at[at(row0 + index * size, size), columns]

        copies.start(f"{name}y", source(at(share * size, size)), place(share), y_dev)

        def pass_on():
            copies.came(f"{name}y")
            if spread:
                copies.start(f"{name}x", place(q), place(q), x_dev)
            copies.start(f"{name}c", place(share), place(share), core_dev)

        def pass_far():
            copies.came(f"{name}x")
            copies.start(f"{name}f", place(q2), place(q2), core_dev)

        def done():
            copies.came(f"{name}c")
            if spread:
                copies.came(f"{name}f")

        return pass_on, pass_far, done

    everything = slice(None)
    chain_send("x", 1, X, own, hid)
    copies.start("xy0", hid, X.at[rows(c), other], y_dev)
    for j, vector in enumerate((gain1, bias1, gain2, bias2)):
        NV[j : j + 1, own] = row_of(vector[...])
    NV[4:8, own] = jnp.zeros((4, wid), F32)
    copies.start("nv", NV.at[:, own], NV.at[:, other], y_dev)
    wu_on, wu_far, wu_done = weight(
        "wu", lambda rs: wu.at[rs, at((1 - r) * units, units)], WU, wid, wid // 4, everything, True
    )

    seg_row = seg[...].astype(F32)
    seg_col = jnp.transpose(jnp.broadcast_to(seg_row, (128, rows_all)))
    STAT[:, 3:4] = seg_col[:, 0:1]

    def table(i):
        block = at(i * blk, blk)
        starts = jnp.sum(
            (seg_row < STAT[block, 3:4]).astype(F32), axis=1, keepdims=True
        )
        index = lax.broadcasted_iota(jnp.int32, (blk, 1), 0) + i * blk
        lane = lax.broadcasted_iota(jnp.int32, (1, 128), 1)
        turn = jnp.exp(
            lax.rem(lane, ROT // 2).astype(F32) * (-2.0 * math.log(rope_base) / ROT)
        )
        angles = (index.astype(F32) - starts) * turn
        COS[block, :] = jnp.where(lane < ROT, jnp.cos(angles), 1.0)
        SIN[block, :] = jnp.where(
            lane < ROT // 2, -jnp.sin(angles), jnp.where(lane < ROT, jnp.sin(angles), 0.0)
        )

    tiles(cols, table)

    def rotate(head, block, sign):
        first = head[:, :128]
        lane = lax.broadcasted_iota(jnp.int32, first.shape, 1)
        swapped = jnp.where(
            lane < ROT // 2, pltpu.roll(first, 128 - ROT // 2, 1), pltpu.roll(first, ROT // 2, 1)
        )
        turned = first * COS[block, :] + sign * (swapped * SIN[block, :])
        return jnp.concatenate([turned, head[:, 128:]], axis=1)

    sub = 64

    def norm_block(b):
        def part(i):
            rs = at(b * blk + i * sub, sub)
            x = X[rs, :].astype(F32)
            mean = jnp.sum(x, axis=1, keepdims=True) * (1.0 / width)
            square = jnp.sum(x * x, axis=1, keepdims=True) * (1.0 / width)
            inv = lax.rsqrt(square - mean * mean + eps_norm)
            STAT[rs, 0:1] = mean
            STAT[rs, 1:2] = inv
            normal = (x - mean) * inv
            OUTP[rs, :] = (normal * NV[0:1, :] + NV[1:2, :]).astype(BF16)
            N[rs, :] = (normal * NV[2:3, :] + NV[3:4, :]).astype(BF16)

        tiles(blk // sub, part)

    def up_block(b):
        def part(j):
            cs = at(j * TILE, TILE)
            bias = row_of(up_b[at(r * units + j * TILE, TILE)])
            up = dot(N[rows(b), :], WU[:, cs], NN) + bias
            cdf = 0.5 * (1.0 + lax.erf(up * (1.0 / math.sqrt(2.0))))
            HID[rows(b), cs] = (up * cdf).astype(BF16)
            SLOPE[rows(b), cs] = (
                cdf + up * jnp.exp(-0.5 * up * up) * (1.0 / math.sqrt(2.0 * math.pi))
            ).astype(BF16)

        tiles(units // TILE, part)

    fetch_x.wait()
    fetch_g.wait()
    chain_wait("x", 1)
    chain_send("x", 2, X, own)
    row_send("xy1", 1)
    chain_wait("x", 2)
    chain_send("x", 3, X, own)
    row_send("xy2", 2)
    chain_send("g", 1, G, own, cot)
    wu_on()
    copies.came("nv")
    copies.came("xy0")
    norm_block(col_of[0])
    chain_wait("x", 3)
    row_send("xy3", 3)
    copies.start("gy", cot, G.at[rows(c), other], y_dev)
    wq_on, _, wq_done = weight(
        "wq", lambda rs: wq.at[rs, at((1 - r) * heads, heads)], WQ, wid, wid // 2, everything, False
    )

    def rows_of(ref, start, rs):
        return ref.at[at(start + rs.start, rs.size), :]

    wn_on, _, wn_done = weight(
        "wn", lambda rs: rows_of(wn, (1 - r) * units, rs), WN, 0, units // 2, other, False
    )
    wd_on, _, wd_done = weight(
        "wd", lambda rs: rows_of(wd, (1 - r) * HD, rs), WD, 0, HD // 2, other, False
    )
    wu_far()
    copies.came("xy1")
    norm_block(col_of[1])
    fetch_u.wait()
    wu_done()
    up_block(col_of[0])
    up_block(col_of[1])
    chain_wait("g", 1)
    chain_send("g", 2, G, own)
    copies.came("xy2")
    norm_block(col_of[2])
    up_block(col_of[2])
    chain_wait("g", 2)
    chain_send("g", 3, G, own)
    copies.came("xy3")
    norm_block(col_of[3])
    up_block(col_of[3])
    copies.came("gy")
    near_part, far_part = pl.ds(wid, wid // 2), pl.ds(wid + wid // 2, wid // 2)
    chain_send("h", 1, G, near_part)
    chain_send("i", 1, G, far_part)

    def grad_send(name, staged, left, right, n_rows, n_cols, target):
        def part(i):
            cs = at(i * TILE, TILE)
            staged[:, cs] = dot(left(None), right(cs), TN).astype(BF16)

        tiles(n_cols // TILE, part)
        copies.start(name, staged, target, core_dev)

    hid_keep, hid_send = at(k * uh, uh), at((1 - k) * uh, uh)
    att_keep, att_send = at(k * dh, dh), at((1 - k) * dh, dh)

    def out_grad(name, side, left_ref, keep, give, staged, landing):
        base = side * wid

        def give_part(i):
            cs = at(i * TILE, TILE)
            staged[:, cs] = dot(
                left_ref[:, give], G[:, at(base + i * TILE, TILE)], TN
            ).astype(BF16)

        tiles(wid // TILE, give_part)
        copies.start(f"{name}a", staged, landing, core_dev)

    def out_keep(name, side, left_ref, keep, landing):
        base = side * wid
        copies.came(f"{name}a")

        def keep_part(i):
            cs = at(i * TILE, TILE)
            mine = dot(left_ref[:, keep], G[:, at(base + i * TILE, TILE)], TN)
            landing[:, cs] = (mine + landing[:, cs].astype(F32)).astype(BF16)

        tiles(wid // TILE, keep_part)

    down_tiles = [slice(i * TILE, (i + 1) * TILE) for i in range(wid // TILE)]

    def down_give(side, staged, which):
        for i in which:
            cs = down_tiles[i]
            part = dot(HID[:, hid_send], G[:, side * wid + i * TILE : side * wid + (i + 1) * TILE], TN)
            staged[:, cs] = part.astype(BF16)
            copies.start(f"dn{side}a{i}", staged.at[:, cs], S_dn.at[side, :, cs], core_dev)

    def down_keep(side, which):
        half_rows = uh // 2
        give = at((1 - hi) * half_rows, half_rows)
        for i in which:
            cs = down_tiles[i]
            copies.came(f"dn{side}a{i}")
            mine = dot(HID[:, hid_keep], G[:, side * wid + i * TILE : side * wid + (i + 1) * TILE], TN)
            S_dn[side, :, cs] = (mine + S_dn[side, :, cs].astype(F32)).astype(BF16)
            if side == 0:
                copies.start(f"dn0x{i}", S_dn.at[0, :, cs], X_dn.at[:, cs], x_dev)
            else:
                copies.start(f"dn1x{i}", S_dn.at[1, give, cs], V_dn.at[:, cs], x_dev)

    halves = {}

    def cross(name, total, n_rows, landing):
        half_rows = n_rows // 2
        give, keep = at((1 - hi) * half_rows, half_rows), at(hi * half_rows, half_rows)
        copies.start(f"{name}x", total.at[give, :], landing, x_dev)
        halves[name] = (total.at[keep, :], landing)

    def down_crossed(i):
        cs = down_tiles[i]
        copies.came(f"dn1x{i}")
        mine = S_dn[1, at(hi * (uh // 2), uh // 2), cs].astype(F32)
        V_dn[:, cs] = (mine + V_dn[:, cs].astype(F32)).astype(BF16)
        copies.start(f"dn1y{i}", V_dn.at[:, cs], R_dn.at[:, cs], y_dev)

    def crossed(name, target):
        mine, landing = halves[name]
        copies.came(f"{name}x")
        n = landing.shape[0]
        step = min(n, 128)

        def part(i):
            rs = at(i * step, step)
            landing[rs, :] = (mine[rs, :].astype(F32) + landing[rs, :].astype(F32)).astype(BF16)

        tiles(n // step, part)
        copies.start(f"{name}y", landing, target, y_dev)

    def spread_out(name, result, here, came=None, parts=("",)):
        for word in parts:
            copies.came(f"{name}y{word}")
        source = result.at[here] if came is None else came
        copies.start(f"{name}g", source, result.at[here], x_dev)
        copies.start(f"{name}t", source, result.at[here], core_dev)
        if came is not None:
            fetch(came, result.at[here])

    def pass_quarter(name, result, there):
        copies.came(f"{name}g")
        copies.start(f"{name}f", result.at[there], result.at[there], core_dev)

    def finish(name, total, result, here, came=None, parts=("",)):
        for word in parts:
            copies.came(f"{name}x{word}")
        landed = result.at[here] if came is None else came
        n = total.shape[0]
        step = min(n, 128)

        def part(i):
            rs = at(i * step, step)
            landed[rs, :] = (total[rs, :].astype(F32) + landed[rs, :].astype(F32)).astype(BF16)

        tiles(n // step, part)
        copies.start(f"{name}t", landed, result.at[here], core_dev)
        if came is not None:
            fetch(came, result.at[here])

    wide = slice(None)

    def down_at(side, part=None):
        start, n = side * units + k * uh, uh
        if part is not None:
            start, n = start + part * (uh // 2), uh // 2
        return (at(start, n), wide)

    def dense_at(side, part=None):
        start, n = side * HD + k * dh, dh
        if part is not None:
            start, n = start + part * (dh // 2), dh // 2
        return (at(start, n), wide)

    def up_at(side, part=None):
        taken = wide if part is None else at(part * (wid // 2), wid // 2)
        return (taken, at(side * units + k * uh, uh))

    def qkv_at(side, part=None):
        taken = wide if part is None else at(part * (wid // 2), wid // 2)
        return (taken, at(side * heads + k * hh, hh))

    chain_wait("g", 3)
    both_tiles = tuple(range(len(down_tiles)))
    down_give(0, DUP.at[pl.ds(0, uh), :], both_tiles)
    down_keep(0, both_tiles)
    give_u, keep_u = at((1 - k) * uh, uh), at(k * uh, uh)

    def hidden_back(i, side):
        block = at(i * blk, blk)
        TMP[:, at(i * uh, uh)] = dot(
            G[block, side * wid : (side + 1) * wid], WN[give_u, side * wid : (side + 1) * wid], NT
        )


    chain_wait("h", 1)
    chain_send("h", 2, G, near_part)
    fetch_n.wait()
    tiles(cols, lambda i: hidden_back(i, 0))
    chain_wait("i", 1)
    chain_send("i", 2, G, far_part)
    fetch_q.wait()
    wq_on()
    wq_done()

    def qkv_block(i):
        block = at(i * blk, blk)
        for j in range(3):
            bias = row_of(qkv_b[at(r * heads + j * HD, HD)])
            value = dot(OUTP[block, :], WQ[:, j * HD : (j + 1) * HD], NN) + bias
            if j < 2:
                value = rotate(value, block, 1.0)
            QKV[block, j * HD : (j + 1) * HD] = value.astype(BF16)

    tiles(cols, qkv_block)
    chain_wait("h", 2)
    chain_send("h", 3, G, near_part)

    def key_range(i):
        low = max(0, i - 2) * blk
        return slice(i * blk, (i + 1) * blk), slice(low, (i + 1) * blk), low

    def block_scores(i):
        mine, span, low = key_range(i)
        n = span.stop - low
        s = dot(QKV[mine, 0:HD], QKV[span, HD : 2 * HD], NT) * scale
        row_id = lax.broadcasted_iota(jnp.int32, (blk, n), 0) + i * blk
        col_id = lax.broadcasted_iota(jnp.int32, (blk, n), 1) + low
        same = STAT[mine, 3:4] == seg_row[:, span]
        return jnp.where(same & (col_id <= row_id), s, -1e30)

    for i in range(cols):
        mine, span, low = key_range(i)
        s = block_scores(i)
        largest = jnp.max(s, axis=1, keepdims=True)
        p = jnp.exp(s - largest)
        total = jnp.sum(p, axis=1, keepdims=True)
        STAT[mine, 2:3] = largest + jnp.log(total)
        p_low = (p / total).astype(BF16)
        ATT[mine, :] = dot(p_low, QKV[span, 2 * HD :], NN).astype(BF16)
    copies.sent("dn0a0", "dn0a1")
    out_grad("de0", 0, ATT, att_keep, att_send, DUP.at[pl.ds(0, dh), :], S_de.at[0])
    chain_wait("i", 2)
    chain_send("i", 3, G, far_part)
    fetch_d.wait()

    def branch_block(b, side):
        def part(j):
            cs = at(side * wid + j * TILE, TILE)
            both = dot(ATT[rows(b), :], WD[:, cs], NN) + dot(HID[rows(b), :], WN[:, cs], NN)
            OUTP[rows(b), cs] = both.astype(BF16)

        tiles(wid // TILE, part)

    branch_block(col_of[2], 0)
    out_keep("de0", 0, ATT, att_keep, S_de.at[0])
    copies.start("de0x", S_de.at[0], X_de, x_dev)
    branch_block(col_of[3], 0)

    chain_wait("h", 3)
    down_give(1, DUP.at[pl.ds(uh, uh), :], both_tiles[:1])
    at_end, between = lax.rem(c, 3) == 0, lax.rem(c, 3) != 0

    def own_near(name, when):
        copies.start(
            name, OUTP.at[rows(col_of[1]), own], OZ1.at[:, own], {"col": col_of[1]}, when
        )

    for s in (1, 0):
        branch_block(col_of[s], 0)
    down_keep(1, both_tiles[:1])
    chain_wait("i", 3)
    own_near("oa1", at_end)
    down_give(1, DUP.at[pl.ds(uh, uh), :], both_tiles[1:])
    out_grad("de1", 1, ATT, att_keep, att_send, DUP.at[pl.ds(dh, dh), :], S_de.at[1])
    down_keep(1, both_tiles[1:])
    out_keep("de1", 1, ATT, att_keep, S_de.at[1])
    cross("de1", S_de.at[1], dh, V_de)
    wn_on()
    own_near("oc1", between)
    wn_done()
    copies.start("oa2", OUTP.at[rows(col_of[2]), own], OZ2.at[:, own], {"col": col_of[2]})

    copies.sent("dn1a0", "dn1a1", "de0a", "de1a")

    def up_grad_give(i):
        block = at(i * blk, blk)
        back = TMP[:, at(i * uh, uh)] + dot(G[block, other], WN[give_u, other], NT)
        DUP[block, give_u] = (back * SLOPE[block, give_u].astype(F32)).astype(BF16)

    def up_grad_keep(i):
        block = at(i * blk, blk)
        back = dot(G[block, :], WN[keep_u, :], NT)
        DUP[block, keep_u] = (back * SLOPE[block, keep_u].astype(F32)).astype(BF16)

    tiles(cols, up_grad_give)
    down_crossed(0)
    keep_h, give_h = at(k * hh, hh), at((1 - k) * hh, hh)

    def in_give(name, side, right_ref, give, staged, landing):
        def part(i):
            rs = at(i * TILE, TILE)
            lefts = N[:, at(side * wid + i * TILE, TILE)]
            staged[rs, :] = dot(lefts, right_ref[:, give], TN).astype(BF16)

        tiles(wid // TILE, part)
        copies.start(f"{name}{side}a", staged, landing.at[side], core_dev)

    def in_keep(name, side, right_ref, keep, landing, crossing=None):
        copies.came(f"{name}{side}a")
        n = wid // 2

        def part(i):
            rs = at(i * n, n)
            mine = dot(N[:, at(side * wid + i * n, n)], right_ref[:, keep], TN)
            landing[side, rs, :] = (mine + landing[side, rs, :].astype(F32)).astype(BF16)

        if crossing is None:
            tiles(2, part)
        else:
            part(1 - hi)
            crossing()
            part(hi)

    in_give("up", 1, DUP, give_u, SLOPE.at[:, give_u], S_up)
    tiles(cols, up_grad_keep)
    wd_on()
    in_keep("up", 1, DUP, keep_u, S_up, lambda: cross("up1", S_up.at[1], wid, V_up))
    wd_done()
    branch_block(col_of[3], 1)
    copies.start("oy3", OUTP.at[rows(col_of[3]), other], OY.at[1], y_dev)
    for i in range(cols):
        mine = slice(i * blk, (i + 1) * blk)
        DAT[mine, :] = dot(G[mine, :], WD[...], NT).astype(BF16)
    BQ[q, 2:3, :] = jnp.sum(G[:, own].astype(F32), axis=0, keepdims=True)

    copies.sent(*[f"{t}{w}{s}" for t in "xghi" for w in "ud" for s in (1, 2, 3)])
    copies.sent("xy0", "xy1", "xy2", "xy3", "gy", "nv", "wuy", "wux", "wuc", "wuf", "wqy", "wqc")
    copies.sent("dn0x0", "dn0x1", "wny", "wdy", "wdc")
    pl.semaphore_signal(credit.at[0], inc=1, device_id=x_dev, device_id_type=MESH)
    pl.semaphore_signal(credit.at[1], inc=1, device_id=y_dev, device_id_type=MESH)
    pl.semaphore_signal(credit.at[5], inc=1, device_id=core_dev, device_id_type=MESH)
    V_qk = WN.at[pl.ds(0, wid // 2), pl.ds(2 * heads, hh)]

    in_give("up", 0, DUP, give_u, SLOPE.at[:, keep_u], S_up)
    down_crossed(1)
    branch_block(col_of[2], 1)
    copies.start("ob2", OUTP.at[rows(col_of[2]), other], OZ2.at[:, other], {"col": col_of[2]})
    in_keep("up", 0, DUP, keep_u, S_up)
    pl.semaphore_wait(credit.at[0], 1)
    copies.start("up0x", S_up.at[0], G.at[up_at(r)], x_dev)

    branch_block(col_of[1], 1)
    copies.start("ob1", OUTP.at[rows(col_of[1]), other], OZ1.at[:, other], {"col": col_of[1]})
    branch_block(col_of[0], 1)
    crossed("de1", R_de)
    copies.sent("wnc")
    pl.semaphore_signal(credit.at[2], inc=1, device_id=x_dev, device_id_type=MESH)
    pl.semaphore_signal(credit.at[3], inc=1, device_id=y_dev, device_id_type=MESH)
    pl.semaphore_signal(credit.at[6], inc=1, device_id=core_dev, device_id_type=MESH)
    pl.semaphore_signal(credit.at[4], inc=1, device_id=y_dev, device_id_type=MESH)

    def out_block():
        b = col_of[3]
        copies.came("oy3")

        def part(i):
            rs = at(b * blk + i * sub, sub)
            came = OY[1, at(i * sub, sub), :]
            OUTP[rs, own] = (OUTP[rs, own].astype(F32) + came.astype(F32)).astype(BF16)

        tiles(blk // sub, part)
        copies.start("oz3", OUTP.at[rows(b), own], OZ3, {"col": b})

    def again(i):
        rs = at(i * sub, sub)
        normal = (X[rs, :].astype(F32) - STAT[rs, 0:1]) * STAT[rs, 1:2]
        N[rs, :] = (normal * NV[0:1, :] + NV[1:2, :]).astype(BF16)

    tiles(rows_all // sub, again)
    TMP[...] = jnp.zeros_like(TMP)
    for i in range(cols):
        mine, span, low = key_range(i)
        query = QKV[mine, 0:HD]
        p = jnp.exp(block_scores(i) - STAT[mine, 2:3])
        d_p = dot(DAT[mine, :], QKV[span, 2 * HD :], NT)
        delta = jnp.sum(d_p * p, axis=1, keepdims=True)
        d_s = (p * (d_p - delta)).astype(BF16)
        p_low = p.astype(BF16)
        d_query = dot(d_s, QKV[span, HD : 2 * HD], NN) * scale
        QKV[mine, 0:HD] = rotate(d_query, mine, -1.0).astype(BF16)
        for j in range(low // blk, i + 1):
            js = slice(j * blk - low, (j + 1) * blk - low)
            ks, vs = slice(j * HD, (j + 1) * HD), slice((cols + j) * HD, (cols + j + 1) * HD)
            TMP[:, ks] += dot(d_s[:, js], query, TN)
            TMP[:, vs] += dot(p_low[:, js], DAT[mine, :], TN)
    for j in range(cols):
        mine = slice(j * blk, (j + 1) * blk)
        ks, vs = slice(j * HD, (j + 1) * HD), slice((cols + j) * HD, (cols + j + 1) * HD)
        QKV[mine, HD : 2 * HD] = rotate(TMP[:, ks] * scale, mine, -1.0).astype(BF16)
        QKV[mine, 2 * HD :] = TMP[:, vs].astype(BF16)

    copies.sent("up0a", "up1a")
    in_give("qk", 1, QKV, give_h, SLOPE.at[:, pl.ds(hh, hh)], S_qk)
    in_give("qk", 0, QKV, give_h, SLOPE.at[:, pl.ds(0, hh)], S_qk)
    pl.semaphore_wait(credit.at[1], 1)
    crossed("up1", G.at[up_at(r, hi)])
    pl.semaphore_wait(credit.at[2], 1)
    in_keep("qk", 1, QKV, keep_h, S_qk, lambda: cross("qk1", S_qk.at[1], wid, V_qk))
    in_keep("qk", 0, QKV, keep_h, S_qk)
    copies.start("qk0x", S_qk.at[0], WN.at[qkv_at(r)], x_dev)

    def gather_dp(name, slots):
        for word, device in (("c", core_dev), ("x", x_dev), ("d", far_dev)):
            copies.start(f"{name}{word}", slots.at[q], slots.at[q], device)

    def gathered_dp(name, slots):
        for word in "cxd":
            copies.came(f"{name}{word}")
        return slots[0] + slots[1] + slots[2] + slots[3]

    BQ[q, 0:1, :] = jnp.sum(DUP[...].astype(F32), axis=0, keepdims=True)
    BQ[q, 1:2, 0:heads] = jnp.sum(QKV[...].astype(F32), axis=0, keepdims=True)
    BQ[q, 1:2, heads:] = jnp.zeros((1, wid - heads), F32)
    BQ[q, 3:8, :] = jnp.zeros((5, wid), F32)
    gather_dp("b", BQ)

    NSUM[...] = jnp.zeros_like(NSUM)
    pl.semaphore_wait(credit.at[4], 1)

    def norm_back(b):
        rb = rows(b)
        mean, inv = STAT[rb, 0:1], STAT[rb, 1:2]

        def first(j, carry):
            along, plain = carry
            cs = at(j * TILE, TILE)
            one = dot(QKV[rb, :], WQ[cs, :], NT)
            two = dot(DUP[rb, :], WU[cs, :], NT)
            normal = (X[rb, cs].astype(F32) - mean) * inv
            NSUM[0:1, cs] += jnp.sum(one * normal, axis=0, keepdims=True)
            NSUM[1:2, cs] += jnp.sum(one, axis=0, keepdims=True)
            NSUM[2:3, cs] += jnp.sum(two * normal, axis=0, keepdims=True)
            NSUM[3:4, cs] += jnp.sum(two, axis=0, keepdims=True)
            grad = one * NV[0:1, cs] + two * NV[2:3, cs]
            TMP[:, cs] = grad
            along = along + jnp.sum(grad * normal, axis=1, keepdims=True)
            plain = plain + jnp.sum(grad, axis=1, keepdims=True)
            return along, plain

        zero = jnp.zeros((blk, 1), F32)
        along, plain = lax.fori_loop(0, width // TILE, first, (zero, zero))
        along, plain = along * (1.0 / width), plain * (1.0 / width)

        def second(j):
            cs = at(j * TILE, TILE)
            normal = (X[rb, cs].astype(F32) - mean) * inv
            N[rb, cs] = (inv * (TMP[:, cs] - plain - normal * along)).astype(BF16)

        tiles(width // TILE, second)

    EY = [HID.at[pl.ds(j * blk, blk), :] for j in range(3)]
    pl.semaphore_wait(credit.at[3], 1)
    for s in (2, 3):
        norm_back(col_of[s])
        copies.start(f"ey{s}", N.at[rows(col_of[s]), other], EY[s - 1], y_dev)
        if s == 2:
            out_block()
        else:
            spread_out("de1", g_dense, dense_at(1 - r, hi), R_de)
    norm_back(col_of[1])
    copies.start(
        "ezb", N.at[rows(col_of[1]), other], DZ1.at[:, other], {"col": col_of[1]}
    )
    norm_back(col_of[0])
    pl.semaphore_signal(credit.at[7], inc=1, device_id=core_dev, device_id_type=MESH)
    pl.semaphore_signal(credit.at[8], inc=1, device_id=x_dev, device_id_type=MESH)
    SMO[0:4, :] = NSUM[0:4, other]
    copies.start("sy", SMO, SMR, y_dev)

    def mine_at(i):
        return at(c * blk + i * sub, sub)

    def row_rest(buf, names, whole, landing, name):
        for arrival, when in names:
            copies.came(arrival, when)

        def part(i):
            rs = at(i * sub, sub)
            total = buf[mine_at(i), other].astype(F32)
            for ref in whole:
                total = total + ref[rs, other].astype(F32)
            buf[mine_at(i), other] = total.astype(BF16)

        tiles(blk // sub, part)
        copies.start(name, buf.at[rows(c), other], landing, y_dev)

    def total_of(i, buf, whole, parts):
        rs = at(i * sub, sub)
        total = buf[mine_at(i), own].astype(F32)
        for ref in whole:
            total = total + ref[rs, own].astype(F32)
        for ref in parts:
            total = total + ref[rs, :].astype(F32)
        return total

    def x_block(s):
        b = col_of[s]
        copies.came(f"ey{s}")

        def part(i):
            rs = at(b * blk + i * sub, sub)
            came = EY[s - 1][at(i * sub, sub), :]
            N[rs, own] = (N[rs, own].astype(F32) + came.astype(F32)).astype(BF16)

        tiles(blk // sub, part)
        copies.start(
            f"ea{s}", N.at[rows(b), own], DZ.at[s - 2], {"col": col_of[1]}, at_end
        )

    def x_pass(s):
        b = col_of[s]
        copies.came(f"ea{5 - s}", between)

        @pl.when(between)
        def _():
            def part(i):
                rs = at(b * blk + i * sub, sub)
                came = DZ[3 - s, at(i * sub, sub), :]
                N[rs, own] = (N[rs, own].astype(F32) + came.astype(F32)).astype(BF16)

            tiles(blk // sub, part)

        copies.start(f"eb{s}", N.at[rows(b), own], DZ.at[2], {"col": b}, between)

    row_rest(
        OUTP,
        (("oa1", between), ("oc1", at_end), ("oa2", None), ("ob1", None), ("ob2", None)),
        (OZ1, OZ2),
        OY.at[0],
        "oy0",
    )
    pl.semaphore_wait(credit.at[7], 1)
    pl.semaphore_wait(credit.at[8], 1)
    spread_out("dn1", WU, down_at(1 - r, hi), R_dn, both_tiles)
    pl.semaphore_wait(credit.at[5], 1)
    spread_out("up1", G, up_at(1 - r, hi))
    finish("dn0", S_dn.at[0], WU, down_at(r), X_dn, both_tiles)
    finish("de0", S_de.at[0], g_dense, dense_at(r), X_de)
    finish("up0", S_up.at[0], G, up_at(r))
    crossed("qk1", WN.at[qkv_at(r, hi)])
    x_block(2)
    copies.came("sy")
    NZ[c, 0:4, :] = NSUM[0:4, own] + SMR[0:4, :]
    for s in (1, 2, 3):
        copies.start(f"sz{s}", NZ.at[c], NZ.at[c], {"col": col_of[s]})
    x_block(3)
    copies.start("eza", N.at[rows(col_of[1]), own], DZ1.at[:, own], {"col": col_of[1]})
    BS[...] = gathered_dp("b", BQ)
    copies.start("by", BS, BR, y_dev)
    row_rest(N, (("ezb", None),), (DZ1,), EY[0], "ey0")
    x_pass(3)
    pl.semaphore_wait(credit.at[6], 1)
    finish("qk0", S_qk.at[0], WN, qkv_at(r))
    pass_quarter("dn1", WU, down_at(1 - r, 1 - hi))
    x_pass(2)
    for s in (1, 2, 3):
        copies.came(f"sz{s}")
    NQ[q] = NZ[0] + NZ[1] + NZ[2] + NZ[3]
    gather_dp("n", NQ)
    pass_quarter("de1", g_dense, dense_at(1 - r, 1 - hi))
    spread_out("qk1", WN, qkv_at(1 - r, hi))
    for name in ("oz3", "oy0"):
        copies.came(name)

    def out_last(i):
        total = total_of(i, OUTP, (OZ1, OZ2), (OZ3, OY.at[0]))
        total = total + X[mine_at(i), own].astype(F32)
        out[at(i * sub, sub), :] = (total + row_of(dense_b[...] + down_b[...])).astype(BF16)

    tiles(blk // sub, out_last)
    again_g = X.at[pl.ds(0, blk), own]
    fetch_c = pltpu.make_async_copy(cot, again_g, local_sem.at[11])
    fetch_c.start()
    pass_quarter("up1", G, up_at(1 - r, 1 - hi))
    copies.came("by")
    small[0:8, :] = BS[...]
    small[8:16, :] = BR[...]
    small[4:8, :] = gathered_dp("n", NQ)[0:4]
    copies.came("eza")
    copies.came("eb2", at_end)
    copies.came("eb3", between)
    copies.came("ey0")

    fetch_c.wait()

    def x_last(i):
        total = total_of(i, N, (DZ1,), (DZ.at[2], EY[0]))
        in_grad[at(i * sub, sub), :] = again_g[at(i * sub, sub), :].astype(F32) + total

    tiles(blk // sub, x_last)
    pass_quarter("qk1", WN, qkv_at(1 - r, 1 - hi))
    for name in ("dn0", "de0", "up0", "qk0"):
        copies.came(f"{name}t")
    for name in ("dn1", "de1", "up1", "qk1"):
        copies.came(f"{name}t")
        copies.came(f"{name}f")
    for copy in local[6:]:
        copy.wait()
    copies.sent_all()


def scratch(blk, wid, cols, units, heads):
    tokens, width = blk * cols, 2 * wid
    low = [(tokens, width), (width, heads), (HD, width), (tokens, width)]
    V = pltpu.VMEM
    return (
        [V(shape, BF16) for shape in low]
        + [V((tokens, 128), F32)]
        + [
            V(shape, BF16)
            for shape in (
                (tokens, heads), (tokens, HD), (tokens, units), (tokens, units), (tokens, units),
                (tokens, HD), (tokens, width), (blk, width), (blk, width), (blk, wid),
                (2, blk, wid), (blk, width), (3, blk, wid),
                (2, units // 2, wid), (2, HD // 2, wid), (2, wid, units // 2), (2, wid, heads // 2),
                (units // 4, wid), (HD // 4, wid), (units // 4, wid), (HD // 4, wid),
                (wid // 2, units // 2),
                (units // 2, wid), (HD // 2, wid),
            )
        ]
        + [
            V((blk, width), F32),
            V((8, width), F32),
            V((tokens, 128), F32),
            V((tokens, 128), F32),
            V((8, width), F32),
            V((8, wid), F32),
            V((8, wid), F32),
            V((cols, 8, wid), F32),
            V((4, 8, wid), F32),
            V((4, 8, wid), F32),
            V((8, wid), F32),
            V((8, wid), F32),
            pltpu.SemaphoreType.DMA((60,)),
            pltpu.SemaphoreType.DMA((110,)),
            pltpu.SemaphoreType.DMA((12,)),
            pltpu.SemaphoreType.REGULAR((9,)),
        ]
    )


WIDEN_DEPTH, WIDEN_ROWS, WIDEN_COLS = 4, 512, 1024


def widen_kernel(
    out, in_grad, small, g_up, g_qkv, g_down, g_dense,
    out_hbm, in_grad_hbm, d_qkv, d_dense, d_up, d_down, *rest,
):
    sums_hbm, (buf, dense, sem, small_sem), sums = rest[:8], rest[8:12], rest[12:]
    fetch = pltpu.make_async_copy(g_dense, dense, small_sem.at[0])
    fetch.start()
    jobs = []
    for source, target in ((g_up, d_up), (g_down, d_down), (g_qkv, d_qkv), (dense, d_dense)):
        n_rows, n_cols = target.shape
        for row in range(0, n_rows, WIDEN_ROWS):
            for col in range(0, n_cols, WIDEN_COLS):
                span = min(WIDEN_COLS, n_cols - col)
                jobs.append((source, target, row, col, span))
    sent = []
    for j, (source, target, row, col, span) in enumerate(jobs):
        slot = j % WIDEN_DEPTH
        if j >= WIDEN_DEPTH:
            sent[j - WIDEN_DEPTH].wait()
        if source is dense:
            fetch.wait()
        for part in range(0, WIDEN_ROWS, 64):
            buf[slot, part : part + 64, 0:span] = source[
                row + part : row + part + 64, col : col + span
            ].astype(F32)
        copy = pltpu.make_async_copy(
            buf.at[slot, :, pl.ds(0, span)],
            target.at[pl.ds(row, WIDEN_ROWS), pl.ds(col, span)],
            sem.at[slot],
        )
        copy.start()
        sent.append(copy)
        if j == 1:
            gain1, bias1, gain2, bias2, qkv_sum, dense_sum, up_sum, down_sum = sums
            for i, ref in enumerate((gain1, bias1, gain2, bias2)):
                ref[...] = small[4 + i]
            dense_sum[...] = small[2]
            down_sum[...] = small[2]
            r = lax.axis_index("row")
            for ref, index in ((up_sum, 0), (qkv_sum, 1)):
                n = ref.shape[0] // 2
                ref[at(r * n, n)] = small[index, 0:n]
                ref[at((1 - r) * n, n)] = small[8 + index, 0:n]
            pairs = [(out, out_hbm), (in_grad, in_grad_hbm), *zip(sums, sums_hbm)]
            plain = [
                pltpu.make_async_copy(a, b, small_sem.at[1 + i]) for i, (a, b) in enumerate(pairs)
            ]
            for copy in plain:
                copy.start()
    for copy in sent[-WIDEN_DEPTH:] + plain:
        copy.wait()


def swap(value, axis, mask):
    size = lax.axis_size(axis)
    return lax.ppermute(value, axis, [(i, i ^ mask) for i in range(size)])


def shards(
    hidden_in,
    segment,
    norm1_gain,
    norm1_bias,
    norm2_gain,
    norm2_bias,
    qkv_weight,
    qkv_bias,
    dense_weight,
    dense_bias,
    up_weight,
    up_bias,
    down_weight,
    down_bias,
    cotangent,
):
    blk, wid = hidden_in.shape
    cols = lax.axis_size("col")
    heads, units = qkv_weight.shape[1] // 2, up_weight.shape[1] // 2
    vectors = (
        norm1_gain, norm1_bias, norm2_gain, norm2_bias, qkv_bias, up_bias, dense_bias, down_bias,
    )
    vmem = pl.BlockSpec(memory_space=pltpu.VMEM)
    far = pl.BlockSpec(memory_space=pl.ANY)
    shape = jax.ShapeDtypeStruct
    V = pltpu.VMEM
    width, units_all, heads_all = 2 * wid, 2 * units, 2 * heads
    out, in_grad, small, g_up, g_qkv, g_down, g_dense = pl.pallas_call(
        functools.partial(step_kernel, (blk, wid, cols)),
        out_shape=(
            V((blk, wid), BF16),
            V((blk, wid), F32),
            V((16, wid), F32),
            V((blk * cols, width), BF16),
            V((units, width), BF16),
            V((width, units), BF16),
            shape(dense_weight.shape, BF16),
        ),
        in_specs=[far] * 6 + [vmem] * 9,
        out_specs=(vmem,) * 6 + (far,),
        scratch_shapes=scratch(blk, wid, cols, units, heads),
        compiler_params=pltpu.CompilerParams(
            collective_id=0, has_side_effects=True, vmem_limit_bytes=52743168
        ),
        name="step",
    )(
        hidden_in, cotangent, qkv_weight, up_weight, dense_weight, down_weight, segment, *vectors
    )

    grads = (g_up, g_qkv, g_down, g_dense)
    mask = 4
    while mask < lax.axis_size("dp"):
        grads = tuple(
            (g.astype(F32) + swap(g, "dp", mask).astype(F32)).astype(BF16) for g in grads
        )
        small = small + swap(small, "dp", mask)
        mask *= 2
    lengths = [wid] * 4 + [heads_all, wid, units_all, wid]
    results = [
        (out.shape, BF16),
        (in_grad.shape, F32),
        (qkv_weight.shape, F32),
        (dense_weight.shape, F32),
        (up_weight.shape, F32),
        (down_weight.shape, F32),
    ]
    widened = pl.pallas_call(
        widen_kernel,
        out_shape=[shape(*result) for result in results] + [shape((n,), F32) for n in lengths],
        in_specs=[vmem] * 6 + [pl.BlockSpec(memory_space=pltpu.HBM)],
        out_specs=[far] * (len(results) + len(lengths)),
        scratch_shapes=[
            V((WIDEN_DEPTH, WIDEN_ROWS, WIDEN_COLS), F32),
            V(dense_weight.shape, BF16),
            pltpu.SemaphoreType.DMA((WIDEN_DEPTH,)),
            pltpu.SemaphoreType.DMA((3 + len(lengths),)),
        ]
        + [V((n,), F32) for n in lengths],
        compiler_params=pltpu.CompilerParams(vmem_limit_bytes=12 << 20),
        name="widen",
    )(out, in_grad, small, *grads)
    out, in_grad, d_qkv, d_dense, d_up, d_down, *sums = widened
    return (
        out,
        in_grad,
        sums[0],
        sums[1],
        sums[2],
        sums[3],
        d_qkv,
        sums[4],
        d_dense,
        sums[5],
        d_up,
        sums[6],
        d_down,
        sums[7],
    )


def solution(mesh):
    return jax.shard_map(
        shards,
        mesh=mesh,
        in_specs=(
            P(("dp", "col"), "row"),
            P("dp", None),
            P("row"),
            P("row"),
            P("row"),
            P("row"),
            P("row", "col"),
            P("col"),
            P("col", "row"),
            P("row"),
            P("row", "col"),
            P("col"),
            P("col", "row"),
            P("row"),
            P(("dp", "col"), "row"),
        ),
        out_specs=(
            P(("dp", "col"), "row"),
            P(("dp", "col"), "row"),
            P("row"),
            P("row"),
            P("row"),
            P("row"),
            P("row", "col"),
            P("col"),
            P("col", "row"),
            P("row"),
            P("row", "col"),
            P("col"),
            P("col", "row"),
            P("row"),
        ),
        check_vma=False,
    )
```

```python
import functools
import math

import jax
import jax.numpy as jnp
from jax import lax
from jax.experimental import pallas as pl
from jax.experimental.pallas import tpu as pltpu
from jax.sharding import PartitionSpec as P

HD = 256
ROT = 64
F32 = jnp.float32
BF16 = jnp.bfloat16
MESH = pl.DeviceIdType.MESH

eps_norm = 1e-05
rope_base = 10000.0
TILE = 512
NN = (((1,), (0,)), ((), ()))
NT = (((1,), (1,)), ((), ()))
TN = (((0,), (0,)), ((), ()))


def dot(left, right, dims):
    return lax.dot_general(left, right, dims, preferred_element_type=F32)


class Copies:
    def __init__(self, send_sem, recv_sem):
        self.send_sem, self.recv_sem = send_sem, recv_sem
        self.made, self.open, self.free, self.slot = {}, {}, [], {}
        self.used = 0

    def start(self, name, source, target, device, when=None):
        if self.free:
            slot = self.free.pop(0)
        else:
            slot, self.used = self.used, self.used + 1
        index = len(self.made)
        self.slot[name] = slot
        copy = pltpu.make_async_remote_copy(
            src_ref=source,
            dst_ref=target,
            send_sem=self.send_sem.at[slot],
            recv_sem=self.recv_sem.at[index],
            device_id=device,
            device_id_type=MESH,
        )
        self.made[name] = copy
        self.open[name] = when
        guarded(when, copy.start)

    def came(self, name, when=None):
        guarded(when, self.made[name].wait_recv)

    def sent(self, *names):
        for name in names:
            guarded(self.open.pop(name), self.made[name].wait_send)
            self.free.append(self.slot[name])

    def sent_all(self):
        self.sent(*list(self.open))


def guarded(when, action):
    if when is None:
        action()
    else:
        pl.when(when)(action)


def row_of(vector):
    return vector.reshape(1, vector.shape[0])


def at(start, size):
    return pl.ds(pl.multiple_of(start, size), size)


def tiles(count, body):
    lax.fori_loop(0, count, lambda i, carry: (body(i), carry)[1], 0)


def step_kernel(
    sizes,
    hid, cot, wq, wu, wd, wn, seg, gain1, bias1, gain2, bias2, qkv_b, up_b, dense_b, down_b,
    out, in_grad, small, G, WN, WU, g_dense,
    X, WQ, WD, N, STAT, QKV, ATT, HID, SLOPE, DUP, DAT, OUTP, OZ1, OZ2, OZ3, OY, DZ1, DZ,
    S_dn, S_de, S_up, S_qk, R_dn, R_de, V_dn, V_de, V_up, X_dn, X_de, TMP, NV, COS, SIN, NSUM, SMO, SMR, NZ, NQ, BQ, BS, BR,
    send_sem, recv_sem, local_sem, credit,
):
    blk, wid, cols = sizes
    rows_all = blk * cols
    width = 2 * wid
    heads, units = WQ.shape[1], WU.shape[1]
    hh, uh, dh = heads // 2, units // 2, HD // 2
    r = lax.axis_index("row")
    c = lax.axis_index("col")
    dp = lax.axis_index("dp")
    k = lax.rem(dp, 2)
    hi = lax.rem(lax.div(dp, 2), 2)
    q = k + 2 * hi
    core_dev = {"dp": dp + 1 - 2 * k}
    x_dev = {"dp": dp + 2 - 4 * hi}
    far_dev = {"dp": dp + 3 - 2 * k - 4 * hi}
    y_dev = {"row": 1 - r}
    c_low, c_high = lax.rem(c, 2), lax.div(c, 2)
    col_of = [c, c + 1 - 2 * c_low, c + 2 - 4 * c_high, 3 - c]
    own, other = pl.ds(0, wid), pl.ds(wid, wid)
    scale = 1.0 / math.sqrt(HD)
    copies = Copies(send_sem, recv_sem)

    barrier = pltpu.get_barrier_semaphore()
    for device in (core_dev, x_dev, y_dev):
        pl.semaphore_signal(barrier, inc=1, device_id=device, device_id_type=MESH)
    for move, inside in ((1, c < cols - 1), (-1, c >= 1)):

        @pl.when(inside)
        def _():
            pl.semaphore_signal(
                barrier, inc=1, device_id={"col": c + move}, device_id_type=MESH
            )

    local = []

    def fetch(source, target):
        copy = pltpu.make_async_copy(source, target, local_sem.at[len(local)])
        copy.start()
        local.append(copy)
        return copy

    fetch_x = fetch(hid, X.at[at(c * blk, blk), own])
    fetch_g = fetch(cot, G.at[at(c * blk, blk), own])
    fetch_u = fetch(wu.at[:, at(r * units, units)], WU.at[own, :])
    fetch_q = fetch(wq.at[:, at(r * heads, heads)], WQ.at[own, :])
    fetch_n = fetch(wn.at[at(r * units, units), :], WN.at[:, own])
    fetch_d = fetch(wd.at[at(r * HD, HD), :], WD.at[:, own])
    pl.semaphore_wait(
        barrier, 3 + (c < cols - 1).astype(jnp.int32) + (c >= 1).astype(jnp.int32)
    )

    def rows(b):
        return at(b * blk, blk)

    def chain_send(tag, step, buf, columns, first=None):
        for word, move, edge in (("u", 1, c < cols - 1), ("d", -1, c >= 1)):
            block = c - move * (step - 1)
            valid = edge & (block >= 0) & (block <= cols - 1)
            source = first if first is not None else buf.at[rows(block), columns]
            copies.start(
                f"{tag}{word}{step}", source, buf.at[rows(block), columns], {"col": c + move}, valid
            )

    def chain_wait(tag, step):
        copies.came(f"{tag}u{step}", c >= step)
        copies.came(f"{tag}d{step}", c + step <= cols - 1)

    def row_send(name, s):
        b = col_of[s]
        copies.start(name, X.at[rows(b), own], X.at[rows(b), other], y_dev)

    q2 = q + 2 - 4 * hi

    def weight(name, source, full, row0, size, columns, spread):
        share = q if spread else k

        def place(index):
            return full.at[at(row0 + index * size, size), columns]

        copies.start(f"{name}y", source(at(share * size, size)), place(share), y_dev)

        def pass_on():
            copies.came(f"{name}y")
            if spread:
                copies.start(f"{name}x", place(q), place(q), x_dev)
            copies.start(f"{name}c", place(share), place(share), core_dev)

        def pass_far():
            copies.came(f"{name}x")
            copies.start(f"{name}f", place(q2), place(q2), core_dev)

        def done():
            copies.came(f"{name}c")
            if spread:
                copies.came(f"{name}f")

        return pass_on, pass_far, done

    everything = slice(None)
    chain_send("x", 1, X, own, hid)
    copies.start("xy0", hid, X.at[rows(c), other], y_dev)
    for j, vector in enumerate((gain1, bias1, gain2, bias2)):
        NV[j : j + 1, own] = row_of(vector[...])
    NV[4:8, own] = jnp.zeros((4, wid), F32)
    copies.start("nv", NV.at[:, own], NV.at[:, other], y_dev)
    wu_on, wu_far, wu_done = weight(
        "wu", lambda rs: wu.at[rs, at((1 - r) * units, units)], WU, wid, wid // 4, everything, True
    )

    seg_row = seg[...].astype(F32)
    seg_col = jnp.transpose(jnp.broadcast_to(seg_row, (128, rows_all)))
    STAT[:, 3:4] = seg_col[:, 0:1]

    def table(i):
        block = at(i * blk, blk)
        starts = jnp.sum(
            (seg_row < STAT[block, 3:4]).astype(F32), axis=1, keepdims=True
        )
        index = lax.broadcasted_iota(jnp.int32, (blk, 1), 0) + i * blk
        lane = lax.broadcasted_iota(jnp.int32, (1, 128), 1)
        turn = jnp.exp(
            lax.rem(lane, ROT // 2).astype(F32) * (-2.0 * math.log(rope_base) / ROT)
        )
        angles = (index.astype(F32) - starts) * turn
        COS[block, :] = jnp.where(lane < ROT, jnp.cos(angles), 1.0)
        SIN[block, :] = jnp.where(
            lane < ROT // 2, -jnp.sin(angles), jnp.where(lane < ROT, jnp.sin(angles), 0.0)
        )

    tiles(cols, table)

    def rotate(head, block, sign):
        first = head[:, :128]
        lane = lax.broadcasted_iota(jnp.int32, first.shape, 1)
        swapped = jnp.where(
            lane < ROT // 2, pltpu.roll(first, 128 - ROT // 2, 1), pltpu.roll(first, ROT // 2, 1)
        )
        turned = first * COS[block, :] + sign * (swapped * SIN[block, :])
        return jnp.concatenate([turned, head[:, 128:]], axis=1)

    sub = 64

    def norm_block(b):
        def part(i):
            rs = at(b * blk + i * sub, sub)
            x = X[rs, :].astype(F32)
            mean = jnp.sum(x, axis=1, keepdims=True) * (1.0 / width)
            square = jnp.sum(x * x, axis=1, keepdims=True) * (1.0 / width)
            inv = lax.rsqrt(square - mean * mean + eps_norm)
            STAT[rs, 0:1] = mean
            STAT[rs, 1:2] = inv
            normal = (x - mean) * inv
            OUTP[rs, :] = (normal * NV[0:1, :] + NV[1:2, :]).astype(BF16)
            N[rs, :] = (normal * NV[2:3, :] + NV[3:4, :]).astype(BF16)

        tiles(blk // sub, part)

    def up_block(b):
        def part(j):
            cs = at(j * TILE, TILE)
            bias = row_of(up_b[at(r * units + j * TILE, TILE)])
            up = dot(N[rows(b), :], WU[:, cs], NN) + bias
            cdf = 0.5 * (1.0 + lax.erf(up * (1.0 / math.sqrt(2.0))))
            HID[rows(b), cs] = (up * cdf).astype(BF16)
            SLOPE[rows(b), cs] = (
                cdf + up * jnp.exp(-0.5 * up * up) * (1.0 / math.sqrt(2.0 * math.pi))
            ).astype(BF16)

        tiles(units // TILE, part)

    fetch_x.wait()
    fetch_g.wait()
    chain_wait("x", 1)
    chain_send("x", 2, X, own)
    row_send("xy1", 1)
    chain_wait("x", 2)
    chain_send("x", 3, X, own)
    row_send("xy2", 2)
    chain_send("g", 1, G, own, cot)
    wu_on()
    copies.came("nv")
    copies.came("xy0")
    norm_block(col_of[0])
    chain_wait("x", 3)
    row_send("xy3", 3)
    copies.start("gy", cot, G.at[rows(c), other], y_dev)
    wq_on, _, wq_done = weight(
        "wq", lambda rs: wq.at[rs, at((1 - r) * heads, heads)], WQ, wid, wid // 2, everything, False
    )

    def rows_of(ref, start, rs):
        return ref.at[at(start + rs.start, rs.size), :]

    wn_on, _, wn_done = weight(
        "wn", lambda rs: rows_of(wn, (1 - r) * units, rs), WN, 0, units // 2, other, False
    )
    wd_on, _, wd_done = weight(
        "wd", lambda rs: rows_of(wd, (1 - r) * HD, rs), WD, 0, HD // 2, other, False
    )
    wu_far()
    copies.came("xy1")
    norm_block(col_of[1])
    fetch_u.wait()
    wu_done()
    up_block(col_of[0])
    up_block(col_of[1])
    chain_wait("g", 1)
    chain_send("g", 2, G, own)
    copies.came("xy2")
    norm_block(col_of[2])
    up_block(col_of[2])
    chain_wait("g", 2)
    chain_send("g", 3, G, own)
    copies.came("xy3")
    norm_block(col_of[3])
    up_block(col_of[3])
    copies.came("gy")
    near_part, far_part = pl.ds(wid, wid // 2), pl.ds(wid + wid // 2, wid // 2)
    chain_send("h", 1, G, near_part)
    chain_send("i", 1, G, far_part)

    def grad_send(name, staged, left, right, n_rows, n_cols, target):
        def part(i):
            cs = at(i * TILE, TILE)
            staged[:, cs] = dot(left(None), right(cs), TN).astype(BF16)

        tiles(n_cols // TILE, part)
        copies.start(name, staged, target, core_dev)

    hid_keep, hid_send = at(k * uh, uh), at((1 - k) * uh, uh)
    att_keep, att_send = at(k * dh, dh), at((1 - k) * dh, dh)

    def out_grad(name, side, left_ref, keep, give, staged, landing):
        base = side * wid

        def give_part(i):
            cs = at(i * TILE, TILE)
            staged[:, cs] = dot(
                left_ref[:, give], G[:, at(base + i * TILE, TILE)], TN
            ).astype(BF16)

        tiles(wid // TILE, give_part)
        copies.start(f"{name}a", staged, landing, core_dev)

    def out_keep(name, side, left_ref, keep, landing):
        base = side * wid
        copies.came(f"{name}a")

        def keep_part(i):
            cs = at(i * TILE, TILE)
            mine = dot(left_ref[:, keep], G[:, at(base + i * TILE, TILE)], TN)
            landing[:, cs] = (mine + landing[:, cs].astype(F32)).astype(BF16)

        tiles(wid // TILE, keep_part)

    down_tiles = [slice(i * TILE, (i + 1) * TILE) for i in range(wid // TILE)]

    def down_give(side, staged, which):
        for i in which:
            cs = down_tiles[i]
            part = dot(HID[:, hid_send], G[:, side * wid + i * TILE : side * wid + (i + 1) * TILE], TN)
            staged[:, cs] = part.astype(BF16)
            copies.start(f"dn{side}a{i}", staged.at[:, cs], S_dn.at[side, :, cs], core_dev)

    def down_keep(side, which):
        half_rows = uh // 2
        give = at((1 - hi) * half_rows, half_rows)
        for i in which:
            cs = down_tiles[i]
            copies.came(f"dn{side}a{i}")
            mine = dot(HID[:, hid_keep], G[:, side * wid + i * TILE : side * wid + (i + 1) * TILE], TN)
            S_dn[side, :, cs] = (mine + S_dn[side, :, cs].astype(F32)).astype(BF16)
            if side == 0:
                copies.start(f"dn0x{i}", S_dn.at[0, :, cs], X_dn.at[:, cs], x_dev)
            else:
                copies.start(f"dn1x{i}", S_dn.at[1, give, cs], V_dn.at[:, cs], x_dev)

    halves = {}

    def cross(name, total, n_rows, landing):
        half_rows = n_rows // 2
        give, keep = at((1 - hi) * half_rows, half_rows), at(hi * half_rows, half_rows)
        copies.start(f"{name}x", total.at[give, :], landing, x_dev)
        halves[name] = (total.at[keep, :], landing)

    def down_crossed(i):
        cs = down_tiles[i]
        copies.came(f"dn1x{i}")
        mine = S_dn[1, at(hi * (uh // 2), uh // 2), cs].astype(F32)
        V_dn[:, cs] = (mine + V_dn[:, cs].astype(F32)).astype(BF16)
        copies.start(f"dn1y{i}", V_dn.at[:, cs], R_dn.at[:, cs], y_dev)

    def crossed(name, target):
        mine, landing = halves[name]
        copies.came(f"{name}x")
        n = landing.shape[0]
        step = min(n, 128)

        def part(i):
            rs = at(i * step, step)
            landing[rs, :] = (mine[rs, :].astype(F32) + landing[rs, :].astype(F32)).astype(BF16)

        tiles(n // step, part)
        copies.start(f"{name}y", landing, target, y_dev)

    def spread_out(name, result, here, came=None, parts=("",)):
        for word in parts:
            copies.came(f"{name}y{word}")
        source = result.at[here] if came is None else came
        copies.start(f"{name}g", source, result.at[here], x_dev)
        copies.start(f"{name}t", source, result.at[here], core_dev)
        if came is not None:
            fetch(came, result.at[here])

    def pass_quarter(name, result, there):
        copies.came(f"{name}g")
        copies.start(f"{name}f", result.at[there], result.at[there], core_dev)

    def finish(name, total, result, here, came=None, parts=("",)):
        for word in parts:
            copies.came(f"{name}x{word}")
        landed = result.at[here] if came is None else came
        n = total.shape[0]
        step = min(n, 128)

        def part(i):
            rs = at(i * step, step)
            landed[rs, :] = (total[rs, :].astype(F32) + landed[rs, :].astype(F32)).astype(BF16)

        tiles(n // step, part)
        copies.start(f"{name}t", landed, result.at[here], core_dev)
        if came is not None:
            fetch(came, result.at[here])

    wide = slice(None)

    def down_at(side, part=None):
        start, n = side * units + k * uh, uh
        if part is not None:
            start, n = start + part * (uh // 2), uh // 2
        return (at(start, n), wide)

    def dense_at(side, part=None):
        start, n = side * HD + k * dh, dh
        if part is not None:
            start, n = start + part * (dh // 2), dh // 2
        return (at(start, n), wide)

    def up_at(side, part=None):
        taken = wide if part is None else at(part * (wid // 2), wid // 2)
        return (taken, at(side * units + k * uh, uh))

    def qkv_at(side, part=None):
        taken = wide if part is None else at(part * (wid // 2), wid // 2)
        return (taken, at(side * heads + k * hh, hh))

    chain_wait("g", 3)
    both_tiles = tuple(range(len(down_tiles)))
    down_give(0, DUP.at[pl.ds(0, uh), :], both_tiles)
    down_keep(0, both_tiles)
    give_u, keep_u = at((1 - k) * uh, uh), at(k * uh, uh)

    def hidden_back(i, side):
        block = at(i * blk, blk)
        TMP[:, at(i * uh, uh)] = dot(
            G[block, side * wid : (side + 1) * wid], WN[give_u, side * wid : (side + 1) * wid], NT
        )


    chain_wait("h", 1)
    chain_send("h", 2, G, near_part)
    fetch_n.wait()
    tiles(cols, lambda i: hidden_back(i, 0))
    chain_wait("i", 1)
    chain_send("i", 2, G, far_part)
    fetch_q.wait()
    wq_on()
    wq_done()

    def qkv_block(i):
        block = at(i * blk, blk)
        for j in range(3):
            bias = row_of(qkv_b[at(r * heads + j * HD, HD)])
            value = dot(OUTP[block, :], WQ[:, j * HD : (j + 1) * HD], NN) + bias
            if j < 2:
                value = rotate(value, block, 1.0)
            QKV[block, j * HD : (j + 1) * HD] = value.astype(BF16)

    tiles(cols, qkv_block)
    chain_wait("h", 2)
    chain_send("h", 3, G, near_part)

    def key_range(i):
        low = max(0, i - 2) * blk
        return slice(i * blk, (i + 1) * blk), slice(low, (i + 1) * blk), low

    def block_scores(i):
        mine, span, low = key_range(i)
        n = span.stop - low
        s = dot(QKV[mine, 0:HD], QKV[span, HD : 2 * HD], NT) * scale
        row_id = lax.broadcasted_iota(jnp.int32, (blk, n), 0) + i * blk
        col_id = lax.broadcasted_iota(jnp.int32, (blk, n), 1) + low
        same = STAT[mine, 3:4] == seg_row[:, span]
        return jnp.where(same & (col_id <= row_id), s, -1e30)

    for i in range(cols):
        mine, span, low = key_range(i)
        s = block_scores(i)
        largest = jnp.max(s, axis=1, keepdims=True)
        p = jnp.exp(s - largest)
        total = jnp.sum(p, axis=1, keepdims=True)
        STAT[mine, 2:3] = largest + jnp.log(total)
        p_low = (p / total).astype(BF16)
        ATT[mine, :] = dot(p_low, QKV[span, 2 * HD :], NN).astype(BF16)
    copies.sent("dn0a0", "dn0a1")
    out_grad("de0", 0, ATT, att_keep, att_send, DUP.at[pl.ds(0, dh), :], S_de.at[0])
    chain_wait("i", 2)
    chain_send("i", 3, G, far_part)
    fetch_d.wait()

    def branch_block(b, side):
        def part(j):
            cs = at(side * wid + j * TILE, TILE)
            both = dot(ATT[rows(b), :], WD[:, cs], NN) + dot(HID[rows(b), :], WN[:, cs], NN)
            OUTP[rows(b), cs] = both.astype(BF16)

        tiles(wid // TILE, part)

    branch_block(col_of[2], 0)
    out_keep("de0", 0, ATT, att_keep, S_de.at[0])
    copies.start("de0x", S_de.at[0], X_de, x_dev)
    branch_block(col_of[3], 0)

    chain_wait("h", 3)
    down_give(1, DUP.at[pl.ds(uh, uh), :], both_tiles[:1])
    at_end, between = lax.rem(c, 3) == 0, lax.rem(c, 3) != 0

    def own_near(name, when):
        copies.start(
            name, OUTP.at[rows(col_of[1]), own], OZ1.at[:, own], {"col": col_of[1]}, when
        )

    for s in (1, 0):
        branch_block(col_of[s], 0)
    down_keep(1, both_tiles[:1])
    chain_wait("i", 3)
    own_near("oa1", at_end)
    down_give(1, DUP.at[pl.ds(uh, uh), :], both_tiles[1:])
    out_grad("de1", 1, ATT, att_keep, att_send, DUP.at[pl.ds(dh, dh), :], S_de.at[1])
    down_keep(1, both_tiles[1:])
    out_keep("de1", 1, ATT, att_keep, S_de.at[1])
    cross("de1", S_de.at[1], dh, V_de)
    wn_on()
    own_near("oc1", between)
    wn_done()
    copies.start("oa2", OUTP.at[rows(col_of[2]), own], OZ2.at[:, own], {"col": col_of[2]})

    copies.sent("dn1a0", "dn1a1", "de0a", "de1a")

    def up_grad_give(i):
        block = at(i * blk, blk)
        back = TMP[:, at(i * uh, uh)] + dot(G[block, other], WN[give_u, other], NT)
        DUP[block, give_u] = (back * SLOPE[block, give_u].astype(F32)).astype(BF16)

    def up_grad_keep(i):
        block = at(i * blk, blk)
        back = dot(G[block, :], WN[keep_u, :], NT)
        DUP[block, keep_u] = (back * SLOPE[block, keep_u].astype(F32)).astype(BF16)

    tiles(cols, up_grad_give)
    down_crossed(0)
    keep_h, give_h = at(k * hh, hh), at((1 - k) * hh, hh)

    def in_give(name, side, right_ref, give, staged, landing):
        def part(i):
            rs = at(i * TILE, TILE)
            lefts = N[:, at(side * wid + i * TILE, TILE)]
            staged[rs, :] = dot(lefts, right_ref[:, give], TN).astype(BF16)

        tiles(wid // TILE, part)
        copies.start(f"{name}{side}a", staged, landing.at[side], core_dev)

    def in_keep(name, side, right_ref, keep, landing, crossing=None):
        copies.came(f"{name}{side}a")
        n = wid // 2

        def part(i):
            rs = at(i * n, n)
            mine = dot(N[:, at(side * wid + i * n, n)], right_ref[:, keep], TN)
            landing[side, rs, :] = (mine + landing[side, rs, :].astype(F32)).astype(BF16)

        if crossing is None:
            tiles(2, part)
        else:
            part(1 - hi)
            crossing()
            part(hi)

    in_give("up", 1, DUP, give_u, SLOPE.at[:, give_u], S_up)
    tiles(cols, up_grad_keep)
    wd_on()
    in_keep("up", 1, DUP, keep_u, S_up, lambda: cross("up1", S_up.at[1], wid, V_up))
    wd_done()
    branch_block(col_of[3], 1)
    copies.start("oy3", OUTP.at[rows(col_of[3]), other], OY.at[1], y_dev)
    for i in range(cols):
        mine = slice(i * blk, (i + 1) * blk)
        DAT[mine, :] = dot(G[mine, :], WD[...], NT).astype(BF16)
    BQ[q, 2:3, :] = jnp.sum(G[:, own].astype(F32), axis=0, keepdims=True)

    copies.sent(*[f"{t}{w}{s}" for t in "xghi" for w in "ud" for s in (1, 2, 3)])
    copies.sent("xy0", "xy1", "xy2", "xy3", "gy", "nv", "wuy", "wux", "wuc", "wuf", "wqy", "wqc")
    copies.sent("dn0x0", "dn0x1", "wny", "wdy", "wdc")
    pl.semaphore_signal(credit.at[0], inc=1, device_id=x_dev, device_id_type=MESH)
    pl.semaphore_signal(credit.at[1], inc=1, device_id=y_dev, device_id_type=MESH)
    pl.semaphore_signal(credit.at[5], inc=1, device_id=core_dev, device_id_type=MESH)
    V_qk = WN.at[pl.ds(0, wid // 2), pl.ds(2 * heads, hh)]

    in_give("up", 0, DUP, give_u, SLOPE.at[:, keep_u], S_up)
    down_crossed(1)
    branch_block(col_of[2], 1)
    copies.start("ob2", OUTP.at[rows(col_of[2]), other], OZ2.at[:, other], {"col": col_of[2]})
    in_keep("up", 0, DUP, keep_u, S_up)
    pl.semaphore_wait(credit.at[0], 1)
    copies.start("up0x", S_up.at[0], G.at[up_at(r)], x_dev)

    branch_block(col_of[1], 1)
    copies.start("ob1", OUTP.at[rows(col_of[1]), other], OZ1.at[:, other], {"col": col_of[1]})
    branch_block(col_of[0], 1)
    crossed("de1", R_de)
    copies.sent("wnc")
    pl.semaphore_signal(credit.at[2], inc=1, device_id=x_dev, device_id_type=MESH)
    pl.semaphore_signal(credit.at[3], inc=1, device_id=y_dev, device_id_type=MESH)
    pl.semaphore_signal(credit.at[6], inc=1, device_id=core_dev, device_id_type=MESH)
    pl.semaphore_signal(credit.at[4], inc=1, device_id=y_dev, device_id_type=MESH)

    def out_block():
        b = col_of[3]
        copies.came("oy3")

        def part(i):
            rs = at(b * blk + i * sub, sub)
            came = OY[1, at(i * sub, sub), :]
            OUTP[rs, own] = (OUTP[rs, own].astype(F32) + came.astype(F32)).astype(BF16)

        tiles(blk // sub, part)
        copies.start("oz3", OUTP.at[rows(b), own], OZ3, {"col": b})

    def again(i):
        rs = at(i * sub, sub)
        normal = (X[rs, :].astype(F32) - STAT[rs, 0:1]) * STAT[rs, 1:2]
        N[rs, :] = (normal * NV[0:1, :] + NV[1:2, :]).astype(BF16)

    tiles(rows_all // sub, again)
    TMP[...] = jnp.zeros_like(TMP)
    for i in range(cols):
        mine, span, low = key_range(i)
        query = QKV[mine, 0:HD]
        p = jnp.exp(block_scores(i) - STAT[mine, 2:3])
        d_p = dot(DAT[mine, :], QKV[span, 2 * HD :], NT)
        delta = jnp.sum(d_p * p, axis=1, keepdims=True)
        d_s = (p * (d_p - delta)).astype(BF16)
        p_low = p.astype(BF16)
        d_query = dot(d_s, QKV[span, HD : 2 * HD], NN) * scale
        QKV[mine, 0:HD] = rotate(d_query, mine, -1.0).astype(BF16)
        for j in range(low // blk, i + 1):
            js = slice(j * blk - low, (j + 1) * blk - low)
            ks, vs = slice(j * HD, (j + 1) * HD), slice((cols + j) * HD, (cols + j + 1) * HD)
            TMP[:, ks] += dot(d_s[:, js], query, TN)
            TMP[:, vs] += dot(p_low[:, js], DAT[mine, :], TN)
    for j in range(cols):
        mine = slice(j * blk, (j + 1) * blk)
        ks, vs = slice(j * HD, (j + 1) * HD), slice((cols + j) * HD, (cols + j + 1) * HD)
        QKV[mine, HD : 2 * HD] = rotate(TMP[:, ks] * scale, mine, -1.0).astype(BF16)
        QKV[mine, 2 * HD :] = TMP[:, vs].astype(BF16)

    copies.sent("up0a", "up1a")
    in_give("qk", 1, QKV, give_h, SLOPE.at[:, pl.ds(hh, hh)], S_qk)
    in_give("qk", 0, QKV, give_h, SLOPE.at[:, pl.ds(0, hh)], S_qk)
    pl.semaphore_wait(credit.at[1], 1)
    crossed("up1", G.at[up_at(r, hi)])
    pl.semaphore_wait(credit.at[2], 1)
    in_keep("qk", 1, QKV, keep_h, S_qk, lambda: cross("qk1", S_qk.at[1], wid, V_qk))
    in_keep("qk", 0, QKV, keep_h, S_qk)
    copies.start("qk0x", S_qk.at[0], WN.at[qkv_at(r)], x_dev)

    def gather_dp(name, slots):
        for word, device in (("c", core_dev), ("x", x_dev), ("d", far_dev)):
            copies.start(f"{name}{word}", slots.at[q], slots.at[q], device)

    def gathered_dp(name, slots):
        for word in "cxd":
            copies.came(f"{name}{word}")
        return slots[0] + slots[1] + slots[2] + slots[3]

    BQ[q, 0:1, :] = jnp.sum(DUP[...].astype(F32), axis=0, keepdims=True)
    BQ[q, 1:2, 0:heads] = jnp.sum(QKV[...].astype(F32), axis=0, keepdims=True)
    BQ[q, 1:2, heads:] = jnp.zeros((1, wid - heads), F32)
    BQ[q, 3:8, :] = jnp.zeros((5, wid), F32)
    gather_dp("b", BQ)

    NSUM[...] = jnp.zeros_like(NSUM)
    pl.semaphore_wait(credit.at[4], 1)

    def norm_back(b):
        rb = rows(b)
        mean, inv = STAT[rb, 0:1], STAT[rb, 1:2]

        def first(j, carry):
            along, plain = carry
            cs = at(j * TILE, TILE)
            one = dot(QKV[rb, :], WQ[cs, :], NT)
            two = dot(DUP[rb, :], WU[cs, :], NT)
            normal = (X[rb, cs].astype(F32) - mean) * inv
            NSUM[0:1, cs] += jnp.sum(one * normal, axis=0, keepdims=True)
            NSUM[1:2, cs] += jnp.sum(one, axis=0, keepdims=True)
            NSUM[2:3, cs] += jnp.sum(two * normal, axis=0, keepdims=True)
            NSUM[3:4, cs] += jnp.sum(two, axis=0, keepdims=True)
            grad = one * NV[0:1, cs] + two * NV[2:3, cs]
            TMP[:, cs] = grad
            along = along + jnp.sum(grad * normal, axis=1, keepdims=True)
            plain = plain + jnp.sum(grad, axis=1, keepdims=True)
            return along, plain

        zero = jnp.zeros((blk, 1), F32)
        along, plain = lax.fori_loop(0, width // TILE, first, (zero, zero))
        along, plain = along * (1.0 / width), plain * (1.0 / width)

        def second(j):
            cs = at(j * TILE, TILE)
            normal = (X[rb, cs].astype(F32) - mean) * inv
            N[rb, cs] = (inv * (TMP[:, cs] - plain - normal * along)).astype(BF16)

        tiles(width // TILE, second)

    EY = [HID.at[pl.ds(j * blk, blk), :] for j in range(3)]
    pl.semaphore_wait(credit.at[3], 1)
    for s in (2, 3):
        norm_back(col_of[s])
        copies.start(f"ey{s}", N.at[rows(col_of[s]), other], EY[s - 1], y_dev)
        if s == 2:
            out_block()
        else:
            spread_out("de1", g_dense, dense_at(1 - r, hi), R_de)
    norm_back(col_of[1])
    copies.start(
        "ezb", N.at[rows(col_of[1]), other], DZ1.at[:, other], {"col": col_of[1]}
    )
    norm_back(col_of[0])
    pl.semaphore_signal(credit.at[7], inc=1, device_id=core_dev, device_id_type=MESH)
    pl.semaphore_signal(credit.at[8], inc=1, device_id=x_dev, device_id_type=MESH)
    SMO[0:4, :] = NSUM[0:4, other]
    copies.start("sy", SMO, SMR, y_dev)

    def mine_at(i):
        return at(c * blk + i * sub, sub)

    def row_rest(buf, names, whole, landing, name):
        for arrival, when in names:
            copies.came(arrival, when)

        def part(i):
            rs = at(i * sub, sub)
            total = buf[mine_at(i), other].astype(F32)
            for ref in whole:
                total = total + ref[rs, other].astype(F32)
            buf[mine_at(i), other] = total.astype(BF16)

        tiles(blk // sub, part)
        copies.start(name, buf.at[rows(c), other], landing, y_dev)

    def total_of(i, buf, whole, parts):
        rs = at(i * sub, sub)
        total = buf[mine_at(i), own].astype(F32)
        for ref in whole:
            total = total + ref[rs, own].astype(F32)
        for ref in parts:
            total = total + ref[rs, :].astype(F32)
        return total

    def x_block(s):
        b = col_of[s]
        copies.came(f"ey{s}")

        def part(i):
            rs = at(b * blk + i * sub, sub)
            came = EY[s - 1][at(i * sub, sub), :]
            N[rs, own] = (N[rs, own].astype(F32) + came.astype(F32)).astype(BF16)

        tiles(blk // sub, part)
        copies.start(
            f"ea{s}", N.at[rows(b), own], DZ.at[s - 2], {"col": col_of[1]}, at_end
        )

    def x_pass(s):
        b = col_of[s]
        copies.came(f"ea{5 - s}", between)

        @pl.when(between)
        def _():
            def part(i):
                rs = at(b * blk + i * sub, sub)
                came = DZ[3 - s, at(i * sub, sub), :]
                N[rs, own] = (N[rs, own].astype(F32) + came.astype(F32)).astype(BF16)

            tiles(blk // sub, part)

        copies.start(f"eb{s}", N.at[rows(b), own], DZ.at[2], {"col": b}, between)

    row_rest(
        OUTP,
        (("oa1", between), ("oc1", at_end), ("oa2", None), ("ob1", None), ("ob2", None)),
        (OZ1, OZ2),
        OY.at[0],
        "oy0",
    )
    pl.semaphore_wait(credit.at[7], 1)
    pl.semaphore_wait(credit.at[8], 1)
    spread_out("dn1", WU, down_at(1 - r, hi), R_dn, both_tiles)
    pl.semaphore_wait(credit.at[5], 1)
    spread_out("up1", G, up_at(1 - r, hi))
    finish("dn0", S_dn.at[0], WU, down_at(r), X_dn, both_tiles)
    finish("de0", S_de.at[0], g_dense, dense_at(r), X_de)
    finish("up0", S_up.at[0], G, up_at(r))
    crossed("qk1", WN.at[qkv_at(r, hi)])
    x_block(2)
    copies.came("sy")
    NZ[c, 0:4, :] = NSUM[0:4, own] + SMR[0:4, :]
    for s in (1, 2, 3):
        copies.start(f"sz{s}", NZ.at[c], NZ.at[c], {"col": col_of[s]})
    x_block(3)
    copies.start("eza", N.at[rows(col_of[1]), own], DZ1.at[:, own], {"col": col_of[1]})
    BS[...] = gathered_dp("b", BQ)
    copies.start("by", BS, BR, y_dev)
    row_rest(N, (("ezb", None),), (DZ1,), EY[0], "ey0")
    x_pass(3)
    pl.semaphore_wait(credit.at[6], 1)
    finish("qk0", S_qk.at[0], WN, qkv_at(r))
    pass_quarter("dn1", WU, down_at(1 - r, 1 - hi))
    x_pass(2)
    for s in (1, 2, 3):
        copies.came(f"sz{s}")
    NQ[q] = NZ[0] + NZ[1] + NZ[2] + NZ[3]
    gather_dp("n", NQ)
    pass_quarter("de1", g_dense, dense_at(1 - r, 1 - hi))
    spread_out("qk1", WN, qkv_at(1 - r, hi))
    for name in ("oz3", "oy0"):
        copies.came(name)

    def out_last(i):
        total = total_of(i, OUTP, (OZ1, OZ2), (OZ3, OY.at[0]))
        total = total + X[mine_at(i), own].astype(F32)
        out[at(i * sub, sub), :] = (total + row_of(dense_b[...] + down_b[...])).astype(BF16)

    tiles(blk // sub, out_last)
    again_g = X.at[pl.ds(0, blk), own]
    fetch_c = pltpu.make_async_copy(cot, again_g, local_sem.at[11])
    fetch_c.start()
    pass_quarter("up1", G, up_at(1 - r, 1 - hi))
    copies.came("by")
    small[0:8, :] = BS[...]
    small[8:16, :] = BR[...]
    small[4:8, :] = gathered_dp("n", NQ)[0:4]
    copies.came("eza")
    copies.came("eb2", at_end)
    copies.came("eb3", between)
    copies.came("ey0")

    fetch_c.wait()

    def x_last(i):
        total = total_of(i, N, (DZ1,), (DZ.at[2], EY[0]))
        in_grad[at(i * sub, sub), :] = again_g[at(i * sub, sub), :].astype(F32) + total

    tiles(blk // sub, x_last)
    pass_quarter("qk1", WN, qkv_at(1 - r, 1 - hi))
    for name in ("dn0", "de0", "up0", "qk0"):
        copies.came(f"{name}t")
    for name in ("dn1", "de1", "up1", "qk1"):
        copies.came(f"{name}t")
        copies.came(f"{name}f")
    for copy in local[6:]:
        copy.wait()
    copies.sent_all()


def scratch(blk, wid, cols, units, heads):
    tokens, width = blk * cols, 2 * wid
    low = [(tokens, width), (width, heads), (HD, width), (tokens, width)]
    V = pltpu.VMEM
    return (
        [V(shape, BF16) for shape in low]
        + [V((tokens, 128), F32)]
        + [
            V(shape, BF16)
            for shape in (
                (tokens, heads), (tokens, HD), (tokens, units), (tokens, units), (tokens, units),
                (tokens, HD), (tokens, width), (blk, width), (blk, width), (blk, wid),
                (2, blk, wid), (blk, width), (3, blk, wid),
                (2, units // 2, wid), (2, HD // 2, wid), (2, wid, units // 2), (2, wid, heads // 2),
                (units // 4, wid), (HD // 4, wid), (units // 4, wid), (HD // 4, wid),
                (wid // 2, units // 2),
                (units // 2, wid), (HD // 2, wid),
            )
        ]
        + [
            V((blk, width), F32),
            V((8, width), F32),
            V((tokens, 128), F32),
            V((tokens, 128), F32),
            V((8, width), F32),
            V((8, wid), F32),
            V((8, wid), F32),
            V((cols, 8, wid), F32),
            V((4, 8, wid), F32),
            V((4, 8, wid), F32),
            V((8, wid), F32),
            V((8, wid), F32),
            pltpu.SemaphoreType.DMA((60,)),
            pltpu.SemaphoreType.DMA((110,)),
            pltpu.SemaphoreType.DMA((12,)),
            pltpu.SemaphoreType.REGULAR((9,)),
        ]
    )


WIDEN_DEPTH, WIDEN_ROWS, WIDEN_COLS = 4, 512, 1024


def widen_kernel(
    out, in_grad, small, g_up, g_qkv, g_down,
    out_hbm, in_grad_hbm, d_qkv, d_up, d_down, *rest,
):
    sums_hbm, (buf, sem, small_sem), sums = rest[:8], rest[8:11], rest[11:]
    jobs = []
    for source, target in ((g_up, d_up), (g_down, d_down), (g_qkv, d_qkv)):
        n_rows, n_cols = target.shape
        for row in range(0, n_rows, WIDEN_ROWS):
            for col in range(0, n_cols, WIDEN_COLS):
                span = min(WIDEN_COLS, n_cols - col)
                jobs.append((source, target, row, col, span))
    sent = []
    for j, (source, target, row, col, span) in enumerate(jobs):
        slot = j % WIDEN_DEPTH
        if j >= WIDEN_DEPTH:
            sent[j - WIDEN_DEPTH].wait()
        for part in range(0, WIDEN_ROWS, 64):
            buf[slot, part : part + 64, 0:span] = source[
                row + part : row + part + 64, col : col + span
            ].astype(F32)
        copy = pltpu.make_async_copy(
            buf.at[slot, :, pl.ds(0, span)],
            target.at[pl.ds(row, WIDEN_ROWS), pl.ds(col, span)],
            sem.at[slot],
        )
        copy.start()
        sent.append(copy)
        if j == 1:
            gain1, bias1, gain2, bias2, qkv_sum, dense_sum, up_sum, down_sum = sums
            for i, ref in enumerate((gain1, bias1, gain2, bias2)):
                ref[...] = small[4 + i]
            dense_sum[...] = small[2]
            down_sum[...] = small[2]
            r = lax.axis_index("row")
            for ref, index in ((up_sum, 0), (qkv_sum, 1)):
                n = ref.shape[0] // 2
                ref[at(r * n, n)] = small[index, 0:n]
                ref[at((1 - r) * n, n)] = small[8 + index, 0:n]
            pairs = [(out, out_hbm), (in_grad, in_grad_hbm), *zip(sums, sums_hbm)]
            plain = [
                pltpu.make_async_copy(a, b, small_sem.at[i]) for i, (a, b) in enumerate(pairs)
            ]
            for copy in plain:
                copy.start()
    for copy in sent[-WIDEN_DEPTH:] + plain:
        copy.wait()


def swap(value, axis, mask):
    size = lax.axis_size(axis)
    return lax.ppermute(value, axis, [(i, i ^ mask) for i in range(size)])


def shards(
    hidden_in,
    segment,
    norm1_gain,
    norm1_bias,
    norm2_gain,
    norm2_bias,
    qkv_weight,
    qkv_bias,
    dense_weight,
    dense_bias,
    up_weight,
    up_bias,
    down_weight,
    down_bias,
    cotangent,
):
    blk, wid = hidden_in.shape
    cols = lax.axis_size("col")
    heads, units = qkv_weight.shape[1] // 2, up_weight.shape[1] // 2
    vectors = (
        norm1_gain, norm1_bias, norm2_gain, norm2_bias, qkv_bias, up_bias, dense_bias, down_bias,
    )
    vmem = pl.BlockSpec(memory_space=pltpu.VMEM)
    far = pl.BlockSpec(memory_space=pl.ANY)
    shape = jax.ShapeDtypeStruct
    V = pltpu.VMEM
    width, units_all, heads_all = 2 * wid, 2 * units, 2 * heads
    out, in_grad, small, g_up, g_qkv, g_down, g_dense = pl.pallas_call(
        functools.partial(step_kernel, (blk, wid, cols)),
        out_shape=(
            V((blk, wid), BF16),
            V((blk, wid), F32),
            V((16, wid), F32),
            V((blk * cols, width), BF16),
            V((units, width), BF16),
            V((width, units), BF16),
            shape(dense_weight.shape, BF16),
        ),
        in_specs=[far] * 6 + [vmem] * 9,
        out_specs=(vmem,) * 6 + (far,),
        scratch_shapes=scratch(blk, wid, cols, units, heads),
        compiler_params=pltpu.CompilerParams(
            collective_id=0, has_side_effects=True, vmem_limit_bytes=52743168
        ),
        name="step",
    )(
        hidden_in, cotangent, qkv_weight, up_weight, dense_weight, down_weight, segment, *vectors
    )

    grads = (g_up, g_qkv, g_down, g_dense)
    mask = 4
    while mask < lax.axis_size("dp"):
        grads = tuple(
            (g.astype(F32) + swap(g, "dp", mask).astype(F32)).astype(BF16) for g in grads
        )
        small = small + swap(small, "dp", mask)
        mask *= 2
    lengths = [wid] * 4 + [heads_all, wid, units_all, wid]
    results = [
        (out.shape, BF16),
        (in_grad.shape, F32),
        (qkv_weight.shape, F32),
        (up_weight.shape, F32),
        (down_weight.shape, F32),
    ]
    widened = pl.pallas_call(
        widen_kernel,
        out_shape=[shape(*result) for result in results] + [shape((n,), F32) for n in lengths],
        in_specs=[vmem] * 6,
        out_specs=[far] * (len(results) + len(lengths)),
        scratch_shapes=[
            V((WIDEN_DEPTH, WIDEN_ROWS, WIDEN_COLS), F32),
            pltpu.SemaphoreType.DMA((WIDEN_DEPTH,)),
            pltpu.SemaphoreType.DMA((2 + len(lengths),)),
        ]
        + [V((n,), F32) for n in lengths],
        compiler_params=pltpu.CompilerParams(vmem_limit_bytes=12 << 20),
        name="widen",
    )(out, in_grad, small, *grads[:3])
    d_dense = grads[3].astype(F32)
    out, in_grad, d_qkv, d_up, d_down, *sums = widened
    return (
        out,
        in_grad,
        sums[0],
        sums[1],
        sums[2],
        sums[3],
        d_qkv,
        sums[4],
        d_dense,
        sums[5],
        d_up,
        sums[6],
        d_down,
        sums[7],
    )


def solution(mesh):
    return jax.shard_map(
        shards,
        mesh=mesh,
        in_specs=(
            P(("dp", "col"), "row"),
            P("dp", None),
            P("row"),
            P("row"),
            P("row"),
            P("row"),
            P("row", "col"),
            P("col"),
            P("col", "row"),
            P("row"),
            P("row", "col"),
            P("col"),
            P("col", "row"),
            P("row"),
            P(("dp", "col"), "row"),
        ),
        out_specs=(
            P(("dp", "col"), "row"),
            P(("dp", "col"), "row"),
            P("row"),
            P("row"),
            P("row"),
            P("row"),
            P("row", "col"),
            P("col"),
            P("col", "row"),
            P("row"),
            P("row", "col"),
            P("col"),
            P("col", "row"),
            P("row"),
        ),
        check_vma=False,
    )
```
